32 devices in a mesh: dp: 4 (over x, core), seq: 8 (over z, y).
Axes of the slice: x: 2, y: 2, z: 4, core: 2. Of those that a mesh axis runs over, the one named last changes fastest.
Arguments:
- tokens: bfloat16 [32768, 1152], P(('dp', 'seq')), may hold values from -6 to 6
- condition: bfloat16 [128, 1152], P('dp'), may hold values from -6 to 6
- lengths: int32 [128], P(('dp', 'seq')), may hold values from 1 to 256, 22937 in all
- kept_index: int32 [128, 256], P(('dp', 'seq')), may hold values from 0 to 255, each once within a row
- heads_weight: bfloat16 [1152, 3456], P('seq'), may hold values from -0.1875 to 0.1875
- heads_bias: bfloat16 [2304], replicated, may hold values from -1.5 to 1.5
- merge_weight: bfloat16 [1152, 1152], P('seq'), may hold values from -1.5 to 1.5
- merge_bias: bfloat16 [1152], replicated, may hold values from -4 to 4
- up_weight: bfloat16 [1152, 4608], P('seq'), may hold values from -0.1875 to 0.1875
- up_bias: bfloat16 [4608], replicated, may hold values from -4 to 4
- down_weight: bfloat16 [1152, 4608], P('seq'), may hold values from -0.1875 to 0.1875
- down_bias: bfloat16 [1152], replicated, may hold values from -4 to 4
- modulate_weight: bfloat16 [1152, 6912], P('seq'), may hold values from -0.1875 to 0.1875
- modulate_bias: bfloat16 [6912], replicated, may hold values from -4 to 4
- relative_table: bfloat16 [16, 961], replicated, may hold values from -6 to 6
- cotangent: bfloat16 [32768, 1152], P(('dp', 'seq')), may hold values from -6 to 6
Outputs:
- output: bfloat16 [32768, 1152], P(('dp', 'seq'))
- tokens_grad: float32 [32768, 1152], P(('dp', 'seq'))
- heads_weight_grad: float32 [1152, 3456], P('seq')
- merge_weight_grad: float32 [1152, 1152], P('seq')
- up_weight_grad: float32 [1152, 4608], P('seq')
- down_weight_grad: float32 [1152, 4608], P('seq')
- modulate_weight_grad: float32 [1152, 6912], P('seq')
- heads_bias_grad: float32 [2304], replicated
- merge_bias_grad: float32 [1152], replicated
- up_bias_grad: float32 [4608], replicated
- down_bias_grad: float32 [1152], replicated
- modulate_bias_grad: float32 [6912], replicated
- relative_table_grad: float32 [16, 961], replicated
The draws below stay inside these ranges and needn't reach their ends.
Inputs may be any that keep to these rules, and one draw needn't show every extreme that they name: The first lengths[s] slots of sample s hold its kept tokens, the rest are empty. Each sample's row is a permutation of the 256 patch positions; slot r's patch lies at row kept_index // 16, column kept_index % 16.
All inputs are finite; a program needn't handle non-finite values. No bound on the sum of `lengths` on one device may be relied on, other than what follows from the above.
Results may differ from the reference program's by a relative error of at most 0.019.
Values may be sent and summed in bfloat16 or wider, within the bound.
No kernel may reach another device: no remote copies, remote signals or barrier semaphores. Data moves between devices by JAX's collectives and lax.ppermute only.
A program may use at most 320 MiB of HBM per device.

```python
import math
import jax
import jax.numpy as jnp
import numpy as np
from jax import lax

D = 1152
HEADS = 16
HEAD = 72
FF = 4608
SIDE = 16
GRID = 256
RELS = 961
SAMPLES = 128
TOKENS = 32768


def levels(key, extent, cuts, low, high):
    loudness = 1.0
    for dim, blocks in cuts:
        draws = jax.random.uniform(jax.random.fold_in(jax.random.fold_in(key, 6), dim), (blocks,), jnp.float32, low / len(cuts), high / len(cuts))
        loudness = loudness * jnp.repeat(jnp.exp(draws), extent[dim] // blocks).reshape((-1,) + (1,) * (len(extent) - 1 - dim))
    return loudness


def split_up(number_of, total, reach, skew):
    weights = [(1 << 20) // math.isqrt(rank ** skew) + 1 for rank in range(2, number_of + 1)]
    spare, holding = total - reach - (number_of - 1), [1] * (number_of - 1)
    while spare > 0:
        movable = [i for i in range(number_of - 1) if holding[i] < reach]
        pool, budget = sum([weights[i] for i in movable]), spare
        for i in movable:
            more = min(reach - holding[i], max(1, budget * weights[i] // pool), spare)
            holding[i] = holding[i] + more
            spare = spare - more
    return np.array([reach] + holding)


def uneven_parts(key, count, total, bound, skew):
    if count == 2:
        one = jax.random.randint(key, (), max(1, total - bound), min(bound, total - 1) + 1)
        return jnp.stack([one, total - one])
    tallies = jnp.asarray(split_up(count, total, bound, skew), jnp.int32)
    pairs = (count - 1) // 2
    donor, sink = tallies[1:1 + 2 * pairs:2], tallies[2:2 + 2 * pairs:2]
    room = jnp.minimum(donor - 1, bound - sink)
    shifted = jax.random.randint(jax.random.fold_in(key, 1), (pairs,), 0, 1 << 20) % (room + 1)
    tallies = tallies.at[1:1 + 2 * pairs:2].set(donor - shifted).at[2:2 + 2 * pairs:2].set(sink + shifted)
    return tallies[jax.random.permutation(jax.random.fold_in(key, 2), count)]


def centred(key, dims, scale, most, shards=(), held_as=jnp.bfloat16):
    values = jax.random.normal(key, dims, jnp.float32) * scale
    if len(shards) > 0:
        values = levels(key, dims, shards, -0.22, 0.18) * values
    return jnp.clip(values, min=-most, max=most).astype(held_as)


def setup_inputs(seed: int = 0) -> dict:
    arg_keys = jax.random.split(jax.random.key(seed), 17)
    return {
        "tokens": centred(arg_keys[0], (TOKENS, D), 1.0, 6.0, ((0, 32),)),
        "condition": centred(arg_keys[1], (SAMPLES, D), 1.0, 6.0, ((0, 4),)),
        "lengths": uneven_parts(arg_keys[2], SAMPLES, 7 * GRID * SAMPLES // 10, GRID, 1).astype(jnp.int32),
        "kept_index": jax.vmap(lambda own: jax.random.permutation(own, GRID))(jax.random.split(arg_keys[3], SAMPLES)).reshape((SAMPLES, GRID)).astype(jnp.int32),
        "heads_weight": centred(arg_keys[4], (D, 3 * D), D ** -0.5, 0.1875, ((0, 8),)),
        "heads_bias": centred(arg_keys[5], (2 * D,), 0.1, 1.5),
        "merge_weight": centred(arg_keys[6], (D, D), (max(1, D // 64)) ** -0.5, 1.5, ((0, 8),)),
        "merge_bias": centred(arg_keys[7], (D,), 0.3, 4.0),
        "up_weight": centred(arg_keys[8], (D, FF), D ** -0.5, 0.1875, ((0, 8),)),
        "up_bias": centred(arg_keys[9], (FF,), 0.3, 4.0),
        "down_weight": centred(arg_keys[10], (D, FF), (FF // 4) ** -0.5, 0.1875, ((0, 8),)),
        "down_bias": centred(arg_keys[11], (D,), 0.3, 4.0),
        "modulate_weight": centred(arg_keys[12], (D, 6 * D), D ** -0.5, 0.1875, ((0, 8),)),
        "modulate_bias": centred(arg_keys[13], (6 * D,), 0.3, 4.0),
        "relative_table": centred(arg_keys[14], (HEADS, RELS), 1.0, 6.0),
        "cotangent": centred(arg_keys[15], (TOKENS, D), 1.0, 6.0, ((0, 32),)),
    }


@jax.custom_vjp
def low(v):
    return lax.optimization_barrier(v.astype(jnp.bfloat16)).astype(jnp.float32)

@jax.custom_vjp
def low_back(v):
    return v

def low_keep(v):
    return (low(v), None)

def low_pass(kept, grad):
    return (grad,)

def back_keep(v):
    return (v, None)

def back_low(kept, grad):
    return (low(grad),)
low.defvjp(low_keep, low_pass)
low_back.defvjp(back_keep, back_low)
epsilon = 1e-06

def layer_norm(values):
    center = values - lax.optimization_barrier(jnp.mean(values, axis=-1, keepdims=True))
    spread = lax.optimization_barrier(jnp.mean(center * center, axis=-1, keepdims=True))
    return center * lax.rsqrt(spread + epsilon)

def matmul_high(left, right):
    return jnp.dot(left, right, precision=lax.Precision.HIGHEST, preferred_element_type=jnp.float32)

def relative_index(positions):
    row_place = positions // SIDE
    col_place = positions % SIDE
    row_gap = row_place[..., :, None] - row_place[..., None, :] + (SIDE - 1)
    col_gap = col_place[..., :, None] - col_place[..., None, :] + (SIDE - 1)
    return (row_gap * (2 * SIDE - 1) + col_gap).astype(jnp.int32)

def sample_attention(packed, length, positions, table):
    parts = packed.reshape(GRID, 3, HEADS, HEAD)
    scaling = 1.0 / math.sqrt(HEAD)
    scores = jnp.einsum('qhe,khe->hqk', parts[:, 0], parts[:, 1], precision=lax.Precision.HIGHEST) * scaling
    scores = low_back(scores + jnp.take(table, relative_index(positions), axis=1))
    living = jnp.arange(GRID) < length
    scores = jnp.where(living[None, None, :], scores, -1e+30)
    peak = lax.optimization_barrier(jnp.max(scores, axis=-1, keepdims=True))
    expo = jnp.exp(scores - peak)
    probs = low(expo / lax.optimization_barrier(jnp.sum(expo, axis=-1, keepdims=True)))
    mixed = jnp.einsum('hqk,khe->qhe', probs, parts[:, 2], precision=lax.Precision.HIGHEST)
    return low(low_back(mixed.reshape(GRID, D)))

def block_forward(slab, condition, lengths, kept_index, weights):
    heads_weight, heads_bias, merge_weight, merge_bias, up_weight, up_bias, down_weight, down_bias, modulate_weight, modulate_bias, relative_table = weights
    amount = condition.shape[0]
    silu_cond = low(jax.nn.silu(condition))
    modulation = low_back(matmul_high(silu_cond, modulate_weight) + modulate_bias).reshape(amount, 1, 6, D)
    shift_one = modulation[:, :, 0]
    scale_one = modulation[:, :, 1]
    gate_one = modulation[:, :, 2]
    shift_two = modulation[:, :, 3]
    scale_two = modulation[:, :, 4]
    gate_two = modulation[:, :, 5]
    values = slab.reshape(amount, GRID, D)
    hidden_one = low(layer_norm(values) * (1.0 + scale_one) + shift_one)
    full_bias = jnp.concatenate([heads_bias[:D], jnp.zeros((D,), jnp.float32), heads_bias[D:]])
    packed = low(low_back(matmul_high(hidden_one.reshape(amount * GRID, D), heads_weight) + full_bias))
    attend = jax.checkpoint(sample_attention)
    attended = lax.map(lambda items: attend(items[0], items[1], items[2], relative_table), (packed.reshape(amount, GRID, 3 * D), lengths, kept_index))
    attended = attended.reshape(amount * GRID, D)
    branch = low_back(matmul_high(attended, merge_weight) + merge_bias).reshape(amount, GRID, D)
    middle = values + gate_one * branch
    hidden_two = low(layer_norm(middle) * (1.0 + scale_two) + shift_two)
    up_value = low_back(matmul_high(hidden_two.reshape(amount * GRID, D), up_weight) + up_bias)
    activated = low(jax.nn.gelu(up_value, approximate=True))
    mlp_out = low_back(matmul_high(activated, down_weight.T) + down_bias).reshape(amount, GRID, D)
    living = (jnp.arange(GRID)[None, :] < lengths[:, None])[:, :, None]
    return jnp.where(living, middle + gate_two * mlp_out, 0.0).reshape(amount * GRID, D)

def reference(tokens, condition, lengths, kept_index, heads_weight, heads_bias, merge_weight, merge_bias, up_weight, up_bias, down_weight, down_bias, modulate_weight, modulate_bias, relative_table, cotangent):
    weights = tuple((item.astype(jnp.float32) for item in (heads_weight, heads_bias, merge_weight, merge_bias, up_weight, up_bias, down_weight, down_bias, modulate_weight, modulate_bias, relative_table)))
    group = math.gcd(SAMPLES, max(1, 4096 // GRID))
    rounds = SAMPLES // group
    inputs = (tokens.astype(jnp.float32).reshape(rounds, group * GRID, D), condition.astype(jnp.float32).reshape(rounds, group, D), lengths.reshape(rounds, group), kept_index.reshape(rounds, group, GRID), cotangent.astype(jnp.float32).reshape(rounds, group * GRID, D))

    def advance(totals, items):
        slab, cond_part, lens_part, index_part, cot_part = items

        def forward(values, params):
            return block_forward(values, cond_part, lens_part, index_part, params)
        result, pullback = jax.vjp(forward, slab, weights)
        slab_grad, weight_grads = pullback(cot_part)
        return (jax.tree.map(jnp.add, totals, weight_grads), (result, slab_grad))
    totals, (results, slab_grads) = lax.scan(advance, tuple((jnp.zeros_like(item) for item in weights)), inputs)
    return (results.reshape(TOKENS, D).astype(jnp.bfloat16), slab_grads.reshape(TOKENS, D), totals[0], totals[2], totals[4], totals[6], totals[8], totals[1], totals[3], totals[5], totals[7], totals[9], totals[10])
```

```python
import functools
import math

import jax
import jax.numpy as jnp
import numpy as np
from jax import lax
from jax.experimental import pallas as pl
from jax.experimental.pallas import tpu as pltpu
from jax.sharding import PartitionSpec as P

D = 1152
HEADS = 16
HEAD = 72
FF = 4608
SIDE = 16
GRID = 256
SPAN = 2 * SIDE - 1
WIDE = 4608
TILE = 768
ROWS8 = 144
QUARTERS = 4
LIFT = math.log2(math.e)
SCALE = 1.0 / math.sqrt(HEAD)
EPS = 1e-06
ORDER = (0, 4, 2, 6, 1, 5, 3, 7)
BF = jnp.bfloat16
F32 = jnp.float32
VMEM_LIMIT = 60 * 1024 * 1024


def dot(a, b):
    return jnp.dot(a, b, preferred_element_type=F32)


def dot_rt(a, b):
    return lax.dot_general(a, b, (((1,), (1,)), ((), ())), preferred_element_type=F32)


def dot_lt(a, b):
    return lax.dot_general(a, b, (((0,), (0,)), ((), ())), preferred_element_type=F32)


def params():
    return pltpu.CompilerParams(
        vmem_limit_bytes=VMEM_LIMIT, dimension_semantics=("arbitrary",)
    )


def cost(flops, bytes_accessed, transcendentals=0):
    return pl.CostEstimate(
        flops=int(flops), bytes_accessed=int(bytes_accessed), transcendentals=int(transcendentals)
    )


def rows_spec(width):
    return lambda first: pl.BlockSpec((GRID, width), lambda s, *_: (s + first, 0))


def own_rows(width):
    return lambda first: pl.BlockSpec((GRID, width), lambda s, *_: (s, 0))


def per_sample(*tail):
    return lambda first: pl.BlockSpec((1,) + tail, lambda s, *_: (s + first,) + (0,) * len(tail))


def fixed(*shape, at=None):
    where = (0,) * len(shape) if at is None else at
    return lambda first: pl.BlockSpec(shape, lambda s, *_: where)


def anywhere(first):
    return pl.BlockSpec(memory_space=pl.ANY)


def call(kernel, scal, inputs, in_specs, outs, scratch, span, name, price, prior=None, steps=None):
    first, samples = span
    kept = [] if prior is None else [(i, v) for i, v in enumerate(prior) if v is not None]
    count = len(inputs)

    def body(scal_ref, *refs):
        kernel(span, scal_ref, *refs[:count], *refs[count + len(kept) :])

    return pl.pallas_call(
        body,
        grid_spec=pltpu.PrefetchScalarGridSpec(
            num_scalar_prefetch=1,
            grid=(samples if steps is None else steps,),
            in_specs=[spec(first) for spec in in_specs] + [anywhere(first)] * len(kept),
            out_specs=[spec(first) for _, _, spec in outs],
            scratch_shapes=scratch,
        ),
        out_shape=[jax.ShapeDtypeStruct(shape, kind) for shape, kind, _ in outs],
        input_output_aliases={1 + count + n: i for n, (i, _) in enumerate(kept)},
        compiler_params=params(),
        cost_estimate=price,
        name=name,
    )(scal, *inputs, *[v for _, v in kept])


def normal(values):
    center = values - jnp.mean(values, axis=-1, keepdims=True)
    inverse = lax.rsqrt(jnp.mean(center * center, axis=-1, keepdims=True) + EPS)
    return center * inverse, inverse


def norm_back(unit, inverse, grad):
    return (
        grad
        - jnp.mean(grad, axis=-1, keepdims=True)
        - unit * jnp.mean(grad * unit, axis=-1, keepdims=True)
    ) * inverse


def accumulate(ref, value, step):
    @pl.when(step == 0)
    def _():
        ref[...] = value

    @pl.when(step > 0)
    def _():
        ref[...] = ref[...] + value


def column_sum(values):
    return jnp.sum(values.astype(F32), axis=0, keepdims=True)


def place_kernel(span, scal, tokens, cotangent, index, xg, cg, mask):
    length = scal[2 + span[0] + pl.program_id(0)]
    spots = lax.broadcasted_iota(jnp.int32, (GRID, GRID), 0)
    slots = lax.broadcasted_iota(jnp.int32, (GRID, GRID), 1)
    hit = spots == index[0]
    xg[...] = dot(hit.astype(F32).astype(BF), tokens[...]).astype(BF)
    alive = jnp.logical_and(hit, slots < length).astype(F32).astype(BF)
    cg[...] = dot(alive, cotangent[...]).astype(BF)
    row = dot_rt(jnp.ones((8, GRID), BF), alive)[0:1]
    mask[0] = jnp.where(row > 0.5, 0.0, -1e30)


def bias_kernel(span, scal, strips, out):
    strip = strips[0]
    for row in range(SIDE):
        start = (SIDE - 1 - row) * SIDE
        out[0, row * SIDE : (row + 1) * SIDE, :] = strip[:, start : start + GRID] * LIFT


def strips_kernel(span, scal, first, second, out):
    out[...] = jnp.zeros_like(out)
    for row in range(SIDE):
        start = (SIDE - 1 - row) * SIDE
        rows = slice(row * SIDE, (row + 1) * SIDE)
        out[0, :, start : start + GRID] = out[0, :, start : start + GRID] + (first[0, rows, :] + second[0, rows, :])


def window(h):
    start = jnp.minimum((h * HEAD) // 128 * 128, D - 256)
    lanes = lax.broadcasted_iota(jnp.int32, (1, 256), 1) + start
    inside = jnp.logical_and(lanes >= h * HEAD, lanes < (h + 1) * HEAD)
    return pl.multiple_of(start, 128), inside.astype(F32).astype(BF)


def piece_copies(pieces, gap_dp, scal, target, sems):
    copies = []
    for i, gap in enumerate(ORDER):
        rows = pl.ds(pl.multiple_of((scal[0] ^ gap) * ROWS8, ROWS8), ROWS8)
        source = pieces[2 * (gap_dp // 2) + i // 4].at[i % 4]
        copies.append(pltpu.make_async_copy(source, target.at[rows, :], sems.at[i]))
    return copies


def qkv_kernel(span, scal, xg, mods, full_bias, weight, h1, packed):
    unit, _ = normal(xg[...].astype(F32))
    hidden = (unit * (1.0 + mods[0, 1:2]) + mods[0, 0:1]).astype(BF)
    h1[...] = hidden
    for j in range(3):
        cols = slice(j * D, (j + 1) * D)
        packed[:, cols] = (dot(hidden, weight[j]) + full_bias[:, cols]).astype(BF)


def attend_kernel(span, scal, packed, mask, table, attended, lse, mixed):
    mixed[...] = jnp.zeros_like(mixed)
    lse[...] = jnp.zeros_like(lse)
    lane = lax.broadcasted_iota(jnp.int32, (GRID, 128), 1)

    def head(h, _):
        start, inside = window(h)
        query = packed[:, pl.ds(start, 256)] * inside
        key = packed[:, pl.ds(pl.multiple_of(D + start, 128), 256)]
        value = packed[:, pl.ds(pl.multiple_of(2 * D + start, 128), 256)] * inside
        scores = dot_rt(query, key) * (SCALE * LIFT) + table[h] + mask[0]
        peak = jnp.max(scores, axis=1, keepdims=True)
        expo = jnp.exp2(scores - peak)
        mass = jnp.sum(expo, axis=1, keepdims=True)
        probs = (expo * (1.0 / mass)).astype(BF)
        cols = pl.ds(start, 256)
        mixed[:, cols] = mixed[:, cols] + dot(probs, value)
        lse[...] = jnp.where(lane == h, peak + jnp.log2(mass), lse[...])
        return 0

    lax.fori_loop(0, HEADS, head, 0, unroll=HEADS)
    attended[...] = mixed[...].astype(BF)


def merge_kernel(span, scal, attended, xg, cg, mods, merge_bias, weight, branch, middle, h2, gm, gm_sum):
    low = (mods[0, 5:6] * cg[...].astype(F32)).astype(BF)
    gm[...] = low
    accumulate(gm_sum, column_sum(low), pl.program_id(0))
    merged = dot(attended[...], weight[0]) + merge_bias[...]
    branch[...] = merged.astype(BF)
    mid = xg[...].astype(F32) + mods[0, 2:3] * merged
    middle[...] = mid
    unit, _ = normal(mid)
    h2[...] = (unit * (1.0 + mods[0, 4:5]) + mods[0, 3:4]).astype(BF)


def up_kernel(samples, gaps, scal, quarters, h2, bias, *refs):
    step = pl.program_id(0)
    if gaps is None:
        weight, act, slope = refs
        matrix = lambda: weight[0]
    else:
        pieces = refs[:4]
        act, slope, spread, target, sems, out_sems = refs[4:]
        steps = len(gaps)
        matrix = lambda: target[step]
        fetch = [piece_copies(pieces, gap, scal, target.at[n], sems.at[n]) for n, gap in enumerate(gaps)]
        store = [pltpu.make_async_copy(target.at[n], spread.at[n], out_sems.at[n]) for n in range(steps)]
        for n in range(steps):
            @pl.when(step == 0)
            def _():
                for copy in fetch[n]:
                    copy.start()
        for n in range(steps):
            @pl.when(step == n)
            def _():
                for copy in fetch[n]:
                    copy.wait()
                store[n].start()

    root = math.sqrt(2.0 / math.pi)
    for s in range(samples):
        rows = slice(s * GRID, (s + 1) * GRID)
        u = dot(h2[rows, :], matrix()) + bias[...]
        square = u * u
        t = jnp.tanh(u * ((root * 0.044715) * square + root))
        half = 0.5 * t + 0.5
        act[rows, :] = (u * half).astype(BF)
        bell = half * (1.0 - half)
        slope[rows, :] = (half + bell * (u * ((6 * root * 0.044715) * square + 2 * root))).astype(BF)
    if gaps is not None:
        for n in range(steps):
            @pl.when(step == steps - 1)
            def _():
                store[n].wait()


def up_quarters(h2, bias, weight, scal, quarters, gaps):
    count, steps = h2.shape[0], quarters.shape[0]
    column = pl.BlockSpec((None, count, D), lambda k, *_: (k, 0, 0))
    out = [jax.ShapeDtypeStruct((steps, count, D), BF)] * 2
    if gaps is None:
        weight = [weight]
        weight_specs, out_specs, scratch = [pl.BlockSpec((1, D, D), lambda k, scal, q: (q[k], 0, 0))], [column] * 2, []
    else:
        weight_specs, out_specs = [anywhere(0)] * 4, [column] * 2 + [anywhere(0)]
        out = out + [jax.ShapeDtypeStruct((steps, D, D), BF)]
        scratch = [pltpu.VMEM((steps, D, D), BF), pltpu.SemaphoreType.DMA((steps, 8)), pltpu.SemaphoreType.DMA((steps,))]
    return pl.pallas_call(
        functools.partial(up_kernel, count // GRID, gaps),
        grid_spec=pltpu.PrefetchScalarGridSpec(
            num_scalar_prefetch=2,
            grid=(steps,),
            in_specs=[pl.BlockSpec((count, D), lambda k, *_: (0, 0)), pl.BlockSpec((1, D), lambda k, scal, q: (0, q[k]))]
            + weight_specs,
            out_specs=out_specs,
            scratch_shapes=scratch,
        ),
        out_shape=out,
        compiler_params=params(),
        cost_estimate=cost(2 * count * D * D * steps, 2 * D * steps * (3 * count + 2 * D), count * D * steps),
        name="up",
    )(scal, quarters, h2, bias, *weight)


def act_back_kernel(samples, scal, quarters, gm, slope, weight, *refs):
    gu, gu_sum = refs[-2:]
    total = jnp.zeros((1, D), F32)
    for s in range(samples):
        rows = slice(s * GRID, (s + 1) * GRID)
        low = (dot(gm[rows, :], weight[0]) * slope[rows, :].astype(F32)).astype(BF)
        gu[0, rows, :] = low
        total = total + column_sum(low)
    gu_sum[...] = total


def act_back(gm, slope, weight, scal, quarters, prior):
    count, steps = gm.shape[0], quarters.shape[0]
    whole = pl.BlockSpec((count, D), lambda k, *_: (0, 0))
    return pl.pallas_call(
        functools.partial(act_back_kernel, count // GRID),
        grid_spec=pltpu.PrefetchScalarGridSpec(
            num_scalar_prefetch=2,
            grid=(steps,),
            in_specs=[
                whole,
                pl.BlockSpec((None, count, D), lambda k, *_: (k, 0, 0)),
                pl.BlockSpec((1, D, D), lambda k, scal, q: (q[k], 0, 0)),
            ]
            + [anywhere(0)] * (prior is not None),
            out_specs=[
                pl.BlockSpec((1, count, D), lambda k, *_: (k, 0, 0)),
                pl.BlockSpec((1, D), lambda k, scal, q: (0, q[k])),
            ],
        ),
        out_shape=[jax.ShapeDtypeStruct((steps, count, D), BF), jax.ShapeDtypeStruct((1, FF), F32)],
        input_output_aliases={} if prior is None else {5: 1},
        compiler_params=params(),
        cost_estimate=cost(2 * count * D * D * steps, 2 * D * steps * (2 * count + D)),
        name="act_back",
    )(scal, quarters, gm, slope, weight, *([] if prior is None else [prior]))


def turned_product(parts, scal, quarters, weights, late, late_specs, outs, finish, span, name, prior=None):
    first, samples = span
    count, tiles = samples * GRID, quarters.shape[0]
    kept = [] if prior is None else [(i, v) for i, v in enumerate(prior) if v is not None]
    starts = np.minimum(np.cumsum([0] + [p.shape[0] if p.ndim == 3 else p.shape[1] // D for p in parts]), tiles)
    used = len(parts) + len(weights)

    def body(scal_ref, quarters_ref, *refs):
        total = refs[-1]
        ins, ws = refs[: len(parts)], refs[len(parts) : used]
        late_refs = refs[used : used + len(late)]
        out_refs = refs[used + len(late) + len(kept) : -1]
        step = pl.program_id(0)
        for n, ref in enumerate(ins):
            w = ws[n % len(ws)]

            @pl.when(jnp.logical_and(step >= starts[n], step < starts[n + 1]))
            def _():
                for s in range(samples):
                    part = dot_rt(ref[s * GRID : (s + 1) * GRID, :], w[0])

                    @pl.when(step == 0)
                    def _():
                        total[s] = part

                    @pl.when(step > 0)
                    def _():
                        total[s] = total[s] + part

        @pl.when(step >= tiles)
        def _():
            finish(span, scal_ref, step - tiles, total[step - tiles], late_refs, out_refs)

    def shift(spec):
        block = spec(first)
        return pl.BlockSpec(block.block_shape, lambda k, *a: block.index_map(jnp.maximum(k - tiles, 0), *a))

    def part_spec(n):
        low, high = int(starts[n]), int(starts[n + 1]) - 1
        offset = 0 if parts[n].shape[-2] == count else first // samples
        return column_block(parts[n], count, D, lambda k, *_: jnp.clip(k, low, high) - low, offset)

    def weight_spec(n):
        if len(weights) == 1:
            return pl.BlockSpec((1, D, D), lambda k, scal, q: (q[jnp.minimum(k, tiles - 1)], 0, 0))
        low, high = int(starts[n]), int(starts[n + 1]) - 1
        return pl.BlockSpec((1, D, D), lambda k, *_: (jnp.clip(k, low, high) - low, 0, 0))

    return pl.pallas_call(
        body,
        grid_spec=pltpu.PrefetchScalarGridSpec(
            num_scalar_prefetch=2,
            grid=(tiles + samples,),
            in_specs=[part_spec(n) for n in range(len(parts))]
            + [weight_spec(n) for n in range(len(weights))]
            + [shift(spec) for spec in late_specs]
            + [anywhere(0)] * len(kept),
            out_specs=[shift(spec) for _, _, spec in outs],
            scratch_shapes=[pltpu.VMEM((samples, GRID, D), F32)],
        ),
        out_shape=[jax.ShapeDtypeStruct(shape, kind) for shape, kind, _ in outs],
        input_output_aliases={2 + used + len(late) + n: i for n, (i, _) in enumerate(kept)},
        compiler_params=params(),
        cost_estimate=cost(2 * count * D * D * tiles, 2 * D * tiles * (count + D) + 10 * count * D),
        name=name,
    )(scal, quarters, *parts, *weights, *late, *[v for _, v in kept])


def mid_back_finish(span, scal, sample, grad, late, outs):
    middle, branch, cg, mods = late
    gmid, gbr, gbr_sum, grads = outs
    unit, inverse = normal(middle[...])
    whole = cg[...].astype(F32) + norm_back(unit, inverse, grad * (1.0 + mods[0, 4:5]))
    gmid[...] = whole
    low = (mods[0, 2:3] * whole).astype(BF)
    gbr[...] = low
    accumulate(gbr_sum, column_sum(low), sample)
    grads[0, 0:1] = column_sum(whole * branch[...].astype(F32))
    grads[0, 1:2] = column_sum(grad)
    grads[0, 2:3] = column_sum(grad * unit)


def front_back_finish(span, scal, sample, grad, late, outs):
    xg, gmid, mods, column = late
    tgrad, grads = outs
    unit, inverse = normal(xg[...].astype(F32))
    grads[0, 0:1] = column_sum(grad)
    grads[0, 1:2] = column_sum(grad * unit)
    whole = gmid[...] + norm_back(unit, inverse, grad * (1.0 + mods[0, 1:2]))
    pick = (lax.broadcasted_iota(jnp.int32, (GRID, GRID), 1) == column[...]).astype(F32).astype(BF)
    high = whole.astype(BF)
    rest = (whole - high.astype(F32)).astype(BF)
    tgrad[...] = dot(pick, high) + dot(pick, rest)


def down_finish(span, scal, sample, product, late, outs):
    middle, cg, mods, bias, column = late
    out, grads = outs
    mlp = product + bias[...]
    grads[0] = column_sum(cg[...].astype(F32) * mlp)
    final = (middle[...] + mods[0, 5:6] * mlp).astype(BF)
    length = scal[2 + span[0] + sample]
    spots = lax.broadcasted_iota(jnp.int32, (GRID, GRID), 1)
    slots = lax.broadcasted_iota(jnp.int32, (GRID, GRID), 0)
    pick = jnp.logical_and(spots == column[...], slots < length).astype(F32).astype(BF)
    out[...] = dot(pick, final).astype(BF)


def attend_back_kernel(span, scal, gbr, packed, lse, mask, table, weight, joined, joined_sum, placed, gatt, gq, gk, gv):
    gatt[...] = dot_rt(gbr[...], weight[0]).astype(BF)
    for ref in (gq, gk, gv):
        ref[...] = jnp.zeros_like(ref)

    @pl.when(pl.program_id(0) == 0)
    def _():
        placed[...] = jnp.zeros_like(placed)
        joined_sum[...] = jnp.zeros_like(joined_sum)

    lane = lax.broadcasted_iota(jnp.int32, (GRID, 128), 1)

    def head(h, _):
        start, inside = window(h)
        cols = pl.ds(start, 256)
        query = packed[:, cols] * inside
        key = packed[:, pl.ds(pl.multiple_of(D + start, 128), 256)] * inside
        value = packed[:, pl.ds(pl.multiple_of(2 * D + start, 128), 256)]
        grad = gatt[:, cols] * inside
        scores = dot_rt(query, key) * (SCALE * LIFT) + table[h] + mask[0]
        own = jnp.sum(jnp.where(lane == h, lse[...], 0.0), axis=1, keepdims=True)
        probs = jnp.exp2(scores - own)
        gprobs = dot_rt(grad, value)
        weighted = probs * gprobs
        inner = jnp.sum(weighted, axis=1, keepdims=True)
        gscores = (weighted - probs * inner).astype(BF)
        placed[h] = placed[h] + gscores.astype(F32)
        gq[:, cols] = gq[:, cols] + dot(gscores, key)
        gk[:, cols] = gk[:, cols] + dot_lt(gscores, query)
        gv[:, cols] = gv[:, cols] + dot_lt(probs.astype(BF), grad)
        return 0

    lax.fori_loop(0, HEADS, head, 0, unroll=HEADS)
    for j, (ref, factor) in enumerate(((gq, SCALE), (gk, SCALE), (gv, 1.0))):
        cols = slice(j * D, (j + 1) * D)
        low = (ref[...] * factor).astype(BF)
        joined[:, cols] = low
        joined_sum[:, cols] = joined_sum[:, cols] + column_sum(low)
    joined[:, 3 * D :] = gbr[...]


def column_block(array, rows, width, at, row=0):
    if array.ndim == 2:
        return pl.BlockSpec((rows, width), lambda *a: (row, at(*a)))
    return pl.BlockSpec((None, rows, width), lambda *a: (at(*a), row, 0))


def plain_outer_kernel(kinds, scal, *refs):
    lefts, (right, out) = refs[:kinds], refs[kinds:]
    for kind, left in enumerate(lefts):
        def product():
            out[0] = dot_lt(left[...], right[...]).astype(BF)

        if kinds == 1:
            product()
        else:
            pl.when((pl.program_id(0) == QUARTERS - 1) == (kind == 1))(product)


def plain_outer(lefts, right, scal, name):
    count = right.shape[-2]
    return pl.pallas_call(
        functools.partial(plain_outer_kernel, len(lefts)),
        grid_spec=pltpu.PrefetchScalarGridSpec(
            num_scalar_prefetch=1,
            grid=(QUARTERS,),
            in_specs=[pl.BlockSpec((count, D), lambda q, *_: (0, 0))] * len(lefts)
            + [column_block(right, count, D, lambda q, *_: q)],
            out_specs=pl.BlockSpec((1, D, D), lambda q, *_: (q, 0, 0)),
        ),
        out_shape=jax.ShapeDtypeStruct((QUARTERS, D, D), BF),
        compiler_params=params(),
        cost_estimate=cost(2 * count * D * WIDE, 2 * count * (D + WIDE) + 2 * D * WIDE),
        name=name,
    )(scal, *lefts, right)


def outer_kernel(kinds, sources, tile_width, roles, parts, order, scal, blocks, *refs):
    lefts, rights = refs[: sources * kinds], refs[sources * kinds : sources * (kinds + 1)]
    outs, tile = refs[sources * (kinds + 1) : -1], refs[-1]
    step = pl.program_id(0)

    def product(kind, cols):
        total = dot_lt(lefts[sources * kind][...], rights[0][:, cols])
        for n in range(1, sources):
            total = total + dot_lt(lefts[sources * kind + n][...], rights[n][:, cols])
        tile[:, cols] = total.astype(BF)

    if kinds == 1:
        product(0, slice(0, tile_width))
    else:
        half = tile_width // 2
        for part in range(2):
            from_first = blocks[step] * 2 + part < 3 * D // half
            cols = slice(part * half, (part + 1) * half)
            pl.when(from_first)(functools.partial(product, 0, cols))
            pl.when(jnp.logical_not(from_first))(functools.partial(product, 1, cols))
    for r in range(roles):
        @pl.when(step == r)
        def _():
            for i in range(8):
                start = i * ROWS8 if order is None else pl.multiple_of((scal[0] ^ order[i]) * ROWS8, ROWS8)
                rows = pl.ds(start, ROWS8)
                outs[parts * r + i * parts // 8][i % (8 // parts)] = tile[rows, :]


def outer_tiles(lefts, rights, scal, blocks, width, parts, order, name):
    count, kinds, roles, sources = rights[0].shape[-2], len(lefts), blocks.shape[0], len(rights)
    some = pl.BlockSpec((8 // parts, ROWS8, width), lambda r, *_: (0, 0, 0))
    each = sources // len(lefts[0])
    left_specs = [pl.BlockSpec((count, D), lambda r, *_, n=n: (n, 0)) for n in range(each)] * (len(lefts[0]) * kinds)
    return pl.pallas_call(
        functools.partial(outer_kernel, kinds, sources, width, roles, parts, order),
        grid_spec=pltpu.PrefetchScalarGridSpec(
            num_scalar_prefetch=2,
            grid=(roles,),
            in_specs=left_specs + [column_block(rights[0], count, width, lambda r, scal, blocks: blocks[r])] * sources,
            out_specs=[some] * (parts * roles),
            scratch_shapes=[pltpu.VMEM((D, width), BF)],
        ),
        out_shape=[jax.ShapeDtypeStruct((8 // parts, ROWS8, width), BF)] * (parts * roles),
        compiler_params=params(),
        cost_estimate=cost(
            2 * sources * count * D * width * roles, 2 * sources * count * (D * kinds + width * roles)
        ),
        name=name,
    )(scal, blocks, *[v for left in lefts for v in left for _ in range(each)], *rights)


ON_THE_WAY = []


def flip(value, axis, size, bit):
    ON_THE_WAY.append(lax.ppermute(value, axis, [(i, i ^ bit) for i in range(size)]))
    return ON_THE_WAY[-1]


def bits_of(size):
    return [1 << k for k in range(size.bit_length() - 1)]


def gather_steps(value, axes):
    for axis, size in axes:
        own = lax.axis_index(axis)
        for bit in bits_of(size):
            (value,) = yield [value]
            other = flip(value, axis, size, bit)
            low = (own & bit) == 0
            value = jnp.concatenate([jnp.where(low, value, other), jnp.where(low, other, value)], axis=0)
    return value


def scatter_steps(value, axis, size):
    own = lax.axis_index(axis)
    for bit in bits_of(size):
        value = value.reshape((value.shape[0] // 2, 2) + value.shape[1:])
        low = (own & bit) == 0
        keep = jnp.where(low, value[:, 0], value[:, 1])
        send = jnp.where(low, value[:, 1], value[:, 0]).astype(BF)
        (send,) = yield [send]
        value = keep + flip(send, axis, size, bit).astype(F32)
    return value


class Chain:
    def __init__(self, steps):
        self.steps, self.result = steps, None
        self.ready = next(steps)

    def advance(self, operands):
        if self.result is None:
            try:
                self.ready = self.steps.send(operands)
            except StopIteration as end:
                self.ready, self.result = [], end.value

    def finish(self):
        while self.result is None:
            self.advance(self.ready)
        return self.result


def slot(inputs, chains=(), after=(), slow=()):
    chains, slow = list(chains), list(slow)
    inputs, operands, _ = lax.optimization_barrier(
        (tuple(inputs), [c.ready for c in chains + slow], (*after, *ON_THE_WAY))
    )
    ON_THE_WAY.clear()
    for chain, ready in zip(slow, operands[len(chains) :]):
        chain.advance(ready)
    ON_THE_WAY.clear()
    for chain, ready in zip(chains, operands):
        chain.advance(ready)
    return inputs


class Wires:
    def __init__(self, mesh):
        self.dp, self.seq = mesh.shape["dp"], mesh.shape["seq"]
        self.cube = self.dp == 4 and self.seq == 8
        self.place, self.me = lax.axis_index("dp"), lax.axis_index("seq")

    def far(self, value, bit):
        return flip(value, "seq", self.seq, bit)

    def across(self, value):
        return flip(value, "dp", self.dp, 2)

    def sibling(self, value):
        return flip(value, "dp", self.dp, 1)

    def quarter(self, shards):
        if len(shards) == 1:
            return lax.dynamic_slice_in_dim(shards[0], self.place * D, D, 1)[None]
        heads = lax.dynamic_slice_in_dim(shards[0], jnp.minimum(self.place, 2) * D, D, 1)
        return jnp.where(self.place == 3, shards[1], heads)[None]

    def gather(self, quarter):
        return lax.all_gather(quarter, ("dp", "seq"), axis=0, tiled=True).reshape(QUARTERS, D, D)

    def gather_steps(self, quarter):
        (one,) = yield [quarter]
        two = jnp.concatenate([one, self.far(one, 4)], axis=0)
        (two,) = yield [two]
        four = jnp.concatenate([two, self.far(two, 2)], axis=0)
        (four,) = yield [four]
        rest, cross = self.far(four, 1), self.across(four)
        rest, cross, four = yield [rest, cross, four]
        cross_rest, near = self.across(rest), [self.sibling(four), self.sibling(rest), self.sibling(cross)]
        cross_rest, *near = yield [cross_rest, *near]
        return [four, rest, cross, cross_rest], [*near, self.sibling(cross_rest)]

    def scatter(self, whole):
        rows = D // self.seq
        parts = whole.reshape(QUARTERS * self.seq, rows, D)
        return lax.psum_scatter(parts, ("dp", "seq"), scatter_dimension=0, tiled=True)

    def spread(self, part):
        parts = yield from gather_steps(part, (("dp", self.dp),))
        return jnp.concatenate([parts[q] for q in range(QUARTERS)], axis=1)

    def reduce_quarter(self, cross, quarter, groups):
        got = {}
        for group in groups:
            sent = yield [cross[part] for part in group]
            for part, value in zip(group, sent):
                got[part] = self.across(value)
        upper = [(quarter[part].astype(F32) + got[part].astype(F32)).astype(BF) for part in (2, 3)]
        left = [part for part in (0, 1) if part not in got]
        send, *sent = yield [jnp.concatenate(upper, axis=0)] + [cross[part] for part in left]
        near = self.far(send, 1)
        for part, value in zip(left, sent):
            got[part] = self.across(value)
        (send,) = yield [(total_of([quarter[1], got[1]], 0, 2) + near[2:4].astype(F32)).astype(BF)]
        parts = [quarter[0], got[0], near, self.far(send, 2)]
        (send,) = yield [total_of(parts, 1, 2).astype(BF)]
        parts.append(self.far(send, 4))
        return (yield from self.spread(total_of(parts, 0, 1).astype(BF)))

    def reduce(self, give):
        core, x = self.place % 2, self.place // 2
        give = yield [give[1], give[0], give[2]]
        got = [self.sibling(value) for value in give]
        keep = yield []
        cross, quarter, common = [keep[1], got[0]], [keep[0], got[1]], [keep[2], got[2]]
        (high,) = yield [total_of(cross, 4, 8).astype(BF)]
        high = self.across(high)
        low, send = yield [total_of(cross, 0, 4).astype(BF), total_of(common, 4, 8).astype(BF)]
        low = self.across(low)
        common.append(self.far(send, 1))
        send, other = yield [
            (total_of(quarter, 4, 8) + high.astype(F32)).astype(BF), total_of(common, 2, 4).astype(BF)
        ]
        quarter += [low, self.far(send, 1)]
        common.append(self.far(other, 2))
        send, other = yield [total_of(quarter, 2, 4).astype(BF), total_of(common, 1, 2).astype(BF)]
        quarter.append(self.far(send, 2))
        common.append(self.far(other, 4))
        send, end = yield [total_of(quarter, 1, 2).astype(BF), total_of(common, 0, 1).astype(BF)]
        quarter.append(self.far(send, 4))
        (ends,) = yield [jnp.concatenate([total_of(quarter, 0, 1).astype(BF), end], axis=0)]
        other = self.across(ends)
        shared = (ends[1].astype(F32) + other[1].astype(F32)).astype(BF)
        (mine,) = yield [jnp.stack([ends[0], other[0], shared])]
        theirs = self.sibling(mine)
        columns = []
        first, left = core == 0, x == 0
        for quarter_index in range(4):
            of_core, of_x = divmod(quarter_index, 2)
            near, far = (mine, theirs) if of_core == 0 else (theirs, mine)
            same = jnp.where(first, near[:2], far[:2])
            columns.append(jnp.where(left == (of_x == 0), same[0], same[1]))
        columns.append(jnp.where(first, mine[2], theirs[2]))
        columns.append(jnp.where(first, theirs[2], mine[2]))
        return jnp.concatenate(columns, axis=1)

    def roles(self):
        core, x = self.place % 2, self.place // 2
        return jnp.stack([2 * core + x, 2 * core + 1 - x, 4 + core]).astype(jnp.int32)


def total_of(parts, start, stop):
    summed = 0.0
    for part in parts:
        summed = summed + part[start:stop].astype(F32)
    return summed


def unit_gaps():
    spots = np.arange(SIDE)
    reach = np.arange(SPAN)
    return (spots[None, :, None] - spots[None, None, :] + (SIDE - 1) == reach[:, None, None]).astype(np.float32)


def local(
    mesh,
    tokens,
    condition,
    lengths,
    kept_index,
    heads_weight,
    heads_bias,
    merge_weight,
    merge_bias,
    up_weight,
    up_bias,
    down_weight,
    down_bias,
    modulate_weight,
    modulate_bias,
    relative_table,
    cotangent,
):
    ON_THE_WAY.clear()
    wires = Wires(mesh)
    dp, seq = wires.dp, wires.seq
    samples, count = kept_index.shape[0], tokens.shape[0]
    shard_rows = heads_weight.shape[0]
    everything, half_a, half_b = (0, samples), (0, samples // 2), (samples // 2, samples - samples // 2)
    everyone = (("seq", seq), ("dp", dp))
    line = lambda v: v.astype(F32).reshape(1, -1)
    scal = jnp.concatenate([jnp.stack([wires.me, wires.place]).astype(jnp.int32), lengths])
    in_order = jnp.arange(QUARTERS, dtype=jnp.int32)

    own_cols = lax.dynamic_slice_in_dim(condition, wires.me * shard_rows, shard_rows, 1)
    own_silu = jax.nn.silu(own_cols.astype(F32)).astype(BF)
    partial = dot(own_silu, modulate_weight).reshape(seq, samples, 6 * D)
    mod_chain = Chain(scatter_steps(partial, "seq", seq))
    cond_chain = Chain(gather_steps(own_cols, (("dp", dp),)))
    joint = wires.gather(wires.quarter([heads_weight, merge_weight]))
    up_chain = [Chain(wires.gather_steps(wires.quarter([up_weight])))] if wires.cube else []
    upw = None if wires.cube else wires.gather(wires.quarter([up_weight]))

    index_row = kept_index.reshape(samples, 1, GRID)
    index_col = kept_index.reshape(count, 1)
    inputs = slot((tokens, cotangent, index_row), [cond_chain], slow=up_chain)
    xg, cg, mask = call(
        place_kernel, scal, inputs, [rows_spec(D), rows_spec(D), per_sample(1, GRID)],
        [((count, D), BF, rows_spec(D)), ((count, D), BF, rows_spec(D)), ((samples, 1, GRID), F32, per_sample(1, GRID))],
        [], everything, "place", cost(4 * count * GRID * D, 8 * count * D),
    )
    (later, _) = lax.optimization_barrier((down_weight, mask))
    downw = wires.gather(wires.quarter([later]))

    gaps = unit_gaps()
    turned = relative_table.reshape(HEADS, SPAN, SPAN)[:, ::-1]
    strips = jnp.einsum("hkj,jpq->hpkq", turned, jnp.asarray(gaps, BF), preferred_element_type=F32)
    strips = jnp.pad(strips.reshape(HEADS, SIDE, SPAN * SIDE), ((0, 0), (0, 0), (0, SIDE)))
    inputs = slot((strips,), up_chain + [mod_chain, cond_chain], (mask,))
    (table,) = call(
        bias_kernel, scal, inputs, [per_sample(SIDE, 2 * GRID)], [((HEADS, GRID, GRID), F32, per_sample(GRID, GRID))],
        [], (0, HEADS), "bias", cost(0, 5 << 20),
    )
    (table,) = slot((table,), [mod_chain], slow=up_chain)
    (table,) = slot((table,), [mod_chain])
    modulation = mod_chain.finish().reshape(samples, 6 * D) + modulate_bias.astype(F32)
    mods = modulation.reshape(samples, 6, D)

    full_bias = jnp.concatenate([heads_bias[:D], jnp.zeros((D,), BF), heads_bias[D:]])
    inputs = slot((xg, mods, line(full_bias), joint), slow=up_chain, after=(table,))
    h1, packed = call(
        qkv_kernel, scal, inputs,
        [rows_spec(D), per_sample(6, D), fixed(1, 3 * D), fixed(3, D, D)],
        [((count, D), BF, rows_spec(D)), ((count, 3 * D), BF, rows_spec(3 * D))],
        [], everything, "qkv", cost(2 * count * D * 3 * D, 22 << 20),
    )
    inputs = slot((packed, mask, table))
    attended, lse = call(
        attend_kernel, scal, inputs, [rows_spec(3 * D), per_sample(1, GRID), fixed(HEADS, GRID, GRID)],
        [((count, D), BF, rows_spec(D)), ((count, 128), F32, rows_spec(128))],
        [pltpu.VMEM((GRID, D), F32)], everything, "attend", cost(4 * count * GRID * 256 * HEADS, 15 << 20, count * GRID * HEADS),
    )
    inputs = slot((attended, xg, cg, mods, line(merge_bias), joint), slow=up_chain)
    branch, middle, h2, gm, gm_sum = call(
        merge_kernel, scal, inputs,
        [rows_spec(D), rows_spec(D), rows_spec(D), per_sample(6, D), fixed(1, D), fixed(1, D, D, at=(3, 0, 0))],
        [((count, D), BF, rows_spec(D)), ((count, D), F32, rows_spec(D)), ((count, D), BF, rows_spec(D)),
         ((count, D), BF, rows_spec(D)), ((1, D), F32, fixed(1, D))],
        [], everything, "merge", cost(2 * count * D * D, 20 << 20),
    )

    def pair(values):
        return [[v, wires.sibling(v)] for v in values]

    up_line, sums = line(up_bias), []
    if wires.cube:
        place = wires.place.astype(jnp.int32)
        own_quarters, their_quarters = jnp.stack([place, place ^ 2]), jnp.stack([place ^ 1, place ^ 3])
        order, cross_first = jnp.concatenate([own_quarters, their_quarters]), jnp.array([1, 0], jnp.int32)
        own_pieces, their_pieces = up_chain[0].finish()
        h2, *their_pieces = slot((h2, *their_pieces))
        act_theirs, slope_theirs, up_theirs = up_quarters(h2, up_line, their_pieces, scal, their_quarters, (1, 3))
        h2, *own_pieces = slot((h2, *own_pieces), after=(act_theirs,))
        arrived = wires.sibling(act_theirs)
        gm_pair, h2_pair = pair([gm, h2])
        act_own, slope_own, up_own = up_quarters(h2, up_line, own_pieces, scal, own_quarters, (0, 2))
        acts, upws = [act_own, act_theirs], [up_own, up_theirs]
        act_own, arrived = slot((act_own, arrived))
        tiles = outer_tiles([gm_pair], [act_own, arrived], scal, cross_first, D, 4, ORDER, "down_outer")
        down_sum = Chain(wires.reduce_quarter(tiles[:4], tiles[4:], ((2,), (3,))))
        gm, slope_theirs, downw = slot((gm, slope_theirs, downw), after=(tiles[0],))
        gu_theirs, gu_sum = act_back(gm, slope_theirs, downw, scal, their_quarters, None)
        gm, slope_own, downw, gu_sum = slot((gm, slope_own, downw, gu_sum), [down_sum], (gu_theirs,))
        arrived = wires.sibling(gu_theirs)
        gu_own, gu_sum = act_back(gm, slope_own, downw, scal, own_quarters, gu_sum)
        gu_parts = [gu_own, gu_theirs]
        gu_own, arrived = slot((gu_own, arrived), [down_sum])
        tiles = outer_tiles([h2_pair], [gu_own, arrived], scal, cross_first, D, 4, ORDER, "up_outer")
        up_sum = Chain(wires.reduce_quarter(tiles[:4], tiles[4:], ((2, 3),)))
        sums = [down_sum, up_sum]
        gu_parts = slot(gu_parts, [down_sum], (tiles[0],))
    else:
        order, upws = in_order, [upw]
        act, slope = up_quarters(h2, up_line, upw, scal, in_order, None)
        down_part = wires.scatter(plain_outer([gm], act, scal, "down_outer"))
        gu, gu_sum = act_back(gm, slope, downw, scal, in_order, None)
        up_part = wires.scatter(plain_outer([h2], gu, scal, "up_outer"))
        acts, gu_parts = [act], [gu]

    gmid, gbr, gbr_sum, mid_grads = turned_product(
        gu_parts, scal, order, upws, (middle, branch, cg, mods), [rows_spec(D), rows_spec(D), rows_spec(D), per_sample(6, D)],
        [((count, D), F32, rows_spec(D)), ((count, D), BF, rows_spec(D)), ((1, D), F32, fixed(1, D)), ((samples, 3, D), F32, per_sample(3, D))],
        mid_back_finish, everything, "mid_back",
    )
    mid_all = lax.all_gather(mid_grads.reshape(1, samples * 3, D), ("dp", "seq"), axis=0, tiled=True)
    mid_all = mid_all.astype(BF).reshape(-1, 3 * D)
    def attend_part(chains, after, span):
        inputs = slot((gbr, packed, lse, mask, table, joint), chains, after)
        return call(
            attend_back_kernel, scal, inputs,
            [rows_spec(D), rows_spec(3 * D), rows_spec(128), per_sample(1, GRID), fixed(HEADS, GRID, GRID), fixed(1, D, D, at=(3, 0, 0))],
            [((span[1] * GRID, WIDE), BF, own_rows(WIDE)),
             ((1, 3 * D), F32, fixed(1, 3 * D)), ((HEADS, GRID, GRID), F32, fixed(HEADS, GRID, GRID))],
            [pltpu.VMEM((GRID, D), BF)] + [pltpu.VMEM((GRID, D), F32)] * 3,
            span, "attend_back", cost(count * D * D + 5 * count * GRID * 256 * HEADS, 20 << 20),
        )

    joined_a, joined_sum_a, placed_a = attend_part(sums, (), half_a)
    joined_b, joined_sum_b, placed_b = attend_part(sums, (joined_a,), half_b)
    joined_sum = joined_sum_a + joined_sum_b

    done = joined_b
    if wires.cube:
        lefts, roles = [[h1], [attended]], wires.roles()
        theirs = jnp.stack([roles[0] ^ 2, roles[1] ^ 2, roles[2] ^ 1])
        rights = slot((joined_a, joined_b), slow=sums)
        give = outer_tiles(lefts, rights, scal, theirs, TILE, 1, ORDER, "joint_give")
        joint_sum = Chain(wires.reduce(give))
        rights = slot(rights, [joint_sum], (give[0],), slow=sums[:1])
        keep = outer_tiles(lefts, rights, scal, roles, TILE, 1, ORDER, "joint_keep")
        joint_sum.ready = tuple(keep)
        joint_sum.advance(joint_sum.ready)
        done = keep[0]

    joints = [joint_sum] if wires.cube else []
    placed_a, placed_b = slot((placed_a, placed_b), sums[1:], (done,), slow=joints)
    (strip_grad,) = call(
        strips_kernel, scal, (placed_a, placed_b), [per_sample(GRID, GRID)] * 2,
        [((HEADS, SIDE, 2 * GRID), F32, per_sample(SIDE, 2 * GRID))], [], (0, HEADS), "strips", cost(0, 9 << 20),
    )
    strip_grad = strip_grad[:, :, : SPAN * SIDE].reshape(HEADS, SIDE, SPAN, SIDE)
    table_grad = jnp.einsum(
        "hpkq,jpq->hkj", strip_grad, jnp.asarray(gaps), precision=lax.Precision.HIGHEST
    )[:, ::-1].reshape(-1)
    sizes = [2 * D, D, FF, D, HEADS * SPAN * SPAN]
    loose = jnp.concatenate(
        [joined_sum[0, :D], joined_sum[0, 2 * D :], gbr_sum[0], gu_sum[0], gm_sum[0], table_grad]
    )
    loose = jnp.pad(loose, (0, -loose.shape[0] % 1024)).reshape(-1, 128)
    loose = jnp.sum(lax.all_gather(loose, ("dp", "seq")), axis=0)
    done = strip_grad
    def front_part(own, chains, after, span, prior):
        (own,) = slot((own,), chains, after)
        return turned_product(
            [own], scal, in_order[:3], [joint], (xg, gmid, mods, index_col),
            [rows_spec(D), rows_spec(D), per_sample(6, D), rows_spec(1)],
            [((count, D), F32, rows_spec(D)), ((samples, 2, D), F32, per_sample(2, D))],
            front_back_finish, span, "front_back", prior,
        )

    def down_part_of(chains, after, span, prior, slow=()):
        own = slot(acts, chains, after, slow)
        return turned_product(
            own, scal, order, [downw], (middle, cg, mods, line(down_bias), index_col),
            [rows_spec(D), rows_spec(D), per_sample(6, D), fixed(1, D), rows_spec(1)],
            [((count, D), BF, rows_spec(D)), ((samples, 1, D), F32, per_sample(1, D))],
            down_finish, span, "down", prior,
        )

    output, down_grads = down_part_of([], (done,), half_a, None, joints)
    output, down_grads = down_part_of(joints, (down_grads,), half_b, [output, down_grads])
    tgrad, front_grads = front_part(joined_a, joints + sums, (output,), half_a, None)
    tgrad, front_grads = front_part(joined_b, joints + sums, (front_grads,), half_b, [tgrad, front_grads])

    end_grads = jnp.concatenate([front_grads, down_grads], axis=1).astype(BF).reshape(samples, 3 * D)
    end_chain = Chain(gather_steps(end_grads, everyone))
    if wires.cube:
        for _ in range(2):
            (mid_all,) = slot((mid_all,), [joint_sum, end_chain])
        up_grad, down_grad, joint_grad = up_sum.finish(), down_sum.finish(), joint_sum.finish()
    else:
        up_grad = Chain(wires.spread(up_part)).finish()
        down_grad = Chain(wires.spread(down_part)).finish()
        joint_grad = wires.scatter(plain_outer([h1, attended], jnp.concatenate([joined_a, joined_b]), scal, "joint_outer"))
        joint_grad = Chain(wires.spread(joint_grad)).finish()
    loose = loose.reshape(-1)
    end_all = end_chain.finish()
    mod_all = jnp.concatenate([end_all[:, : 2 * D], mid_all, end_all[:, 2 * D :]], axis=1)
    silu_all = jax.nn.silu(cond_chain.finish().astype(F32)).astype(BF)
    modulate_grad = dot_lt(silu_all, mod_all)
    modulate_total = jnp.sum(mod_all.astype(F32), axis=0)

    edges = np.cumsum([0] + sizes)
    heads_total, merge_total, up_total, down_total, table_total = [
        loose[a:b] for a, b in zip(edges[:-1], edges[1:])
    ]
    return (
        output,
        tgrad,
        joint_grad[:, : 3 * D].astype(F32),
        joint_grad[:, 3 * D :].astype(F32),
        up_grad.astype(F32),
        down_grad.astype(F32),
        modulate_grad,
        heads_total,
        merge_total,
        up_total,
        down_total,
        modulate_total,
        table_total.reshape(HEADS, SPAN * SPAN),
    )


def solution(mesh):
    in_specs = (
        P(("dp", "seq"), None),
        P("dp", None),
        P(("dp", "seq")),
        P(("dp", "seq"), None),
        P("seq", None),
        P(),
        P("seq", None),
        P(),
        P("seq", None),
        P(),
        P("seq", None),
        P(),
        P("seq", None),
        P(),
        P(),
        P(("dp", "seq"), None),
    )
    out_specs = (
        P(("dp", "seq"), None),
        P(("dp", "seq"), None),
        P("seq", None),
        P("seq", None),
        P("seq", None),
        P("seq", None),
        P("seq", None),
        P(),
        P(),
        P(),
        P(),
        P(),
        P(),
    )
    return jax.shard_map(
        functools.partial(local, mesh), mesh=mesh, in_specs=in_specs, out_specs=out_specs, check_vma=False
    )
```

```python
import functools
import math

import jax
import jax.numpy as jnp
import numpy as np
from jax import lax
from jax.experimental import pallas as pl
from jax.experimental.pallas import tpu as pltpu
from jax.sharding import PartitionSpec as P

D = 1152
HEADS = 16
HEAD = 72
FF = 4608
SIDE = 16
GRID = 256
SPAN = 2 * SIDE - 1
WIDE = 4608
TILE = 768
ROWS8 = 144
QUARTERS = 4
LIFT = math.log2(math.e)
SCALE = 1.0 / math.sqrt(HEAD)
EPS = 1e-06
ORDER = (0, 4, 2, 6, 1, 5, 3, 7)
BF = jnp.bfloat16
F32 = jnp.float32
VMEM_LIMIT = 60 * 1024 * 1024


def dot(a, b):
    return jnp.dot(a, b, preferred_element_type=F32)


def dot_rt(a, b):
    return lax.dot_general(a, b, (((1,), (1,)), ((), ())), preferred_element_type=F32)


def dot_lt(a, b):
    return lax.dot_general(a, b, (((0,), (0,)), ((), ())), preferred_element_type=F32)


def params():
    return pltpu.CompilerParams(
        vmem_limit_bytes=VMEM_LIMIT, dimension_semantics=("arbitrary",)
    )


def cost(flops, bytes_accessed, transcendentals=0):
    return pl.CostEstimate(
        flops=int(flops), bytes_accessed=int(bytes_accessed), transcendentals=int(transcendentals)
    )


def rows_spec(width):
    return lambda first: pl.BlockSpec((GRID, width), lambda s, *_: (s + first, 0))


def own_rows(width):
    return lambda first: pl.BlockSpec((GRID, width), lambda s, *_: (s, 0))


def per_sample(*tail):
    return lambda first: pl.BlockSpec((1,) + tail, lambda s, *_: (s + first,) + (0,) * len(tail))


def four_heads(rows, columns=GRID):
    return lambda first: pl.BlockSpec((4, rows, columns), lambda s, *_: (s, 0, 0))


def fixed(*shape, at=None):
    where = (0,) * len(shape) if at is None else at
    return lambda first: pl.BlockSpec(shape, lambda s, *_: where)


def anywhere(first):
    return pl.BlockSpec(memory_space=pl.ANY)


def call(kernel, scal, inputs, in_specs, outs, scratch, span, name, price, prior=None, steps=None):
    first, samples = span
    kept = [] if prior is None else [(i, v) for i, v in enumerate(prior) if v is not None]
    count = len(inputs)

    def body(scal_ref, *refs):
        kernel(span, scal_ref, *refs[:count], *refs[count + len(kept) :])

    return pl.pallas_call(
        body,
        grid_spec=pltpu.PrefetchScalarGridSpec(
            num_scalar_prefetch=1,
            grid=(samples if steps is None else steps,),
            in_specs=[spec(first) for spec in in_specs] + [anywhere(first)] * len(kept),
            out_specs=[spec(first) for _, _, spec in outs],
            scratch_shapes=scratch,
        ),
        out_shape=[jax.ShapeDtypeStruct(shape, kind) for shape, kind, _ in outs],
        input_output_aliases={1 + count + n: i for n, (i, _) in enumerate(kept)},
        compiler_params=params(),
        cost_estimate=price,
        name=name,
    )(scal, *inputs, *[v for _, v in kept])


def normal(values):
    center = values - jnp.mean(values, axis=-1, keepdims=True)
    inverse = lax.rsqrt(jnp.mean(center * center, axis=-1, keepdims=True) + EPS)
    return center * inverse, inverse


def norm_back(unit, inverse, grad):
    return (
        grad
        - jnp.mean(grad, axis=-1, keepdims=True)
        - unit * jnp.mean(grad * unit, axis=-1, keepdims=True)
    ) * inverse


def accumulate(ref, value, step):
    @pl.when(step == 0)
    def _():
        ref[...] = value

    @pl.when(step > 0)
    def _():
        ref[...] = ref[...] + value


def column_sum(values):
    return jnp.sum(values.astype(F32), axis=0, keepdims=True)


def place_kernel(span, scal, tokens, cotangent, index, xg, cg, mask):
    length = scal[2 + span[0] + pl.program_id(0)]
    spots = lax.broadcasted_iota(jnp.int32, (GRID, GRID), 0)
    slots = lax.broadcasted_iota(jnp.int32, (GRID, GRID), 1)
    hit = spots == index[0]
    xg[...] = dot(hit.astype(F32).astype(BF), tokens[...]).astype(BF)
    alive = jnp.logical_and(hit, slots < length).astype(F32).astype(BF)
    cg[...] = dot(alive, cotangent[...]).astype(BF)
    row = dot_rt(jnp.ones((8, GRID), BF), alive)[0:1]
    mask[0] = jnp.where(row > 0.5, 0.0, -1e30)


def bias_kernel(span, scal, strips, out):
    strip = strips[0]
    for row in range(SIDE):
        start = (SIDE - 1 - row) * SIDE
        out[0, row * SIDE : (row + 1) * SIDE, :] = strip[:, start : start + GRID] * LIFT


def strips_kernel(span, scal, first, second, out):
    for head in range(4):
        total = jnp.zeros((SIDE, 2 * GRID), F32)
        for row in range(SIDE):
            rows = slice(row * SIDE, (row + 1) * SIDE)
            pair = first[head, rows, :] + second[head, rows, :]
            wide = jnp.concatenate([pair, jnp.zeros((SIDE, GRID), F32)], axis=1)
            total = total + pltpu.roll(wide, (SIDE - 1 - row) * SIDE, axis=1)
        out[head] = total


def window(h):
    start = jnp.minimum((h * HEAD) // 128 * 128, D - 256)
    lanes = lax.broadcasted_iota(jnp.int32, (1, 256), 1) + start
    inside = jnp.logical_and(lanes >= h * HEAD, lanes < (h + 1) * HEAD)
    return pl.multiple_of(start, 128), inside.astype(F32).astype(BF)


def piece_copies(pieces, gap_dp, scal, target, sems):
    copies = []
    for i, gap in enumerate(ORDER):
        rows = pl.ds(pl.multiple_of((scal[0] ^ gap) * ROWS8, ROWS8), ROWS8)
        source = pieces[2 * (gap_dp // 2) + i // 4].at[i % 4]
        copies.append(pltpu.make_async_copy(source, target.at[rows, :], sems.at[i]))
    return copies


def qkv_kernel(span, scal, xg, mods, full_bias, weight, h1, packed):
    unit, _ = normal(xg[...].astype(F32))
    hidden = (unit * (1.0 + mods[0, 1:2]) + mods[0, 0:1]).astype(BF)
    h1[...] = hidden
    for j in range(3):
        cols = slice(j * D, (j + 1) * D)
        packed[:, cols] = (dot(hidden, weight[j]) + full_bias[:, cols]).astype(BF)


def attend_kernel(span, scal, packed, mask, table, attended, lse, mixed):
    mixed[...] = jnp.zeros_like(mixed)
    lse[...] = jnp.zeros_like(lse)
    lane = lax.broadcasted_iota(jnp.int32, (GRID, 128), 1)

    def head(h, _):
        start, inside = window(h)
        query = packed[:, pl.ds(start, 256)] * inside
        key = packed[:, pl.ds(pl.multiple_of(D + start, 128), 256)]
        value = packed[:, pl.ds(pl.multiple_of(2 * D + start, 128), 256)] * inside
        scores = dot_rt(query, key) * (SCALE * LIFT) + table[h] + mask[0]
        peak = jnp.max(scores, axis=1, keepdims=True)
        expo = jnp.exp2(scores - peak)
        mass = jnp.sum(expo, axis=1, keepdims=True)
        probs = (expo * (1.0 / mass)).astype(BF)
        cols = pl.ds(start, 256)
        mixed[:, cols] = mixed[:, cols] + dot(probs, value)
        lse[...] = jnp.where(lane == h, peak + jnp.log2(mass), lse[...])
        return 0

    lax.fori_loop(0, HEADS, head, 0, unroll=HEADS)
    attended[...] = mixed[...].astype(BF)


def merge_kernel(span, scal, attended, xg, cg, mods, merge_bias, weight, branch, middle, h2, gm, gm_sum):
    low = (mods[0, 5:6] * cg[...].astype(F32)).astype(BF)
    gm[...] = low
    accumulate(gm_sum, column_sum(low), pl.program_id(0))
    merged = dot(attended[...], weight[0]) + merge_bias[...]
    branch[...] = merged.astype(BF)
    mid = xg[...].astype(F32) + mods[0, 2:3] * merged
    middle[...] = mid
    unit, _ = normal(mid)
    h2[...] = (unit * (1.0 + mods[0, 4:5]) + mods[0, 3:4]).astype(BF)


def up_kernel(samples, gaps, scal, quarters, h2, bias, *refs):
    step = pl.program_id(0)
    if gaps is None:
        weight, act, slope = refs
        matrix = lambda: weight[0]
    else:
        pieces = refs[:4]
        act, slope, spread, target, sems, out_sems = refs[4:]
        steps = len(gaps)
        matrix = lambda: target[step]
        fetch = [piece_copies(pieces, gap, scal, target.at[n], sems.at[n]) for n, gap in enumerate(gaps)]
        store = [pltpu.make_async_copy(target.at[n], spread.at[n], out_sems.at[n]) for n in range(steps)]
        for n in range(steps):
            @pl.when(step == 0)
            def _():
                for copy in fetch[n]:
                    copy.start()
        for n in range(steps):
            @pl.when(step == n)
            def _():
                for copy in fetch[n]:
                    copy.wait()
                store[n].start()

    root = math.sqrt(2.0 / math.pi)
    for s in range(samples):
        rows = slice(s * GRID, (s + 1) * GRID)
        u = dot(h2[rows, :], matrix()) + bias[...]
        square = u * u
        t = jnp.tanh(u * ((root * 0.044715) * square + root))
        half = 0.5 * t + 0.5
        act[rows, :] = (u * half).astype(BF)
        bell = half * (1.0 - half)
        slope[rows, :] = (half + bell * (u * ((6 * root * 0.044715) * square + 2 * root))).astype(BF)
    if gaps is not None:
        for n in range(steps):
            @pl.when(step == steps - 1)
            def _():
                store[n].wait()


def up_quarters(h2, bias, weight, scal, quarters, gaps):
    count, steps = h2.shape[0], quarters.shape[0]
    column = pl.BlockSpec((None, count, D), lambda k, *_: (k, 0, 0))
    out = [jax.ShapeDtypeStruct((steps, count, D), BF)] * 2
    if gaps is None:
        weight = [weight]
        weight_specs, out_specs, scratch = [pl.BlockSpec((1, D, D), lambda k, scal, q: (q[k], 0, 0))], [column] * 2, []
    else:
        weight_specs, out_specs = [anywhere(0)] * 4, [column] * 2 + [anywhere(0)]
        out = out + [jax.ShapeDtypeStruct((steps, D, D), BF)]
        scratch = [pltpu.VMEM((steps, D, D), BF), pltpu.SemaphoreType.DMA((steps, 8)), pltpu.SemaphoreType.DMA((steps,))]
    return pl.pallas_call(
        functools.partial(up_kernel, count // GRID, gaps),
        grid_spec=pltpu.PrefetchScalarGridSpec(
            num_scalar_prefetch=2,
            grid=(steps,),
            in_specs=[pl.BlockSpec((count, D), lambda k, *_: (0, 0)), pl.BlockSpec((1, D), lambda k, scal, q: (0, q[k]))]
            + weight_specs,
            out_specs=out_specs,
            scratch_shapes=scratch,
        ),
        out_shape=out,
        compiler_params=params(),
        cost_estimate=cost(2 * count * D * D * steps, 2 * D * steps * (3 * count + 2 * D), count * D * steps),
        name="up",
    )(scal, quarters, h2, bias, *weight)


def act_back_kernel(samples, scal, quarters, gm, slope, weight, *refs):
    gu, gu_sum = refs[-2:]
    total = jnp.zeros((1, D), F32)
    for s in range(samples):
        rows = slice(s * GRID, (s + 1) * GRID)
        low = (dot(gm[rows, :], weight[0]) * slope[rows, :].astype(F32)).astype(BF)
        gu[0, rows, :] = low
        total = total + column_sum(low)
    gu_sum[...] = total


def act_back(gm, slope, weight, scal, quarters, prior):
    count, steps = gm.shape[0], quarters.shape[0]
    whole = pl.BlockSpec((count, D), lambda k, *_: (0, 0))
    return pl.pallas_call(
        functools.partial(act_back_kernel, count // GRID),
        grid_spec=pltpu.PrefetchScalarGridSpec(
            num_scalar_prefetch=2,
            grid=(steps,),
            in_specs=[
                whole,
                pl.BlockSpec((None, count, D), lambda k, *_: (k, 0, 0)),
                pl.BlockSpec((1, D, D), lambda k, scal, q: (q[k], 0, 0)),
            ]
            + [anywhere(0)] * (prior is not None),
            out_specs=[
                pl.BlockSpec((1, count, D), lambda k, *_: (k, 0, 0)),
                pl.BlockSpec((1, D), lambda k, scal, q: (0, q[k])),
            ],
        ),
        out_shape=[jax.ShapeDtypeStruct((steps, count, D), BF), jax.ShapeDtypeStruct((1, FF), F32)],
        input_output_aliases={} if prior is None else {5: 1},
        compiler_params=params(),
        cost_estimate=cost(2 * count * D * D * steps, 2 * D * steps * (2 * count + D)),
        name="act_back",
    )(scal, quarters, gm, slope, weight, *([] if prior is None else [prior]))


def turned_product(parts, scal, quarters, weights, late, late_specs, outs, finish, span, name, prior=None):
    first, samples = span
    count, tiles = samples * GRID, quarters.shape[0]
    kept = [] if prior is None else [(i, v) for i, v in enumerate(prior) if v is not None]
    used = len(parts) + len(weights)

    def body(scal_ref, quarters_ref, *refs):
        ins, ws = refs[: len(parts)], refs[len(parts) : used]
        late_refs = refs[used : used + len(late)]
        out_refs = refs[used + len(late) + len(kept) :]
        total, tile = None, 0
        for n, ref in enumerate(ins):
            blocks = ref.shape[0] if len(ref.shape) == 3 else ref.shape[1] // D
            for k in range(min(blocks, tiles - tile)):
                left = ref[k] if len(ref.shape) == 3 else ref[:, k * D : (k + 1) * D]
                right = ws[n][k] if len(ws) > 1 else ws[0][quarters_ref[tile]]
                part = dot_rt(left, right)
                total = part if total is None else total + part
                tile += 1
        finish(span, scal_ref, pl.program_id(0), total, late_refs, out_refs)

    def part_spec(part):
        offset = 0 if part.shape[-2] == count else first
        if part.ndim == 2:
            return pl.BlockSpec((GRID, part.shape[1]), lambda s, *_: (s + offset, 0))
        return pl.BlockSpec((part.shape[0], GRID, D), lambda s, *_: (0, s + offset, 0))

    def weight_spec(weight):
        blocks = min(weight.shape[0], tiles)
        return pl.BlockSpec((blocks, D, D), lambda s, *_: (0, 0, 0), pipeline_mode=pl.Buffered(1))

    return pl.pallas_call(
        body,
        grid_spec=pltpu.PrefetchScalarGridSpec(
            num_scalar_prefetch=2,
            grid=(samples,),
            in_specs=[part_spec(part) for part in parts]
            + [weight_spec(weight) for weight in weights]
            + [spec(first) for spec in late_specs]
            + [anywhere(first)] * len(kept),
            out_specs=[spec(first) for _, _, spec in outs],
        ),
        out_shape=[jax.ShapeDtypeStruct(shape, kind) for shape, kind, _ in outs],
        input_output_aliases={2 + used + len(late) + n: i for n, (i, _) in enumerate(kept)},
        compiler_params=params(),
        cost_estimate=cost(2 * count * D * D * tiles, 2 * D * tiles * (count + D) + 10 * count * D),
        name=name,
    )(scal, quarters, *parts, *weights, *late, *[v for _, v in kept])


def mid_back_finish(span, scal, sample, grad, late, outs):
    middle, branch, cg, mods = late
    gmid, gbr, gbr_sum, grads = outs
    unit, inverse = normal(middle[...])
    whole = cg[...].astype(F32) + norm_back(unit, inverse, grad * (1.0 + mods[0, 4:5]))
    gmid[...] = whole
    low = (mods[0, 2:3] * whole).astype(BF)
    gbr[...] = low
    accumulate(gbr_sum, column_sum(low), sample)
    grads[0, 0:1] = column_sum(whole * branch[...].astype(F32))
    grads[0, 1:2] = column_sum(grad)
    grads[0, 2:3] = column_sum(grad * unit)


def front_back_finish(span, scal, sample, grad, late, outs):
    xg, gmid, mods, column = late
    tgrad, grads = outs
    unit, inverse = normal(xg[...].astype(F32))
    grads[0, 0:1] = column_sum(grad)
    grads[0, 1:2] = column_sum(grad * unit)
    whole = gmid[...] + norm_back(unit, inverse, grad * (1.0 + mods[0, 1:2]))
    pick = (lax.broadcasted_iota(jnp.int32, (GRID, GRID), 1) == column[...]).astype(F32).astype(BF)
    high = whole.astype(BF)
    rest = (whole - high.astype(F32)).astype(BF)
    tgrad[...] = dot(pick, high) + dot(pick, rest)


def down_finish(span, scal, sample, product, late, outs):
    middle, cg, mods, bias, column = late
    out, grads = outs
    mlp = product + bias[...]
    grads[0] = column_sum(cg[...].astype(F32) * mlp)
    final = (middle[...] + mods[0, 5:6] * mlp).astype(BF)
    length = scal[2 + span[0] + sample]
    spots = lax.broadcasted_iota(jnp.int32, (GRID, GRID), 1)
    slots = lax.broadcasted_iota(jnp.int32, (GRID, GRID), 0)
    pick = jnp.logical_and(spots == column[...], slots < length).astype(F32).astype(BF)
    out[...] = dot(pick, final).astype(BF)


def attend_back_kernel(span, scal, gbr, packed, lse, mask, table, weight, joined, joined_sum, placed, gatt, gq, gk, gv):
    gatt[...] = dot_rt(gbr[...], weight[0]).astype(BF)
    for ref in (gq, gk, gv):
        ref[...] = jnp.zeros_like(ref)

    @pl.when(pl.program_id(0) == 0)
    def _():
        placed[...] = jnp.zeros_like(placed)
        joined_sum[...] = jnp.zeros_like(joined_sum)

    lane = lax.broadcasted_iota(jnp.int32, (GRID, 128), 1)

    def head(h, _):
        start, inside = window(h)
        cols = pl.ds(start, 256)
        query = packed[:, cols] * inside
        key = packed[:, pl.ds(pl.multiple_of(D + start, 128), 256)] * inside
        value = packed[:, pl.ds(pl.multiple_of(2 * D + start, 128), 256)]
        grad = gatt[:, cols] * inside
        scores = dot_rt(query, key) * (SCALE * LIFT) + table[h] + mask[0]
        own = jnp.sum(jnp.where(lane == h, lse[...], 0.0), axis=1, keepdims=True)
        probs = jnp.exp2(scores - own)
        gprobs = dot_rt(grad, value)
        weighted = probs * gprobs
        inner = jnp.sum(weighted, axis=1, keepdims=True)
        gscores = (weighted - probs * inner).astype(BF)
        placed[h] = placed[h] + gscores.astype(F32)
        gq[:, cols] = gq[:, cols] + dot(gscores, key)
        gk[:, cols] = gk[:, cols] + dot_lt(gscores, query)
        gv[:, cols] = gv[:, cols] + dot_lt(probs.astype(BF), grad)
        return 0

    lax.fori_loop(0, HEADS, head, 0, unroll=HEADS)
    for j, (ref, factor) in enumerate(((gq, SCALE), (gk, SCALE), (gv, 1.0))):
        cols = slice(j * D, (j + 1) * D)
        low = (ref[...] * factor).astype(BF)
        joined[:, cols] = low
        joined_sum[:, cols] = joined_sum[:, cols] + column_sum(low)
    joined[:, 3 * D :] = gbr[...]


def column_block(array, rows, width, at, row=0):
    if array.ndim == 2:
        return pl.BlockSpec((rows, width), lambda *a: (row, at(*a)))
    return pl.BlockSpec((None, rows, width), lambda *a: (at(*a), row, 0))


def plain_outer_kernel(kinds, scal, *refs):
    lefts, (right, out) = refs[:kinds], refs[kinds:]
    for kind, left in enumerate(lefts):
        def product():
            out[0] = dot_lt(left[...], right[...]).astype(BF)

        if kinds == 1:
            product()
        else:
            pl.when((pl.program_id(0) == QUARTERS - 1) == (kind == 1))(product)


def plain_outer(lefts, right, scal, name):
    count = right.shape[-2]
    return pl.pallas_call(
        functools.partial(plain_outer_kernel, len(lefts)),
        grid_spec=pltpu.PrefetchScalarGridSpec(
            num_scalar_prefetch=1,
            grid=(QUARTERS,),
            in_specs=[pl.BlockSpec((count, D), lambda q, *_: (0, 0))] * len(lefts)
            + [column_block(right, count, D, lambda q, *_: q)],
            out_specs=pl.BlockSpec((1, D, D), lambda q, *_: (q, 0, 0)),
        ),
        out_shape=jax.ShapeDtypeStruct((QUARTERS, D, D), BF),
        compiler_params=params(),
        cost_estimate=cost(2 * count * D * WIDE, 2 * count * (D + WIDE) + 2 * D * WIDE),
        name=name,
    )(scal, *lefts, right)


def outer_kernel(kinds, sources, tile_width, roles, parts, order, scal, blocks, *refs):
    lefts, rights = refs[: sources * kinds], refs[sources * kinds : sources * (kinds + 1)]
    outs, tile = refs[sources * (kinds + 1) : -1], refs[-1]
    step = pl.program_id(0)

    def product(kind, cols):
        total = dot_lt(lefts[sources * kind][...], rights[0][:, cols])
        for n in range(1, sources):
            total = total + dot_lt(lefts[sources * kind + n][...], rights[n][:, cols])
        tile[:, cols] = total.astype(BF)

    if kinds == 1:
        product(0, slice(0, tile_width))
    else:
        half = tile_width // 2
        for part in range(2):
            from_first = blocks[step] * 2 + part < 3 * D // half
            cols = slice(part * half, (part + 1) * half)
            pl.when(from_first)(functools.partial(product, 0, cols))
            pl.when(jnp.logical_not(from_first))(functools.partial(product, 1, cols))
    for r in range(roles):
        @pl.when(step == r)
        def _():
            for i in range(8):
                start = i * ROWS8 if order is None else pl.multiple_of((scal[0] ^ order[i]) * ROWS8, ROWS8)
                rows = pl.ds(start, ROWS8)
                outs[parts * r + i * parts // 8][i % (8 // parts)] = tile[rows, :]


def outer_tiles(lefts, rights, scal, blocks, width, parts, order, name):
    count, kinds, roles, sources = rights[0].shape[-2], len(lefts), blocks.shape[0], len(rights)
    some = pl.BlockSpec((8 // parts, ROWS8, width), lambda r, *_: (0, 0, 0))
    each = sources // len(lefts[0])
    left_specs = [pl.BlockSpec((count, D), lambda r, *_, n=n: (n, 0)) for n in range(each)] * (len(lefts[0]) * kinds)
    return pl.pallas_call(
        functools.partial(outer_kernel, kinds, sources, width, roles, parts, order),
        grid_spec=pltpu.PrefetchScalarGridSpec(
            num_scalar_prefetch=2,
            grid=(roles,),
            in_specs=left_specs + [column_block(rights[0], count, width, lambda r, scal, blocks: blocks[r])] * sources,
            out_specs=[some] * (parts * roles),
            scratch_shapes=[pltpu.VMEM((D, width), BF)],
        ),
        out_shape=[jax.ShapeDtypeStruct((8 // parts, ROWS8, width), BF)] * (parts * roles),
        compiler_params=params(),
        cost_estimate=cost(
            2 * sources * count * D * width * roles, 2 * sources * count * (D * kinds + width * roles)
        ),
        name=name,
    )(scal, blocks, *[v for left in lefts for v in left for _ in range(each)], *rights)


ON_THE_WAY = []


def flip(value, axis, size, bit):
    ON_THE_WAY.append(lax.ppermute(value, axis, [(i, i ^ bit) for i in range(size)]))
    return ON_THE_WAY[-1]


def bits_of(size):
    return [1 << k for k in range(size.bit_length() - 1)]


def gather_steps(value, axes):
    for axis, size in axes:
        own = lax.axis_index(axis)
        for bit in bits_of(size):
            (value,) = yield [value]
            other = flip(value, axis, size, bit)
            low = (own & bit) == 0
            value = jnp.concatenate([jnp.where(low, value, other), jnp.where(low, other, value)], axis=0)
    return value


def scatter_steps(value, axis, size):
    own = lax.axis_index(axis)
    for bit in bits_of(size):
        value = value.reshape((value.shape[0] // 2, 2) + value.shape[1:])
        low = (own & bit) == 0
        keep = jnp.where(low, value[:, 0], value[:, 1])
        send = jnp.where(low, value[:, 1], value[:, 0]).astype(BF)
        (send,) = yield [send]
        value = keep + flip(send, axis, size, bit).astype(F32)
    return value


class Chain:
    def __init__(self, steps):
        self.steps, self.result = steps, None
        self.ready = next(steps)

    def advance(self, operands):
        if self.result is None:
            try:
                self.ready = self.steps.send(operands)
            except StopIteration as end:
                self.ready, self.result = [], end.value

    def finish(self):
        while self.result is None:
            self.advance(self.ready)
        return self.result


def slot(inputs, chains=(), after=(), slow=()):
    chains, slow = list(chains), list(slow)
    inputs, operands, _ = lax.optimization_barrier(
        (tuple(inputs), [c.ready for c in chains + slow], (*after, *ON_THE_WAY))
    )
    ON_THE_WAY.clear()
    for chain, ready in zip(slow, operands[len(chains) :]):
        chain.advance(ready)
    ON_THE_WAY.clear()
    for chain, ready in zip(chains, operands):
        chain.advance(ready)
    return inputs


class Wires:
    def __init__(self, mesh):
        self.dp, self.seq = mesh.shape["dp"], mesh.shape["seq"]
        self.cube = self.dp == 4 and self.seq == 8
        self.place, self.me = lax.axis_index("dp"), lax.axis_index("seq")

    def far(self, value, bit):
        return flip(value, "seq", self.seq, bit)

    def across(self, value):
        return flip(value, "dp", self.dp, 2)

    def sibling(self, value):
        return flip(value, "dp", self.dp, 1)

    def quarter(self, shards):
        if len(shards) == 1:
            return lax.dynamic_slice_in_dim(shards[0], self.place * D, D, 1)[None]
        heads = lax.dynamic_slice_in_dim(shards[0], jnp.minimum(self.place, 2) * D, D, 1)
        return jnp.where(self.place == 3, shards[1], heads)[None]

    def gather(self, quarter):
        return lax.all_gather(quarter, ("dp", "seq"), axis=0, tiled=True).reshape(QUARTERS, D, D)

    def gather_steps(self, quarter):
        (one,) = yield [quarter]
        two = jnp.concatenate([one, self.far(one, 4)], axis=0)
        (two,) = yield [two]
        four = jnp.concatenate([two, self.far(two, 2)], axis=0)
        (four,) = yield [four]
        rest, cross = self.far(four, 1), self.across(four)
        rest, cross, four = yield [rest, cross, four]
        cross_rest, near = self.across(rest), [self.sibling(four), self.sibling(rest), self.sibling(cross)]
        cross_rest, *near = yield [cross_rest, *near]
        return [four, rest, cross, cross_rest], [*near, self.sibling(cross_rest)]

    def scatter(self, whole):
        rows = D // self.seq
        parts = whole.reshape(QUARTERS * self.seq, rows, D)
        return lax.psum_scatter(parts, ("dp", "seq"), scatter_dimension=0, tiled=True)

    def spread(self, part):
        parts = yield from gather_steps(part, (("dp", self.dp),))
        return jnp.concatenate([parts[q] for q in range(QUARTERS)], axis=1)

    def reduce_quarter(self, cross, quarter, groups):
        got = {}
        for group in groups:
            sent = yield [cross[part] for part in group]
            for part, value in zip(group, sent):
                got[part] = self.across(value)
        upper = [(quarter[part].astype(F32) + got[part].astype(F32)).astype(BF) for part in (2, 3)]
        left = [part for part in (0, 1) if part not in got]
        send, *sent = yield [jnp.concatenate(upper, axis=0)] + [cross[part] for part in left]
        near = self.far(send, 1)
        for part, value in zip(left, sent):
            got[part] = self.across(value)
        (send,) = yield [(total_of([quarter[1], got[1]], 0, 2) + near[2:4].astype(F32)).astype(BF)]
        parts = [quarter[0], got[0], near, self.far(send, 2)]
        (send,) = yield [total_of(parts, 1, 2).astype(BF)]
        parts.append(self.far(send, 4))
        return (yield from self.spread(total_of(parts, 0, 1).astype(BF)))

    def reduce(self, give):
        core, x = self.place % 2, self.place // 2
        give = yield [give[1], give[0], give[2]]
        got = [self.sibling(value) for value in give]
        keep = yield []
        cross, quarter, common = [keep[1], got[0]], [keep[0], got[1]], [keep[2], got[2]]
        (high,) = yield [total_of(cross, 4, 8).astype(BF)]
        high = self.across(high)
        low, send = yield [total_of(cross, 0, 4).astype(BF), total_of(common, 4, 8).astype(BF)]
        low = self.across(low)
        common.append(self.far(send, 1))
        send, other = yield [
            (total_of(quarter, 4, 8) + high.astype(F32)).astype(BF), total_of(common, 2, 4).astype(BF)
        ]
        quarter += [low, self.far(send, 1)]
        common.append(self.far(other, 2))
        send, other = yield [total_of(quarter, 2, 4).astype(BF), total_of(common, 1, 2).astype(BF)]
        quarter.append(self.far(send, 2))
        common.append(self.far(other, 4))
        send, end = yield [total_of(quarter, 1, 2).astype(BF), total_of(common, 0, 1).astype(BF)]
        quarter.append(self.far(send, 4))
        (ends,) = yield [jnp.concatenate([total_of(quarter, 0, 1).astype(BF), end], axis=0)]
        other = self.across(ends)
        shared = (ends[1].astype(F32) + other[1].astype(F32)).astype(BF)
        (mine,) = yield [jnp.stack([ends[0], other[0], shared])]
        theirs = self.sibling(mine)
        columns = []
        first, left = core == 0, x == 0
        for quarter_index in range(4):
            of_core, of_x = divmod(quarter_index, 2)
            near, far = (mine, theirs) if of_core == 0 else (theirs, mine)
            same = jnp.where(first, near[:2], far[:2])
            columns.append(jnp.where(left == (of_x == 0), same[0], same[1]))
        columns.append(jnp.where(first, mine[2], theirs[2]))
        columns.append(jnp.where(first, theirs[2], mine[2]))
        return jnp.concatenate(columns, axis=1)

    def roles(self):
        core, x = self.place % 2, self.place // 2
        return jnp.stack([2 * core + x, 2 * core + 1 - x, 4 + core]).astype(jnp.int32)


def total_of(parts, start, stop):
    summed = 0.0
    for part in parts:
        summed = summed + part[start:stop].astype(F32)
    return summed


def unit_gaps():
    spots = np.arange(SIDE)
    reach = np.arange(SPAN)
    return (spots[None, :, None] - spots[None, None, :] + (SIDE - 1) == reach[:, None, None]).astype(np.float32)


def local(
    mesh,
    tokens,
    condition,
    lengths,
    kept_index,
    heads_weight,
    heads_bias,
    merge_weight,
    merge_bias,
    up_weight,
    up_bias,
    down_weight,
    down_bias,
    modulate_weight,
    modulate_bias,
    relative_table,
    cotangent,
):
    ON_THE_WAY.clear()
    wires = Wires(mesh)
    dp, seq = wires.dp, wires.seq
    samples, count = kept_index.shape[0], tokens.shape[0]
    shard_rows = heads_weight.shape[0]
    everything, half_a, half_b = (0, samples), (0, samples // 2), (samples // 2, samples - samples // 2)
    everyone = (("seq", seq), ("dp", dp))
    line = lambda v: v.astype(F32).reshape(1, -1)
    scal = jnp.concatenate([jnp.stack([wires.me, wires.place]).astype(jnp.int32), lengths])
    in_order = jnp.arange(QUARTERS, dtype=jnp.int32)

    own_cols = lax.dynamic_slice_in_dim(condition, wires.me * shard_rows, shard_rows, 1)
    own_silu = jax.nn.silu(own_cols.astype(F32)).astype(BF)
    partial = dot(own_silu, modulate_weight).reshape(seq, samples, 6 * D)
    mod_chain = Chain(scatter_steps(partial, "seq", seq))
    cond_chain = Chain(gather_steps(own_cols, (("dp", dp),)))
    joint = wires.gather(wires.quarter([heads_weight, merge_weight]))
    up_chain = [Chain(wires.gather_steps(wires.quarter([up_weight])))] if wires.cube else []
    upw = None if wires.cube else wires.gather(wires.quarter([up_weight]))

    index_row = kept_index.reshape(samples, 1, GRID)
    index_col = kept_index.reshape(count, 1)
    inputs = slot((tokens, cotangent, index_row), [cond_chain], slow=up_chain)
    xg, cg, mask = call(
        place_kernel, scal, inputs, [rows_spec(D), rows_spec(D), per_sample(1, GRID)],
        [((count, D), BF, rows_spec(D)), ((count, D), BF, rows_spec(D)), ((samples, 1, GRID), F32, per_sample(1, GRID))],
        [], everything, "place", cost(4 * count * GRID * D, 8 * count * D),
    )
    (later, _) = lax.optimization_barrier((down_weight, mask))
    downw = wires.gather(wires.quarter([later]))

    gaps = unit_gaps()
    turned = relative_table.reshape(HEADS, SPAN, SPAN)[:, ::-1]
    strips = jnp.einsum("hkj,jpq->hpkq", turned, jnp.asarray(gaps, BF), preferred_element_type=F32)
    strips = jnp.pad(strips.reshape(HEADS, SIDE, SPAN * SIDE), ((0, 0), (0, 0), (0, SIDE)))
    inputs = slot((strips,), up_chain + [mod_chain, cond_chain], (mask,))
    (table,) = call(
        bias_kernel, scal, inputs, [per_sample(SIDE, 2 * GRID)], [((HEADS, GRID, GRID), F32, per_sample(GRID, GRID))],
        [], (0, HEADS), "bias", cost(0, 5 << 20),
    )
    (table,) = slot((table,), [mod_chain], slow=up_chain)
    (table,) = slot((table,), [mod_chain])
    modulation = mod_chain.finish().reshape(samples, 6 * D) + modulate_bias.astype(F32)
    mods = modulation.reshape(samples, 6, D)

    full_bias = jnp.concatenate([heads_bias[:D], jnp.zeros((D,), BF), heads_bias[D:]])
    inputs = slot((xg, mods, line(full_bias), joint), slow=up_chain, after=(table,))
    h1, packed = call(
        qkv_kernel, scal, inputs,
        [rows_spec(D), per_sample(6, D), fixed(1, 3 * D), fixed(3, D, D)],
        [((count, D), BF, rows_spec(D)), ((count, 3 * D), BF, rows_spec(3 * D))],
        [], everything, "qkv", cost(2 * count * D * 3 * D, 22 << 20),
    )
    inputs = slot((packed, mask, table))
    attended, lse = call(
        attend_kernel, scal, inputs, [rows_spec(3 * D), per_sample(1, GRID), fixed(HEADS, GRID, GRID)],
        [((count, D), BF, rows_spec(D)), ((count, 128), F32, rows_spec(128))],
        [pltpu.VMEM((GRID, D), F32)], everything, "attend", cost(4 * count * GRID * 256 * HEADS, 15 << 20, count * GRID * HEADS),
    )
    inputs = slot((attended, xg, cg, mods, line(merge_bias), joint), slow=up_chain)
    branch, middle, h2, gm, gm_sum = call(
        merge_kernel, scal, inputs,
        [rows_spec(D), rows_spec(D), rows_spec(D), per_sample(6, D), fixed(1, D), fixed(1, D, D, at=(3, 0, 0))],
        [((count, D), BF, rows_spec(D)), ((count, D), F32, rows_spec(D)), ((count, D), BF, rows_spec(D)),
         ((count, D), BF, rows_spec(D)), ((1, D), F32, fixed(1, D))],
        [], everything, "merge", cost(2 * count * D * D, 20 << 20),
    )

    def pair(values):
        return [[v, wires.sibling(v)] for v in values]

    up_line, sums = line(up_bias), []
    if wires.cube:
        place = wires.place.astype(jnp.int32)
        own_quarters, their_quarters = jnp.stack([place, place ^ 2]), jnp.stack([place ^ 1, place ^ 3])
        order, cross_first = jnp.concatenate([own_quarters, their_quarters]), jnp.array([1, 0], jnp.int32)
        own_pieces, their_pieces = up_chain[0].finish()
        h2, *their_pieces = slot((h2, *their_pieces))
        act_theirs, slope_theirs, up_theirs = up_quarters(h2, up_line, their_pieces, scal, their_quarters, (1, 3))
        h2, *own_pieces = slot((h2, *own_pieces), after=(act_theirs,))
        arrived = wires.sibling(act_theirs)
        gm_pair, h2_pair = pair([gm, h2])
        act_own, slope_own, up_own = up_quarters(h2, up_line, own_pieces, scal, own_quarters, (0, 2))
        acts, upws = [act_own, act_theirs], [up_own, up_theirs]
        act_own, arrived = slot((act_own, arrived))
        tiles = outer_tiles([gm_pair], [act_own, arrived], scal, cross_first, D, 4, ORDER, "down_outer")
        down_sum = Chain(wires.reduce_quarter(tiles[:4], tiles[4:], ((2,), (3,))))
        gm, slope_theirs, downw = slot((gm, slope_theirs, downw), after=(tiles[0],))
        gu_theirs, gu_sum = act_back(gm, slope_theirs, downw, scal, their_quarters, None)
        gm, slope_own, downw, gu_sum = slot((gm, slope_own, downw, gu_sum), [down_sum], (gu_theirs,))
        arrived = wires.sibling(gu_theirs)
        gu_own, gu_sum = act_back(gm, slope_own, downw, scal, own_quarters, gu_sum)
        gu_parts = [gu_own, gu_theirs]
        gu_own, arrived = slot((gu_own, arrived), [down_sum])
        tiles = outer_tiles([h2_pair], [gu_own, arrived], scal, cross_first, D, 4, ORDER, "up_outer")
        up_sum = Chain(wires.reduce_quarter(tiles[:4], tiles[4:], ((2, 3),)))
        sums = [down_sum, up_sum]
        gu_parts = slot(gu_parts, [down_sum], (tiles[0],))
    else:
        order, upws = in_order, [upw]
        act, slope = up_quarters(h2, up_line, upw, scal, in_order, None)
        down_part = wires.scatter(plain_outer([gm], act, scal, "down_outer"))
        gu, gu_sum = act_back(gm, slope, downw, scal, in_order, None)
        up_part = wires.scatter(plain_outer([h2], gu, scal, "up_outer"))
        acts, gu_parts = [act], [gu]

    gmid, gbr, gbr_sum, mid_grads = turned_product(
        gu_parts, scal, order, upws, (middle, branch, cg, mods), [rows_spec(D), rows_spec(D), rows_spec(D), per_sample(6, D)],
        [((count, D), F32, rows_spec(D)), ((count, D), BF, rows_spec(D)), ((1, D), F32, fixed(1, D)), ((samples, 3, D), F32, per_sample(3, D))],
        mid_back_finish, everything, "mid_back",
    )
    mid_rows = jnp.pad(mid_grads.astype(BF), ((0, 0), (0, 1), (0, 0))).reshape(1, samples * 4, D)
    mid_all = lax.all_gather(mid_rows, ("dp", "seq"), axis=0, tiled=True).reshape(-1, 4, D)[:, :3].reshape(-1, 3 * D)

    def attend_part(chains, after, span):
        inputs = slot((gbr, packed, lse, mask, table, joint), chains, after)
        return call(
            attend_back_kernel, scal, inputs,
            [rows_spec(D), rows_spec(3 * D), rows_spec(128), per_sample(1, GRID), fixed(HEADS, GRID, GRID), fixed(1, D, D, at=(3, 0, 0))],
            [((span[1] * GRID, WIDE), BF, own_rows(WIDE)),
             ((1, 3 * D), F32, fixed(1, 3 * D)), ((HEADS, GRID, GRID), F32, fixed(HEADS, GRID, GRID))],
            [pltpu.VMEM((GRID, D), BF)] + [pltpu.VMEM((GRID, D), F32)] * 3,
            span, "attend_back", cost(count * D * D + 5 * count * GRID * 256 * HEADS, 20 << 20),
        )

    joined_a, joined_sum_a, placed_a = attend_part(sums, (), half_a)
    joined_b, joined_sum_b, placed_b = attend_part(sums, (joined_a,), half_b)
    joined_sum = joined_sum_a + joined_sum_b

    done = joined_b
    if wires.cube:
        lefts, roles = [[h1], [attended]], wires.roles()
        theirs = jnp.stack([roles[0] ^ 2, roles[1] ^ 2, roles[2] ^ 1])
        rights = slot((joined_a, joined_b), slow=sums)
        give = outer_tiles(lefts, rights, scal, theirs, TILE, 1, ORDER, "joint_give")
        joint_sum = Chain(wires.reduce(give))
        rights = slot(rights, [joint_sum], (give[0],), slow=sums[:1])
        keep = outer_tiles(lefts, rights, scal, roles, TILE, 1, ORDER, "joint_keep")
        joint_sum.ready = tuple(keep)
        joint_sum.advance(joint_sum.ready)
        done = keep[0]

    joints = [joint_sum] if wires.cube else []
    placed_a, placed_b = slot((placed_a, placed_b), sums[1:], (done,), slow=joints)
    (strip_grad,) = call(
        strips_kernel, scal, (placed_a, placed_b), [four_heads(GRID)] * 2,
        [((HEADS, SIDE, 2 * GRID), F32, four_heads(SIDE, 2 * GRID))], [], (0, HEADS // 4), "strips", cost(0, 9 << 20),
    )
    strip_grad = strip_grad[:, :, : SPAN * SIDE].reshape(HEADS, SIDE, SPAN, SIDE)
    table_grad = jnp.einsum(
        "hpkq,jpq->hkj", strip_grad, jnp.asarray(gaps), precision=lax.Precision.HIGHEST
    )[:, ::-1].reshape(-1)
    sizes = [2 * D, D, FF, D, HEADS * SPAN * SPAN]
    loose = jnp.concatenate(
        [joined_sum[0, :D], joined_sum[0, 2 * D :], gbr_sum[0], gu_sum[0], gm_sum[0], table_grad]
    )
    loose = jnp.pad(loose, (0, -loose.shape[0] % 1024)).reshape(-1, 128)
    loose = jnp.sum(lax.all_gather(loose, ("dp", "seq")), axis=0)
    done = strip_grad
    def front_part(own, chains, after, span, prior):
        (own,) = slot((own,), chains, after)
        return turned_product(
            [own], scal, in_order[:3], [joint], (xg, gmid, mods, index_col),
            [rows_spec(D), rows_spec(D), per_sample(6, D), rows_spec(1)],
            [((count, D), F32, rows_spec(D)), ((samples, 2, D), F32, per_sample(2, D))],
            front_back_finish, span, "front_back", prior,
        )

    def down_part_of(chains, after, span, prior, slow=()):
        own = slot(acts, chains, after, slow)
        return turned_product(
            own, scal, order, [downw], (middle, cg, mods, line(down_bias), index_col),
            [rows_spec(D), rows_spec(D), per_sample(6, D), fixed(1, D), rows_spec(1)],
            [((count, D), BF, rows_spec(D)), ((samples, 1, D), F32, per_sample(1, D))],
            down_finish, span, "down", prior,
        )

    output, down_grads = down_part_of([], (done,), half_a, None, joints)
    output, down_grads = down_part_of(joints, (down_grads,), half_b, [output, down_grads])
    tgrad, front_grads = front_part(joined_a, joints + sums, (output,), half_a, None)
    tgrad, front_grads = front_part(joined_b, joints + sums, (front_grads,), half_b, [tgrad, front_grads])

    end_grads = jnp.concatenate([front_grads, down_grads], axis=1).astype(BF).reshape(samples, 3 * D)
    end_chain = Chain(gather_steps(end_grads, everyone))
    if wires.cube:
        for _ in range(2):
            (mid_all,) = slot((mid_all,), [joint_sum, end_chain])
        up_grad, down_grad, joint_grad = up_sum.finish(), down_sum.finish(), joint_sum.finish()
    else:
        up_grad = Chain(wires.spread(up_part)).finish()
        down_grad = Chain(wires.spread(down_part)).finish()
        joint_grad = wires.scatter(plain_outer([h1, attended], jnp.concatenate([joined_a, joined_b]), scal, "joint_outer"))
        joint_grad = Chain(wires.spread(joint_grad)).finish()
    loose = loose.reshape(-1)
    end_all = end_chain.finish()
    mod_all = jnp.concatenate([end_all[:, : 2 * D], mid_all, end_all[:, 2 * D :]], axis=1)
    silu_all = jax.nn.silu(cond_chain.finish().astype(F32)).astype(BF)
    modulate_grad = dot_lt(silu_all, mod_all)
    modulate_total = jnp.sum(mod_all.astype(F32), axis=0)

    edges = np.cumsum([0] + sizes)
    heads_total, merge_total, up_total, down_total, table_total = [
        loose[a:b] for a, b in zip(edges[:-1], edges[1:])
    ]
    return (
        output,
        tgrad,
        joint_grad[:, : 3 * D].astype(F32),
        joint_grad[:, 3 * D :].astype(F32),
        up_grad.astype(F32),
        down_grad.astype(F32),
        modulate_grad,
        heads_total,
        merge_total,
        up_total,
        down_total,
        modulate_total,
        table_total.reshape(HEADS, SPAN * SPAN),
    )


def solution(mesh):
    in_specs = (
        P(("dp", "seq"), None),
        P("dp", None),
        P(("dp", "seq")),
        P(("dp", "seq"), None),
        P("seq", None),
        P(),
        P("seq", None),
        P(),
        P("seq", None),
        P(),
        P("seq", None),
        P(),
        P("seq", None),
        P(),
        P(),
        P(("dp", "seq"), None),
    )
    out_specs = (
        P(("dp", "seq"), None),
        P(("dp", "seq"), None),
        P("seq", None),
        P("seq", None),
        P("seq", None),
        P("seq", None),
        P("seq", None),
        P(),
        P(),
        P(),
        P(),
        P(),
        P(),
    )
    return jax.shard_map(
        functools.partial(local, mesh), mesh=mesh, in_specs=in_specs, out_specs=out_specs, check_vma=False
    )
```

```python
import functools
import math

import jax
import jax.numpy as jnp
import numpy as np
from jax import lax
from jax.experimental import pallas as pl
from jax.experimental.pallas import tpu as pltpu
from jax.sharding import PartitionSpec as P

D = 1152
HEADS = 16
HEAD = 72
FF = 4608
SIDE = 16
GRID = 256
SPAN = 2 * SIDE - 1
WIDE = 4608
TILE = 768
ROWS8 = 144
QUARTERS = 4
LIFT = math.log2(math.e)
SCALE = 1.0 / math.sqrt(HEAD)
EPS = 1e-06
ORDER = (0, 4, 2, 6, 1, 5, 3, 7)
BF = jnp.bfloat16
F32 = jnp.float32
VMEM_LIMIT = 60 * 1024 * 1024


def dot(a, b):
    return jnp.dot(a, b, preferred_element_type=F32)


def dot_rt(a, b):
    return lax.dot_general(a, b, (((1,), (1,)), ((), ())), preferred_element_type=F32)


def dot_lt(a, b):
    return lax.dot_general(a, b, (((0,), (0,)), ((), ())), preferred_element_type=F32)


def params():
    return pltpu.CompilerParams(
        vmem_limit_bytes=VMEM_LIMIT, dimension_semantics=("arbitrary",)
    )


def cost(flops, bytes_accessed, transcendentals=0):
    return pl.CostEstimate(
        flops=int(flops), bytes_accessed=int(bytes_accessed), transcendentals=int(transcendentals)
    )


def rows_spec(width):
    return lambda first: pl.BlockSpec((GRID, width), lambda s, *_: (s + first, 0))


def own_rows(width):
    return lambda first: pl.BlockSpec((GRID, width), lambda s, *_: (s, 0))


def per_sample(*tail):
    return lambda first: pl.BlockSpec((1,) + tail, lambda s, *_: (s + first,) + (0,) * len(tail))


def four_heads(rows, columns=GRID):
    return lambda first: pl.BlockSpec((4, rows, columns), lambda s, *_: (s, 0, 0))


def fixed(*shape, at=None):
    where = (0,) * len(shape) if at is None else at
    return lambda first: pl.BlockSpec(shape, lambda s, *_: where)


def anywhere(first):
    return pl.BlockSpec(memory_space=pl.ANY)


def call(kernel, scal, inputs, in_specs, outs, scratch, span, name, price, prior=None, steps=None):
    first, samples = span
    kept = [] if prior is None else [(i, v) for i, v in enumerate(prior) if v is not None]
    count = len(inputs)

    def body(scal_ref, *refs):
        kernel(span, scal_ref, *refs[:count], *refs[count + len(kept) :])

    return pl.pallas_call(
        body,
        grid_spec=pltpu.PrefetchScalarGridSpec(
            num_scalar_prefetch=1,
            grid=(samples if steps is None else steps,),
            in_specs=[spec(first) for spec in in_specs] + [anywhere(first)] * len(kept),
            out_specs=[spec(first) for _, _, spec in outs],
            scratch_shapes=scratch,
        ),
        out_shape=[jax.ShapeDtypeStruct(shape, kind) for shape, kind, _ in outs],
        input_output_aliases={1 + count + n: i for n, (i, _) in enumerate(kept)},
        compiler_params=params(),
        cost_estimate=price,
        name=name,
    )(scal, *inputs, *[v for _, v in kept])


def normal(values):
    center = values - jnp.mean(values, axis=-1, keepdims=True)
    inverse = lax.rsqrt(jnp.mean(center * center, axis=-1, keepdims=True) + EPS)
    return center * inverse, inverse


def norm_back(unit, inverse, grad):
    return (
        grad
        - jnp.mean(grad, axis=-1, keepdims=True)
        - unit * jnp.mean(grad * unit, axis=-1, keepdims=True)
    ) * inverse


def accumulate(ref, value, step):
    @pl.when(step == 0)
    def _():
        ref[...] = value

    @pl.when(step > 0)
    def _():
        ref[...] = ref[...] + value


def column_sum(values):
    return jnp.sum(values.astype(F32), axis=0, keepdims=True)


def place_kernel(span, scal, tokens, cotangent, index, xg, cg, mask):
    length = scal[2 + span[0] + pl.program_id(0)]
    spots = lax.broadcasted_iota(jnp.int32, (GRID, GRID), 0)
    slots = lax.broadcasted_iota(jnp.int32, (GRID, GRID), 1)
    hit = spots == index[0]
    xg[...] = dot(hit.astype(F32).astype(BF), tokens[...]).astype(BF)
    alive = jnp.logical_and(hit, slots < length).astype(F32).astype(BF)
    cg[...] = dot(alive, cotangent[...]).astype(BF)
    row = dot_rt(jnp.ones((8, GRID), BF), alive)[0:1]
    mask[0] = jnp.where(row > 0.5, 0.0, -1e30)


def bias_kernel(span, scal, strips, out):
    strip = strips[0]
    for row in range(SIDE):
        start = (SIDE - 1 - row) * SIDE
        out[0, row * SIDE : (row + 1) * SIDE, :] = strip[:, start : start + GRID] * LIFT


def strips_kernel(span, scal, first, second, out):
    for head in range(4):
        total = jnp.zeros((SIDE, 2 * GRID), F32)
        for row in range(SIDE):
            rows = slice(row * SIDE, (row + 1) * SIDE)
            pair = first[head, rows, :] + second[head, rows, :]
            wide = jnp.concatenate([pair, jnp.zeros((SIDE, GRID), F32)], axis=1)
            total = total + pltpu.roll(wide, (SIDE - 1 - row) * SIDE, axis=1)
        out[head] = total


def window(h):
    start = jnp.minimum((h * HEAD) // 128 * 128, D - 256)
    lanes = lax.broadcasted_iota(jnp.int32, (1, 256), 1) + start
    inside = jnp.logical_and(lanes >= h * HEAD, lanes < (h + 1) * HEAD)
    return pl.multiple_of(start, 128), inside.astype(F32).astype(BF)


def piece_copies(pieces, gap_dp, scal, target, sems):
    copies = []
    for i, gap in enumerate(ORDER):
        rows = pl.ds(pl.multiple_of((scal[0] ^ gap) * ROWS8, ROWS8), ROWS8)
        source = pieces[2 * (gap_dp // 2) + i // 4].at[i % 4]
        copies.append(pltpu.make_async_copy(source, target.at[rows, :], sems.at[i]))
    return copies


def qkv_kernel(span, scal, xg, mods, full_bias, weight, h1, packed):
    unit, _ = normal(xg[...].astype(F32))
    hidden = (unit * (1.0 + mods[0, 1:2]) + mods[0, 0:1]).astype(BF)
    h1[...] = hidden
    for j in range(3):
        cols = slice(j * D, (j + 1) * D)
        packed[:, cols] = (dot(hidden, weight[j]) + full_bias[:, cols]).astype(BF)


def attend_kernel(span, scal, packed, mask, table, attended, lse, mixed):
    mixed[...] = jnp.zeros_like(mixed)
    lse[...] = jnp.zeros_like(lse)
    lane = lax.broadcasted_iota(jnp.int32, (GRID, 128), 1)

    def head(h, _):
        start, inside = window(h)
        query = packed[:, pl.ds(start, 256)] * inside
        key = packed[:, pl.ds(pl.multiple_of(D + start, 128), 256)]
        value = packed[:, pl.ds(pl.multiple_of(2 * D + start, 128), 256)] * inside
        scores = dot_rt(query, key) * (SCALE * LIFT) + table[h] + mask[0]
        peak = jnp.max(scores, axis=1, keepdims=True)
        expo = jnp.exp2(scores - peak)
        mass = jnp.sum(expo, axis=1, keepdims=True)
        probs = (expo * (1.0 / mass)).astype(BF)
        cols = pl.ds(start, 256)
        mixed[:, cols] = mixed[:, cols] + dot(probs, value)
        lse[...] = jnp.where(lane == h, peak + jnp.log2(mass), lse[...])
        return 0

    lax.fori_loop(0, HEADS, head, 0, unroll=HEADS)
    attended[...] = mixed[...].astype(BF)


def merge_kernel(span, scal, attended, xg, cg, mods, merge_bias, weight, branch, middle, h2, gm, gm_sum):
    low = (mods[0, 5:6] * cg[...].astype(F32)).astype(BF)
    gm[...] = low
    accumulate(gm_sum, column_sum(low), pl.program_id(0))
    merged = dot(attended[...], weight[0]) + merge_bias[...]
    branch[...] = merged.astype(BF)
    mid = xg[...].astype(F32) + mods[0, 2:3] * merged
    middle[...] = mid
    unit, _ = normal(mid)
    h2[...] = (unit * (1.0 + mods[0, 4:5]) + mods[0, 3:4]).astype(BF)


def up_kernel(samples, gaps, scal, quarters, h2, bias, *refs):
    step = pl.program_id(0)
    if gaps is None:
        weight, act, slope = refs
        matrix = lambda: weight[0]
    else:
        pieces = refs[:4]
        act, slope, spread, target, sems, out_sems = refs[4:]
        steps = len(gaps)
        matrix = lambda: target[step]
        fetch = [piece_copies(pieces, gap, scal, target.at[n], sems.at[n]) for n, gap in enumerate(gaps)]
        store = [pltpu.make_async_copy(target.at[n], spread.at[n], out_sems.at[n]) for n in range(steps)]
        for n in range(steps):
            @pl.when(step == 0)
            def _():
                for copy in fetch[n]:
                    copy.start()
        for n in range(steps):
            @pl.when(step == n)
            def _():
                for copy in fetch[n]:
                    copy.wait()
                store[n].start()

    root = math.sqrt(2.0 / math.pi)
    for s in range(samples):
        rows = slice(s * GRID, (s + 1) * GRID)
        u = dot(h2[rows, :], matrix()) + bias[...]
        square = u * u
        t = jnp.tanh(u * ((root * 0.044715) * square + root))
        half = 0.5 * t + 0.5
        act[rows, :] = (u * half).astype(BF)
        bell = half * (1.0 - half)
        slope[rows, :] = (half + bell * (u * ((6 * root * 0.044715) * square + 2 * root))).astype(BF)
    if gaps is not None:
        for n in range(steps):
            @pl.when(step == steps - 1)
            def _():
                store[n].wait()


def up_quarters(h2, bias, weight, scal, quarters, gaps):
    count, steps = h2.shape[0], quarters.shape[0]
    column = pl.BlockSpec((None, count, D), lambda k, *_: (k, 0, 0))
    out = [jax.ShapeDtypeStruct((steps, count, D), BF)] * 2
    if gaps is None:
        weight = [weight]
        weight_specs, out_specs, scratch = [pl.BlockSpec((1, D, D), lambda k, scal, q: (q[k], 0, 0))], [column] * 2, []
    else:
        weight_specs, out_specs = [anywhere(0)] * 4, [column] * 2 + [anywhere(0)]
        out = out + [jax.ShapeDtypeStruct((steps, D, D), BF)]
        scratch = [pltpu.VMEM((steps, D, D), BF), pltpu.SemaphoreType.DMA((steps, 8)), pltpu.SemaphoreType.DMA((steps,))]
    return pl.pallas_call(
        functools.partial(up_kernel, count // GRID, gaps),
        grid_spec=pltpu.PrefetchScalarGridSpec(
            num_scalar_prefetch=2,
            grid=(steps,),
            in_specs=[pl.BlockSpec((count, D), lambda k, *_: (0, 0)), pl.BlockSpec((1, D), lambda k, scal, q: (0, q[k]))]
            + weight_specs,
            out_specs=out_specs,
            scratch_shapes=scratch,
        ),
        out_shape=out,
        compiler_params=params(),
        cost_estimate=cost(2 * count * D * D * steps, 2 * D * steps * (3 * count + 2 * D), count * D * steps),
        name="up",
    )(scal, quarters, h2, bias, *weight)


def act_back_kernel(samples, scal, quarters, gm, slope, weight, *refs):
    gu, gu_sum = refs[-2:]
    total = jnp.zeros((1, D), F32)
    for s in range(samples):
        rows = slice(s * GRID, (s + 1) * GRID)
        low = (dot(gm[rows, :], weight[0]) * slope[rows, :].astype(F32)).astype(BF)
        gu[0, rows, :] = low
        total = total + column_sum(low)
    gu_sum[...] = total


def act_back(gm, slope, weight, scal, quarters, prior):
    count, steps = gm.shape[0], quarters.shape[0]
    whole = pl.BlockSpec((count, D), lambda k, *_: (0, 0))
    return pl.pallas_call(
        functools.partial(act_back_kernel, count // GRID),
        grid_spec=pltpu.PrefetchScalarGridSpec(
            num_scalar_prefetch=2,
            grid=(steps,),
            in_specs=[
                whole,
                pl.BlockSpec((None, count, D), lambda k, *_: (k, 0, 0)),
                pl.BlockSpec((1, D, D), lambda k, scal, q: (q[k], 0, 0)),
            ]
            + [anywhere(0)] * (prior is not None),
            out_specs=[
                pl.BlockSpec((1, count, D), lambda k, *_: (k, 0, 0)),
                pl.BlockSpec((1, D), lambda k, scal, q: (0, q[k])),
            ],
        ),
        out_shape=[jax.ShapeDtypeStruct((steps, count, D), BF), jax.ShapeDtypeStruct((1, FF), F32)],
        input_output_aliases={} if prior is None else {5: 1},
        compiler_params=params(),
        cost_estimate=cost(2 * count * D * D * steps, 2 * D * steps * (2 * count + D)),
        name="act_back",
    )(scal, quarters, gm, slope, weight, *([] if prior is None else [prior]))


def turned_product(parts, scal, quarters, weights, late, late_specs, outs, finish, span, name, prior=None):
    first, samples = span
    count, tiles = samples * GRID, quarters.shape[0]
    kept = [] if prior is None else [(i, v) for i, v in enumerate(prior) if v is not None]
    used = len(parts) + len(weights)

    def body(scal_ref, quarters_ref, *refs):
        ins, ws = refs[: len(parts)], refs[len(parts) : used]
        late_refs = refs[used : used + len(late)]
        out_refs = refs[used + len(late) + len(kept) :]
        total, tile = None, 0
        for n, ref in enumerate(ins):
            blocks = ref.shape[0] if len(ref.shape) == 3 else ref.shape[1] // D
            for k in range(min(blocks, tiles - tile)):
                left = ref[k] if len(ref.shape) == 3 else ref[:, k * D : (k + 1) * D]
                right = ws[n][k] if len(ws) > 1 else ws[0][quarters_ref[tile]]
                part = dot_rt(left, right)
                total = part if total is None else total + part
                tile += 1
        finish(span, scal_ref, pl.program_id(0), total, late_refs, out_refs)

    def part_spec(part):
        offset = 0 if part.shape[-2] == count else first
        if part.ndim == 2:
            return pl.BlockSpec((GRID, part.shape[1]), lambda s, *_: (s + offset, 0))
        return pl.BlockSpec((part.shape[0], GRID, D), lambda s, *_: (0, s + offset, 0))

    def weight_spec(weight):
        blocks = min(weight.shape[0], tiles)
        return pl.BlockSpec((blocks, D, D), lambda s, *_: (0, 0, 0), pipeline_mode=pl.Buffered(1))

    return pl.pallas_call(
        body,
        grid_spec=pltpu.PrefetchScalarGridSpec(
            num_scalar_prefetch=2,
            grid=(samples,),
            in_specs=[part_spec(part) for part in parts]
            + [weight_spec(weight) for weight in weights]
            + [spec(first) for spec in late_specs]
            + [anywhere(first)] * len(kept),
            out_specs=[spec(first) for _, _, spec in outs],
        ),
        out_shape=[jax.ShapeDtypeStruct(shape, kind) for shape, kind, _ in outs],
        input_output_aliases={2 + used + len(late) + n: i for n, (i, _) in enumerate(kept)},
        compiler_params=params(),
        cost_estimate=cost(2 * count * D * D * tiles, 2 * D * tiles * (count + D) + 10 * count * D),
        name=name,
    )(scal, quarters, *parts, *weights, *late, *[v for _, v in kept])


def mid_back_finish(span, scal, sample, grad, late, outs):
    middle, branch, cg, mods = late
    gmid, gbr, gbr_sum, grads = outs
    unit, inverse = normal(middle[...])
    whole = cg[...].astype(F32) + norm_back(unit, inverse, grad * (1.0 + mods[0, 4:5]))
    gmid[...] = whole
    low = (mods[0, 2:3] * whole).astype(BF)
    gbr[...] = low
    accumulate(gbr_sum, column_sum(low), sample)
    grads[0, 0:1] = column_sum(whole * branch[...].astype(F32))
    grads[0, 1:2] = column_sum(grad)
    grads[0, 2:3] = column_sum(grad * unit)


def front_back_finish(span, scal, sample, grad, late, outs):
    xg, gmid, mods, column = late
    tgrad, grads = outs
    unit, inverse = normal(xg[...].astype(F32))
    grads[0, 0:1] = column_sum(grad)
    grads[0, 1:2] = column_sum(grad * unit)
    whole = gmid[...] + norm_back(unit, inverse, grad * (1.0 + mods[0, 1:2]))
    pick = (lax.broadcasted_iota(jnp.int32, (GRID, GRID), 1) == column[...]).astype(F32).astype(BF)
    high = whole.astype(BF)
    rest = (whole - high.astype(F32)).astype(BF)
    tgrad[...] = dot(pick, high) + dot(pick, rest)


def down_finish(span, scal, sample, product, late, outs):
    middle, cg, mods, bias, column = late
    out, grads = outs
    mlp = product + bias[...]
    grads[0] = column_sum(cg[...].astype(F32) * mlp)
    final = (middle[...] + mods[0, 5:6] * mlp).astype(BF)
    length = scal[2 + span[0] + sample]
    spots = lax.broadcasted_iota(jnp.int32, (GRID, GRID), 1)
    slots = lax.broadcasted_iota(jnp.int32, (GRID, GRID), 0)
    pick = jnp.logical_and(spots == column[...], slots < length).astype(F32).astype(BF)
    out[...] = dot(pick, final).astype(BF)


def attend_back_kernel(span, scal, gbr, packed, lse, mask, table, weight, joined, joined_sum, placed, gatt, gq, gk, gv):
    gatt[...] = dot_rt(gbr[...], weight[0]).astype(BF)
    for ref in (gq, gk, gv):
        ref[...] = jnp.zeros_like(ref)

    @pl.when(pl.program_id(0) == 0)
    def _():
        placed[...] = jnp.zeros_like(placed)
        joined_sum[...] = jnp.zeros_like(joined_sum)

    lane = lax.broadcasted_iota(jnp.int32, (GRID, 128), 1)

    def head(h, _):
        start, inside = window(h)
        cols = pl.ds(start, 256)
        query = packed[:, cols] * inside
        key = packed[:, pl.ds(pl.multiple_of(D + start, 128), 256)] * inside
        value = packed[:, pl.ds(pl.multiple_of(2 * D + start, 128), 256)]
        grad = gatt[:, cols] * inside
        scores = dot_rt(query, key) * (SCALE * LIFT) + table[h] + mask[0]
        own = jnp.sum(jnp.where(lane == h, lse[...], 0.0), axis=1, keepdims=True)
        probs = jnp.exp2(scores - own)
        gprobs = dot_rt(grad, value)
        weighted = probs * gprobs
        inner = jnp.sum(weighted, axis=1, keepdims=True)
        gscores = (weighted - probs * inner).astype(BF)
        placed[h] = placed[h] + gscores.astype(F32)
        gq[:, cols] = gq[:, cols] + dot(gscores, key)
        gk[:, cols] = gk[:, cols] + dot_lt(gscores, query)
        gv[:, cols] = gv[:, cols] + dot_lt(probs.astype(BF), grad)
        return 0

    lax.fori_loop(0, HEADS, head, 0, unroll=HEADS)
    for j, (ref, factor) in enumerate(((gq, SCALE), (gk, SCALE), (gv, 1.0))):
        cols = slice(j * D, (j + 1) * D)
        low = (ref[...] * factor).astype(BF)
        joined[:, cols] = low
        joined_sum[:, cols] = joined_sum[:, cols] + column_sum(low)
    joined[:, 3 * D :] = gbr[...]


def column_block(array, rows, width, at, row=0):
    if array.ndim == 2:
        return pl.BlockSpec((rows, width), lambda *a: (row, at(*a)))
    return pl.BlockSpec((None, rows, width), lambda *a: (at(*a), row, 0))


def plain_outer_kernel(kinds, scal, *refs):
    lefts, (right, out) = refs[:kinds], refs[kinds:]
    for kind, left in enumerate(lefts):
        def product():
            out[0] = dot_lt(left[...], right[...]).astype(BF)

        if kinds == 1:
            product()
        else:
            pl.when((pl.program_id(0) == QUARTERS - 1) == (kind == 1))(product)


def plain_outer(lefts, right, scal, name):
    count = right.shape[-2]
    return pl.pallas_call(
        functools.partial(plain_outer_kernel, len(lefts)),
        grid_spec=pltpu.PrefetchScalarGridSpec(
            num_scalar_prefetch=1,
            grid=(QUARTERS,),
            in_specs=[pl.BlockSpec((count, D), lambda q, *_: (0, 0))] * len(lefts)
            + [column_block(right, count, D, lambda q, *_: q)],
            out_specs=pl.BlockSpec((1, D, D), lambda q, *_: (q, 0, 0)),
        ),
        out_shape=jax.ShapeDtypeStruct((QUARTERS, D, D), BF),
        compiler_params=params(),
        cost_estimate=cost(2 * count * D * WIDE, 2 * count * (D + WIDE) + 2 * D * WIDE),
        name=name,
    )(scal, *lefts, right)


def outer_kernel(kinds, sources, tile_width, roles, parts, order, scal, blocks, *refs):
    lefts, rights = refs[: sources * kinds], refs[sources * kinds : sources * (kinds + 1)]
    outs, tile = refs[sources * (kinds + 1) : -1], refs[-1]
    step = pl.program_id(0)

    def product(kind, cols):
        total = dot_lt(lefts[sources * kind][...], rights[0][:, cols])
        for n in range(1, sources):
            total = total + dot_lt(lefts[sources * kind + n][...], rights[n][:, cols])
        tile[:, cols] = total.astype(BF)

    if kinds == 1:
        product(0, slice(0, tile_width))
    else:
        half = tile_width // 2
        for part in range(2):
            from_first = blocks[step] * 2 + part < 3 * D // half
            cols = slice(part * half, (part + 1) * half)
            pl.when(from_first)(functools.partial(product, 0, cols))
            pl.when(jnp.logical_not(from_first))(functools.partial(product, 1, cols))
    for r in range(roles):
        @pl.when(step == r)
        def _():
            for i in range(8):
                start = i * ROWS8 if order is None else pl.multiple_of((scal[0] ^ order[i]) * ROWS8, ROWS8)
                rows = pl.ds(start, ROWS8)
                outs[parts * r + i * parts // 8][i % (8 // parts)] = tile[rows, :]


def outer_tiles(lefts, rights, scal, blocks, width, parts, order, name):
    count, kinds, roles, sources = rights[0].shape[-2], len(lefts), blocks.shape[0], len(rights)
    some = pl.BlockSpec((8 // parts, ROWS8, width), lambda r, *_: (0, 0, 0))
    each = sources // len(lefts[0])
    left_specs = [pl.BlockSpec((count, D), lambda r, *_, n=n: (n, 0)) for n in range(each)] * (len(lefts[0]) * kinds)
    return pl.pallas_call(
        functools.partial(outer_kernel, kinds, sources, width, roles, parts, order),
        grid_spec=pltpu.PrefetchScalarGridSpec(
            num_scalar_prefetch=2,
            grid=(roles,),
            in_specs=left_specs + [column_block(rights[0], count, width, lambda r, scal, blocks: blocks[r])] * sources,
            out_specs=[some] * (parts * roles),
            scratch_shapes=[pltpu.VMEM((D, width), BF)],
        ),
        out_shape=[jax.ShapeDtypeStruct((8 // parts, ROWS8, width), BF)] * (parts * roles),
        compiler_params=params(),
        cost_estimate=cost(
            2 * sources * count * D * width * roles, 2 * sources * count * (D * kinds + width * roles)
        ),
        name=name,
    )(scal, blocks, *[v for left in lefts for v in left for _ in range(each)], *rights)


ON_THE_WAY = []


def flip(value, axis, size, bit):
    ON_THE_WAY.append(lax.ppermute(value, axis, [(i, i ^ bit) for i in range(size)]))
    return ON_THE_WAY[-1]


def bits_of(size):
    return [1 << k for k in range(size.bit_length() - 1)]


def gather_steps(value, axes):
    for axis, size in axes:
        own = lax.axis_index(axis)
        for bit in bits_of(size):
            (value,) = yield [value]
            other = flip(value, axis, size, bit)
            low = (own & bit) == 0
            value = jnp.concatenate([jnp.where(low, value, other), jnp.where(low, other, value)], axis=0)
    return value


def scatter_steps(value, axis, size):
    own = lax.axis_index(axis)
    for bit in bits_of(size):
        value = value.reshape((value.shape[0] // 2, 2) + value.shape[1:])
        low = (own & bit) == 0
        keep = jnp.where(low, value[:, 0], value[:, 1])
        send = jnp.where(low, value[:, 1], value[:, 0]).astype(BF)
        (send,) = yield [send]
        value = keep + flip(send, axis, size, bit).astype(F32)
    return value


class Chain:
    def __init__(self, steps):
        self.steps, self.result = steps, None
        self.ready = next(steps)

    def advance(self, operands):
        if self.result is None:
            try:
                self.ready = self.steps.send(operands)
            except StopIteration as end:
                self.ready, self.result = [], end.value

    def finish(self):
        while self.result is None:
            self.advance(self.ready)
        return self.result


def slot(inputs, chains=(), after=(), slow=()):
    chains, slow = list(chains), list(slow)
    inputs, operands, _ = lax.optimization_barrier(
        (tuple(inputs), [c.ready for c in chains + slow], (*after, *ON_THE_WAY))
    )
    ON_THE_WAY.clear()
    for chain, ready in zip(slow, operands[len(chains) :]):
        chain.advance(ready)
    ON_THE_WAY.clear()
    for chain, ready in zip(chains, operands):
        chain.advance(ready)
    return inputs


class Wires:
    def __init__(self, mesh):
        self.dp, self.seq = mesh.shape["dp"], mesh.shape["seq"]
        self.cube = self.dp == 4 and self.seq == 8
        self.place, self.me = lax.axis_index("dp"), lax.axis_index("seq")

    def far(self, value, bit):
        return flip(value, "seq", self.seq, bit)

    def across(self, value):
        return flip(value, "dp", self.dp, 2)

    def sibling(self, value):
        return flip(value, "dp", self.dp, 1)

    def quarter(self, shards):
        if len(shards) == 1:
            return lax.dynamic_slice_in_dim(shards[0], self.place * D, D, 1)[None]
        heads = lax.dynamic_slice_in_dim(shards[0], jnp.minimum(self.place, 2) * D, D, 1)
        return jnp.where(self.place == 3, shards[1], heads)[None]

    def gather(self, quarter):
        return lax.all_gather(quarter, ("dp", "seq"), axis=0, tiled=True).reshape(QUARTERS, D, D)

    def gather_steps(self, quarter):
        (one,) = yield [quarter]
        two = jnp.concatenate([one, self.far(one, 4)], axis=0)
        (two,) = yield [two]
        four = jnp.concatenate([two, self.far(two, 2)], axis=0)
        (four,) = yield [four]
        rest, cross = self.far(four, 1), self.across(four)
        rest, cross, four = yield [rest, cross, four]
        cross_rest, near = self.across(rest), [self.sibling(four), self.sibling(rest), self.sibling(cross)]
        cross_rest, *near = yield [cross_rest, *near]
        return [four, rest, cross, cross_rest], [*near, self.sibling(cross_rest)]

    def scatter(self, whole):
        rows = D // self.seq
        parts = whole.reshape(QUARTERS * self.seq, rows, D)
        return lax.psum_scatter(parts, ("dp", "seq"), scatter_dimension=0, tiled=True)

    def spread(self, part):
        parts = yield from gather_steps(part, (("dp", self.dp),))
        return jnp.concatenate([parts[q] for q in range(QUARTERS)], axis=1)

    def reduce_quarter(self, cross, quarter, groups):
        got = {}
        for group in groups:
            sent = yield [cross[part] for part in group]
            for part, value in zip(group, sent):
                got[part] = self.across(value)
        upper = [(quarter[part].astype(F32) + got[part].astype(F32)).astype(BF) for part in (2, 3)]
        left = [part for part in (0, 1) if part not in got]
        send, *sent = yield [jnp.concatenate(upper, axis=0)] + [cross[part] for part in left]
        near = self.far(send, 1)
        for part, value in zip(left, sent):
            got[part] = self.across(value)
        (send,) = yield [(total_of([quarter[1], got[1]], 0, 2) + near[2:4].astype(F32)).astype(BF)]
        parts = [quarter[0], got[0], near, self.far(send, 2)]
        (send,) = yield [total_of(parts, 1, 2).astype(BF)]
        parts.append(self.far(send, 4))
        return (yield from self.spread(total_of(parts, 0, 1).astype(BF)))

    def reduce(self, give):
        core, x = self.place % 2, self.place // 2
        give = yield [give[1], give[0], give[2]]
        got = [self.sibling(value) for value in give]
        keep = yield []
        cross, quarter, common = [keep[1], got[0]], [keep[0], got[1]], [keep[2], got[2]]
        (high,) = yield [total_of(cross, 4, 8).astype(BF)]
        high = self.across(high)
        low, send = yield [total_of(cross, 0, 4).astype(BF), total_of(common, 4, 8).astype(BF)]
        low = self.across(low)
        common.append(self.far(send, 1))
        send, other = yield [
            (total_of(quarter, 4, 8) + high.astype(F32)).astype(BF), total_of(common, 2, 4).astype(BF)
        ]
        quarter += [low, self.far(send, 1)]
        common.append(self.far(other, 2))
        send, other = yield [total_of(quarter, 2, 4).astype(BF), total_of(common, 1, 2).astype(BF)]
        quarter.append(self.far(send, 2))
        common.append(self.far(other, 4))
        send, end = yield [total_of(quarter, 1, 2).astype(BF), total_of(common, 0, 1).astype(BF)]
        quarter.append(self.far(send, 4))
        (ends,) = yield [jnp.concatenate([total_of(quarter, 0, 1).astype(BF), end], axis=0)]
        other = self.across(ends)
        shared = (ends[1].astype(F32) + other[1].astype(F32)).astype(BF)
        (mine,) = yield [jnp.stack([ends[0], other[0], shared])]
        theirs = self.sibling(mine)
        columns = []
        first, left = core == 0, x == 0
        for quarter_index in range(4):
            of_core, of_x = divmod(quarter_index, 2)
            near, far = (mine, theirs) if of_core == 0 else (theirs, mine)
            same = jnp.where(first, near[:2], far[:2])
            columns.append(jnp.where(left == (of_x == 0), same[0], same[1]))
        columns.append(jnp.where(first, mine[2], theirs[2]))
        columns.append(jnp.where(first, theirs[2], mine[2]))
        return jnp.concatenate(columns, axis=1)

    def roles(self):
        core, x = self.place % 2, self.place // 2
        return jnp.stack([2 * core + x, 2 * core + 1 - x, 4 + core]).astype(jnp.int32)


def total_of(parts, start, stop):
    summed = 0.0
    for part in parts:
        summed = summed + part[start:stop].astype(F32)
    return summed


def unit_gaps():
    spots = np.arange(SIDE)
    reach = np.arange(SPAN)
    return (spots[None, :, None] - spots[None, None, :] + (SIDE - 1) == reach[:, None, None]).astype(np.float32)


def local(
    mesh,
    tokens,
    condition,
    lengths,
    kept_index,
    heads_weight,
    heads_bias,
    merge_weight,
    merge_bias,
    up_weight,
    up_bias,
    down_weight,
    down_bias,
    modulate_weight,
    modulate_bias,
    relative_table,
    cotangent,
):
    ON_THE_WAY.clear()
    wires = Wires(mesh)
    dp, seq = wires.dp, wires.seq
    samples, count = kept_index.shape[0], tokens.shape[0]
    shard_rows = heads_weight.shape[0]
    everything, half_a, half_b = (0, samples), (0, samples // 2), (samples // 2, samples - samples // 2)
    everyone = (("seq", seq), ("dp", dp))
    line = lambda v: v.astype(F32).reshape(1, -1)
    scal = jnp.concatenate([jnp.stack([wires.me, wires.place]).astype(jnp.int32), lengths])
    in_order = jnp.arange(QUARTERS, dtype=jnp.int32)

    own_cols = lax.dynamic_slice_in_dim(condition, wires.me * shard_rows, shard_rows, 1)
    own_silu = jax.nn.silu(own_cols.astype(F32)).astype(BF)
    partial = dot(own_silu, modulate_weight).reshape(seq, samples, 6 * D)
    mod_chain = Chain(scatter_steps(partial, "seq", seq))
    cond_chain = Chain(gather_steps(own_cols, (("dp", dp),)))
    joint = wires.gather(wires.quarter([heads_weight, merge_weight]))
    up_chain = [Chain(wires.gather_steps(wires.quarter([up_weight])))] if wires.cube else []
    upw = None if wires.cube else wires.gather(wires.quarter([up_weight]))

    index_row = kept_index.reshape(samples, 1, GRID)
    index_col = kept_index.reshape(count, 1)
    inputs = slot((tokens, cotangent, index_row), [cond_chain], slow=up_chain)
    xg, cg, mask = call(
        place_kernel, scal, inputs, [rows_spec(D), rows_spec(D), per_sample(1, GRID)],
        [((count, D), BF, rows_spec(D)), ((count, D), BF, rows_spec(D)), ((samples, 1, GRID), F32, per_sample(1, GRID))],
        [], everything, "place", cost(4 * count * GRID * D, 8 * count * D),
    )
    (later, _) = lax.optimization_barrier((down_weight, mask))
    downw = wires.gather(wires.quarter([later]))

    gaps = unit_gaps()
    turned = relative_table.reshape(HEADS, SPAN, SPAN)[:, ::-1]
    strips = jnp.einsum("hkj,jpq->hpkq", turned, jnp.asarray(gaps, BF), preferred_element_type=F32)
    strips = jnp.pad(strips.reshape(HEADS, SIDE, SPAN * SIDE), ((0, 0), (0, 0), (0, SIDE)))
    inputs = slot((strips,), up_chain + [mod_chain, cond_chain], (mask,))
    (table,) = call(
        bias_kernel, scal, inputs, [per_sample(SIDE, 2 * GRID)], [((HEADS, GRID, GRID), F32, per_sample(GRID, GRID))],
        [], (0, HEADS), "bias", cost(0, 5 << 20),
    )
    (table,) = slot((table,), [mod_chain], slow=up_chain)
    (table,) = slot((table,), [mod_chain])
    modulation = mod_chain.finish().reshape(samples, 6 * D) + modulate_bias.astype(F32)
    mods = modulation.reshape(samples, 6, D)

    full_bias = jnp.concatenate([heads_bias[:D], jnp.zeros((D,), BF), heads_bias[D:]])
    inputs = slot((xg, mods, line(full_bias), joint), slow=up_chain, after=(table,))
    h1, packed = call(
        qkv_kernel, scal, inputs,
        [rows_spec(D), per_sample(6, D), fixed(1, 3 * D), fixed(3, D, D)],
        [((count, D), BF, rows_spec(D)), ((count, 3 * D), BF, rows_spec(3 * D))],
        [], everything, "qkv", cost(2 * count * D * 3 * D, 22 << 20),
    )
    inputs = slot((packed, mask, table))
    attended, lse = call(
        attend_kernel, scal, inputs, [rows_spec(3 * D), per_sample(1, GRID), fixed(HEADS, GRID, GRID)],
        [((count, D), BF, rows_spec(D)), ((count, 128), F32, rows_spec(128))],
        [pltpu.VMEM((GRID, D), F32)], everything, "attend", cost(4 * count * GRID * 256 * HEADS, 15 << 20, count * GRID * HEADS),
    )
    inputs = slot((attended, xg, cg, mods, line(merge_bias), joint), slow=up_chain)
    branch, middle, h2, gm, gm_sum = call(
        merge_kernel, scal, inputs,
        [rows_spec(D), rows_spec(D), rows_spec(D), per_sample(6, D), fixed(1, D), fixed(1, D, D, at=(3, 0, 0))],
        [((count, D), BF, rows_spec(D)), ((count, D), F32, rows_spec(D)), ((count, D), BF, rows_spec(D)),
         ((count, D), BF, rows_spec(D)), ((1, D), F32, fixed(1, D))],
        [], everything, "merge", cost(2 * count * D * D, 20 << 20),
    )

    def pair(values):
        return [[v, wires.sibling(v)] for v in values]

    up_line, sums = line(up_bias), []
    if wires.cube:
        place = wires.place.astype(jnp.int32)
        own_quarters, their_quarters = jnp.stack([place, place ^ 2]), jnp.stack([place ^ 1, place ^ 3])
        order, cross_first = jnp.concatenate([own_quarters, their_quarters]), jnp.array([1, 0], jnp.int32)
        own_pieces, their_pieces = up_chain[0].finish()
        h2, *their_pieces = slot((h2, *their_pieces))
        act_theirs, slope_theirs, up_theirs = up_quarters(h2, up_line, their_pieces, scal, their_quarters, (1, 3))
        h2, *own_pieces = slot((h2, *own_pieces), after=(act_theirs,))
        arrived = wires.sibling(act_theirs)
        gm_pair, h2_pair = pair([gm, h2])
        act_own, slope_own, up_own = up_quarters(h2, up_line, own_pieces, scal, own_quarters, (0, 2))
        acts, upws = [act_own, act_theirs], [up_own, up_theirs]
        act_own, arrived = slot((act_own, arrived))
        tiles = outer_tiles([gm_pair], [act_own, arrived], scal, cross_first, D, 4, ORDER, "down_outer")
        down_sum = Chain(wires.reduce_quarter(tiles[:4], tiles[4:], ((2,), (3,))))
        gm, slope_theirs, downw = slot((gm, slope_theirs, downw), after=(tiles[0],))
        gu_theirs, gu_sum = act_back(gm, slope_theirs, downw, scal, their_quarters, None)
        gm, slope_own, downw, gu_sum = slot((gm, slope_own, downw, gu_sum), [down_sum], (gu_theirs,))
        arrived = wires.sibling(gu_theirs)
        gu_own, gu_sum = act_back(gm, slope_own, downw, scal, own_quarters, gu_sum)
        gu_parts = [gu_own, gu_theirs]
        gu_own, arrived = slot((gu_own, arrived), [down_sum])
        tiles = outer_tiles([h2_pair], [gu_own, arrived], scal, cross_first, D, 4, ORDER, "up_outer")
        up_sum = Chain(wires.reduce_quarter(tiles[:4], tiles[4:], ((2, 3),)))
        sums = [down_sum, up_sum]
        gu_parts = slot(gu_parts, [down_sum], (tiles[0],))
    else:
        order, upws = in_order, [upw]
        act, slope = up_quarters(h2, up_line, upw, scal, in_order, None)
        down_part = wires.scatter(plain_outer([gm], act, scal, "down_outer"))
        gu, gu_sum = act_back(gm, slope, downw, scal, in_order, None)
        up_part = wires.scatter(plain_outer([h2], gu, scal, "up_outer"))
        acts, gu_parts = [act], [gu]

    gmid, gbr, gbr_sum, mid_grads = turned_product(
        gu_parts, scal, order, upws, (middle, branch, cg, mods), [rows_spec(D), rows_spec(D), rows_spec(D), per_sample(6, D)],
        [((count, D), F32, rows_spec(D)), ((count, D), BF, rows_spec(D)), ((1, D), F32, fixed(1, D)), ((samples, 3, D), F32, per_sample(3, D))],
        mid_back_finish, everything, "mid_back",
    )
    mid_rows = jnp.pad(mid_grads.astype(BF), ((0, 0), (0, 1), (0, 0))).reshape(1, samples * 4, D)
    mid_all = lax.all_gather(mid_rows, ("dp", "seq"), axis=0, tiled=True).reshape(-1, 4, D)[:, :3].reshape(-1, 3 * D)

    def attend_part(chains, after, span):
        inputs = slot((gbr, packed, lse, mask, table, joint), chains, after)
        return call(
            attend_back_kernel, scal, inputs,
            [rows_spec(D), rows_spec(3 * D), rows_spec(128), per_sample(1, GRID), fixed(HEADS, GRID, GRID), fixed(1, D, D, at=(3, 0, 0))],
            [((span[1] * GRID, WIDE), BF, own_rows(WIDE)),
             ((1, 3 * D), F32, fixed(1, 3 * D)), ((HEADS, GRID, GRID), F32, fixed(HEADS, GRID, GRID))],
            [pltpu.VMEM((GRID, D), BF)] + [pltpu.VMEM((GRID, D), F32)] * 3,
            span, "attend_back", cost(count * D * D + 5 * count * GRID * 256 * HEADS, 20 << 20),
        )

    joined_a, joined_sum_a, placed_a = attend_part(sums, (), half_a)
    joined_b, joined_sum_b, placed_b = attend_part(sums, (joined_a,), half_b)
    joined_sum = joined_sum_a + joined_sum_b

    done = joined_b
    if wires.cube:
        lefts, roles = [[h1], [attended]], wires.roles()
        theirs = jnp.stack([roles[0] ^ 2, roles[1] ^ 2, roles[2] ^ 1])
        rights = slot((joined_a, joined_b), slow=sums)
        give = outer_tiles(lefts, rights, scal, theirs, TILE, 1, ORDER, "joint_give")
        joint_sum = Chain(wires.reduce(give))
        rights = slot(rights, [joint_sum], (give[0],), slow=sums[:1])
        keep = outer_tiles(lefts, rights, scal, roles, TILE, 1, ORDER, "joint_keep")
        joint_sum.ready = tuple(keep)
        joint_sum.advance(joint_sum.ready)
        done = keep[0]

    joints = [joint_sum] if wires.cube else []
    placed_a, placed_b = slot((placed_a, placed_b), (), (done,), slow=joints + sums[1:])
    (strip_grad,) = call(
        strips_kernel, scal, (placed_a, placed_b), [four_heads(GRID)] * 2,
        [((HEADS, SIDE, 2 * GRID), F32, four_heads(SIDE, 2 * GRID))], [], (0, HEADS // 4), "strips", cost(0, 9 << 20),
    )
    strip_grad = strip_grad[:, :, : SPAN * SIDE].reshape(HEADS, SIDE, SPAN, SIDE)
    table_grad = jnp.einsum(
        "hpkq,jpq->hkj", strip_grad, jnp.asarray(gaps), precision=lax.Precision.HIGHEST
    )[:, ::-1].reshape(-1)
    sizes = [2 * D, D, FF, D, HEADS * SPAN * SPAN]
    loose = jnp.concatenate(
        [joined_sum[0, :D], joined_sum[0, 2 * D :], gbr_sum[0], gu_sum[0], gm_sum[0], table_grad]
    )
    loose = jnp.pad(loose, (0, -loose.shape[0] % 1024)).reshape(-1, 128)
    loose = jnp.sum(lax.all_gather(loose, ("dp", "seq")), axis=0)
    done = strip_grad
    def front_part(own, chains, after, span, prior):
        (own,) = slot((own,), chains, after)
        return turned_product(
            [own], scal, in_order[:3], [joint], (xg, gmid, mods, index_col),
            [rows_spec(D), rows_spec(D), per_sample(6, D), rows_spec(1)],
            [((count, D), F32, rows_spec(D)), ((samples, 2, D), F32, per_sample(2, D))],
            front_back_finish, span, "front_back", prior,
        )

    def down_part_of(chains, after, span, prior, slow=()):
        own = slot(acts, chains, after, slow)
        return turned_product(
            own, scal, order, [downw], (middle, cg, mods, line(down_bias), index_col),
            [rows_spec(D), rows_spec(D), per_sample(6, D), fixed(1, D), rows_spec(1)],
            [((count, D), BF, rows_spec(D)), ((samples, 1, D), F32, per_sample(1, D))],
            down_finish, span, "down", prior,
        )

    output, down_grads = down_part_of([], (done,), half_a, None, joints)
    output, down_grads = down_part_of(joints, (down_grads,), half_b, [output, down_grads])
    tgrad, front_grads = front_part(joined_a, joints + sums, (output,), half_a, None)
    tgrad, front_grads = front_part(joined_b, joints + sums, (front_grads,), half_b, [tgrad, front_grads])

    end_grads = jnp.concatenate([front_grads, down_grads], axis=1).astype(BF).reshape(samples, 3 * D)
    end_chain = Chain(gather_steps(end_grads, everyone))
    if wires.cube:
        (mid_all,) = slot((mid_all,), [joint_sum, end_chain])
        (mid_all,) = slot((mid_all,), [joint_sum, end_chain], (loose,))
        up_grad, down_grad, joint_grad = up_sum.finish(), down_sum.finish(), joint_sum.finish()
    else:
        up_grad = Chain(wires.spread(up_part)).finish()
        down_grad = Chain(wires.spread(down_part)).finish()
        joint_grad = wires.scatter(plain_outer([h1, attended], jnp.concatenate([joined_a, joined_b]), scal, "joint_outer"))
        joint_grad = Chain(wires.spread(joint_grad)).finish()
    loose = loose.reshape(-1)
    end_all = end_chain.finish()
    mod_all = jnp.concatenate([end_all[:, : 2 * D], mid_all, end_all[:, 2 * D :]], axis=1)
    silu_all = jax.nn.silu(cond_chain.finish().astype(F32)).astype(BF)
    modulate_grad = dot_lt(silu_all, mod_all)
    modulate_total = jnp.sum(mod_all.astype(F32), axis=0)

    edges = np.cumsum([0] + sizes)
    heads_total, merge_total, up_total, down_total, table_total = [
        loose[a:b] for a, b in zip(edges[:-1], edges[1:])
    ]
    return (
        output,
        tgrad,
        joint_grad[:, : 3 * D].astype(F32),
        joint_grad[:, 3 * D :].astype(F32),
        up_grad.astype(F32),
        down_grad.astype(F32),
        modulate_grad,
        heads_total,
        merge_total,
        up_total,
        down_total,
        modulate_total,
        table_total.reshape(HEADS, SPAN * SPAN),
    )


def solution(mesh):
    in_specs = (
        P(("dp", "seq"), None),
        P("dp", None),
        P(("dp", "seq")),
        P(("dp", "seq"), None),
        P("seq", None),
        P(),
        P("seq", None),
        P(),
        P("seq", None),
        P(),
        P("seq", None),
        P(),
        P("seq", None),
        P(),
        P(),
        P(("dp", "seq"), None),
    )
    out_specs = (
        P(("dp", "seq"), None),
        P(("dp", "seq"), None),
        P("seq", None),
        P("seq", None),
        P("seq", None),
        P("seq", None),
        P("seq", None),
        P(),
        P(),
        P(),
        P(),
        P(),
        P(),
    )
    return jax.shard_map(
        functools.partial(local, mesh), mesh=mesh, in_specs=in_specs, out_specs=out_specs, check_vma=False
    )
```

```python
import functools
import math

import jax
import jax.numpy as jnp
import numpy as np
from jax import lax
from jax.experimental import pallas as pl
from jax.experimental.pallas import tpu as pltpu
from jax.sharding import PartitionSpec as P

D = 1152
HEADS = 16
HEAD = 72
FF = 4608
SIDE = 16
GRID = 256
SPAN = 2 * SIDE - 1
WIDE = 4608
TILE = 768
ROWS8 = 144
QUARTERS = 4
LIFT = math.log2(math.e)
SCALE = 1.0 / math.sqrt(HEAD)
EPS = 1e-06
ORDER = (0, 4, 2, 6, 1, 5, 3, 7)
BF = jnp.bfloat16
F32 = jnp.float32
VMEM_LIMIT = 60 * 1024 * 1024


def dot(a, b):
    return jnp.dot(a, b, preferred_element_type=F32)


def dot_rt(a, b):
    return lax.dot_general(a, b, (((1,), (1,)), ((), ())), preferred_element_type=F32)


def dot_lt(a, b):
    return lax.dot_general(a, b, (((0,), (0,)), ((), ())), preferred_element_type=F32)


def params():
    return pltpu.CompilerParams(
        vmem_limit_bytes=VMEM_LIMIT, dimension_semantics=("arbitrary",)
    )


def cost(flops, bytes_accessed, transcendentals=0):
    return pl.CostEstimate(
        flops=int(flops), bytes_accessed=int(bytes_accessed), transcendentals=int(transcendentals)
    )


def rows_spec(width):
    return lambda first: pl.BlockSpec((GRID, width), lambda s, *_: (s + first, 0))


def own_rows(width):
    return lambda first: pl.BlockSpec((GRID, width), lambda s, *_: (s, 0))


def per_sample(*tail):
    return lambda first: pl.BlockSpec((1,) + tail, lambda s, *_: (s + first,) + (0,) * len(tail))


def four_heads(rows, columns=GRID):
    return lambda first: pl.BlockSpec((4, rows, columns), lambda s, *_: (s, 0, 0))


def fixed(*shape, at=None):
    where = (0,) * len(shape) if at is None else at
    return lambda first: pl.BlockSpec(shape, lambda s, *_: where)


def anywhere(first):
    return pl.BlockSpec(memory_space=pl.ANY)


def call(kernel, scal, inputs, in_specs, outs, scratch, span, name, price, prior=None, steps=None):
    first, samples = span
    kept = [] if prior is None else [(i, v) for i, v in enumerate(prior) if v is not None]
    count = len(inputs)

    def body(scal_ref, *refs):
        kernel(span, scal_ref, *refs[:count], *refs[count + len(kept) :])

    return pl.pallas_call(
        body,
        grid_spec=pltpu.PrefetchScalarGridSpec(
            num_scalar_prefetch=1,
            grid=(samples if steps is None else steps,),
            in_specs=[spec(first) for spec in in_specs] + [anywhere(first)] * len(kept),
            out_specs=[spec(first) for _, _, spec in outs],
            scratch_shapes=scratch,
        ),
        out_shape=[jax.ShapeDtypeStruct(shape, kind) for shape, kind, _ in outs],
        input_output_aliases={1 + count + n: i for n, (i, _) in enumerate(kept)},
        compiler_params=params(),
        cost_estimate=price,
        name=name,
    )(scal, *inputs, *[v for _, v in kept])


def normal(values):
    center = values - jnp.mean(values, axis=-1, keepdims=True)
    inverse = lax.rsqrt(jnp.mean(center * center, axis=-1, keepdims=True) + EPS)
    return center * inverse, inverse


def norm_back(unit, inverse, grad):
    return (
        grad
        - jnp.mean(grad, axis=-1, keepdims=True)
        - unit * jnp.mean(grad * unit, axis=-1, keepdims=True)
    ) * inverse


def accumulate(ref, value, step):
    @pl.when(step == 0)
    def _():
        ref[...] = value

    @pl.when(step > 0)
    def _():
        ref[...] = ref[...] + value


def column_sum(values):
    return jnp.sum(values.astype(F32), axis=0, keepdims=True)


def place_kernel(span, scal, tokens, cotangent, index, xg, cg, mask):
    length = scal[2 + span[0] + pl.program_id(0)]
    spots = lax.broadcasted_iota(jnp.int32, (GRID, GRID), 0)
    slots = lax.broadcasted_iota(jnp.int32, (GRID, GRID), 1)
    hit = spots == index[0]
    xg[...] = dot(hit.astype(F32).astype(BF), tokens[...]).astype(BF)
    alive = jnp.logical_and(hit, slots < length).astype(F32).astype(BF)
    cg[...] = dot(alive, cotangent[...]).astype(BF)
    row = dot_rt(jnp.ones((8, GRID), BF), alive)[0:1]
    mask[0] = jnp.where(row > 0.5, 0.0, -1e30)


def bias_kernel(span, scal, strips, out):
    strip = strips[0]
    for row in range(SIDE):
        start = (SIDE - 1 - row) * SIDE
        out[0, row * SIDE : (row + 1) * SIDE, :] = strip[:, start : start + GRID] * LIFT


def strips_kernel(span, scal, first, second, out):
    for head in range(4):
        total = jnp.zeros((SIDE, 2 * GRID), F32)
        for row in range(SIDE):
            rows = slice(row * SIDE, (row + 1) * SIDE)
            pair = first[head, rows, :] + second[head, rows, :]
            wide = jnp.concatenate([pair, jnp.zeros((SIDE, GRID), F32)], axis=1)
            total = total + pltpu.roll(wide, (SIDE - 1 - row) * SIDE, axis=1)
        out[head] = total


def window(h):
    start = jnp.minimum((h * HEAD) // 128 * 128, D - 256)
    lanes = lax.broadcasted_iota(jnp.int32, (1, 256), 1) + start
    inside = jnp.logical_and(lanes >= h * HEAD, lanes < (h + 1) * HEAD)
    return pl.multiple_of(start, 128), inside.astype(F32).astype(BF)


def piece_copies(pieces, gap_dp, scal, target, sems):
    copies = []
    for i, gap in enumerate(ORDER):
        rows = pl.ds(pl.multiple_of((scal[0] ^ gap) * ROWS8, ROWS8), ROWS8)
        source = pieces[2 * (gap_dp // 2) + i // 4].at[i % 4]
        copies.append(pltpu.make_async_copy(source, target.at[rows, :], sems.at[i]))
    return copies


def qkv_kernel(span, scal, xg, mods, full_bias, weight, h1, packed):
    unit, _ = normal(xg[...].astype(F32))
    hidden = (unit * (1.0 + mods[0, 1:2]) + mods[0, 0:1]).astype(BF)
    h1[...] = hidden
    for j in range(3):
        cols = slice(j * D, (j + 1) * D)
        packed[:, cols] = (dot(hidden, weight[j]) + full_bias[:, cols]).astype(BF)


def attend_kernel(span, scal, packed, mask, table, attended, lse, mixed):
    mixed[...] = jnp.zeros_like(mixed)
    lse[...] = jnp.zeros_like(lse)
    lane = lax.broadcasted_iota(jnp.int32, (GRID, 128), 1)

    def head(h, _):
        start, inside = window(h)
        query = packed[:, pl.ds(start, 256)] * inside
        key = packed[:, pl.ds(pl.multiple_of(D + start, 128), 256)]
        value = packed[:, pl.ds(pl.multiple_of(2 * D + start, 128), 256)] * inside
        scores = dot_rt(query, key) * (SCALE * LIFT) + table[h] + mask[0]
        peak = jnp.max(scores, axis=1, keepdims=True)
        expo = jnp.exp2(scores - peak)
        mass = jnp.sum(expo, axis=1, keepdims=True)
        probs = (expo * (1.0 / mass)).astype(BF)
        cols = pl.ds(start, 256)
        mixed[:, cols] = mixed[:, cols] + dot(probs, value)
        lse[...] = jnp.where(lane == h, peak + jnp.log2(mass), lse[...])
        return 0

    lax.fori_loop(0, HEADS, head, 0, unroll=HEADS)
    attended[...] = mixed[...].astype(BF)


def merge_kernel(span, scal, attended, xg, cg, mods, merge_bias, weight, branch, middle, h2, gm, gm_sum):
    low = (mods[0, 5:6] * cg[...].astype(F32)).astype(BF)
    gm[...] = low
    accumulate(gm_sum, column_sum(low), pl.program_id(0))
    merged = dot(attended[...], weight[0]) + merge_bias[...]
    branch[...] = merged.astype(BF)
    mid = xg[...].astype(F32) + mods[0, 2:3] * merged
    middle[...] = mid
    unit, _ = normal(mid)
    h2[...] = (unit * (1.0 + mods[0, 4:5]) + mods[0, 3:4]).astype(BF)


def up_kernel(samples, gaps, scal, quarters, h2, bias, *refs):
    step = pl.program_id(0)
    if gaps is None:
        weight, act, slope = refs
        matrix = lambda: weight[0]
    else:
        pieces = refs[:4]
        act, slope, spread, target, sems, out_sems = refs[4:]
        steps = len(gaps)
        matrix = lambda: target[step]
        fetch = [piece_copies(pieces, gap, scal, target.at[n], sems.at[n]) for n, gap in enumerate(gaps)]
        store = [pltpu.make_async_copy(target.at[n], spread.at[n], out_sems.at[n]) for n in range(steps)]
        for n in range(steps):
            @pl.when(step == 0)
            def _():
                for copy in fetch[n]:
                    copy.start()
        for n in range(steps):
            @pl.when(step == n)
            def _():
                for copy in fetch[n]:
                    copy.wait()
                store[n].start()

    root = math.sqrt(2.0 / math.pi)
    for s in range(samples):
        rows = slice(s * GRID, (s + 1) * GRID)
        u = dot(h2[rows, :], matrix()) + bias[...]
        square = u * u
        t = jnp.tanh(u * ((root * 0.044715) * square + root))
        half = 0.5 * t + 0.5
        act[rows, :] = (u * half).astype(BF)
        bell = half * (1.0 - half)
        slope[rows, :] = (half + bell * (u * ((6 * root * 0.044715) * square + 2 * root))).astype(BF)
    if gaps is not None:
        for n in range(steps):
            @pl.when(step == steps - 1)
            def _():
                store[n].wait()


def up_quarters(h2, bias, weight, scal, quarters, gaps):
    count, steps = h2.shape[0], quarters.shape[0]
    column = pl.BlockSpec((None, count, D), lambda k, *_: (k, 0, 0))
    out = [jax.ShapeDtypeStruct((steps, count, D), BF)] * 2
    if gaps is None:
        weight = [weight]
        weight_specs, out_specs, scratch = [pl.BlockSpec((1, D, D), lambda k, scal, q: (q[k], 0, 0))], [column] * 2, []
    else:
        weight_specs, out_specs = [anywhere(0)] * 4, [column] * 2 + [anywhere(0)]
        out = out + [jax.ShapeDtypeStruct((steps, D, D), BF)]
        scratch = [pltpu.VMEM((steps, D, D), BF), pltpu.SemaphoreType.DMA((steps, 8)), pltpu.SemaphoreType.DMA((steps,))]
    return pl.pallas_call(
        functools.partial(up_kernel, count // GRID, gaps),
        grid_spec=pltpu.PrefetchScalarGridSpec(
            num_scalar_prefetch=2,
            grid=(steps,),
            in_specs=[pl.BlockSpec((count, D), lambda k, *_: (0, 0)), pl.BlockSpec((1, D), lambda k, scal, q: (0, q[k]))]
            + weight_specs,
            out_specs=out_specs,
            scratch_shapes=scratch,
        ),
        out_shape=out,
        compiler_params=params(),
        cost_estimate=cost(2 * count * D * D * steps, 2 * D * steps * (3 * count + 2 * D), count * D * steps),
        name="up",
    )(scal, quarters, h2, bias, *weight)


def act_back_kernel(samples, scal, quarters, gm, slope, weight, *refs):
    gu, gu_sum = refs[-2:]
    total = jnp.zeros((1, D), F32)
    for s in range(samples):
        rows = slice(s * GRID, (s + 1) * GRID)
        low = (dot(gm[rows, :], weight[0]) * slope[rows, :].astype(F32)).astype(BF)
        gu[0, rows, :] = low
        total = total + column_sum(low)
    gu_sum[...] = total


def act_back(gm, slope, weight, scal, quarters, prior):
    count, steps = gm.shape[0], quarters.shape[0]
    whole = pl.BlockSpec((count, D), lambda k, *_: (0, 0))
    return pl.pallas_call(
        functools.partial(act_back_kernel, count // GRID),
        grid_spec=pltpu.PrefetchScalarGridSpec(
            num_scalar_prefetch=2,
            grid=(steps,),
            in_specs=[
                whole,
                pl.BlockSpec((None, count, D), lambda k, *_: (k, 0, 0)),
                pl.BlockSpec((1, D, D), lambda k, scal, q: (q[k], 0, 0)),
            ]
            + [anywhere(0)] * (prior is not None),
            out_specs=[
                pl.BlockSpec((1, count, D), lambda k, *_: (k, 0, 0)),
                pl.BlockSpec((1, D), lambda k, scal, q: (0, q[k])),
            ],
        ),
        out_shape=[jax.ShapeDtypeStruct((steps, count, D), BF), jax.ShapeDtypeStruct((1, FF), F32)],
        input_output_aliases={} if prior is None else {5: 1},
        compiler_params=params(),
        cost_estimate=cost(2 * count * D * D * steps, 2 * D * steps * (2 * count + D)),
        name="act_back",
    )(scal, quarters, gm, slope, weight, *([] if prior is None else [prior]))


def turned_product(parts, scal, quarters, weights, late, late_specs, outs, finish, span, name, prior=None):
    first, samples = span
    count, tiles = samples * GRID, quarters.shape[0]
    kept = [] if prior is None else [(i, v) for i, v in enumerate(prior) if v is not None]
    used = len(parts) + len(weights)

    def body(scal_ref, quarters_ref, *refs):
        ins, ws = refs[: len(parts)], refs[len(parts) : used]
        late_refs = refs[used : used + len(late)]
        out_refs = refs[used + len(late) + len(kept) :]
        total, tile = None, 0
        for n, ref in enumerate(ins):
            blocks = ref.shape[0] if len(ref.shape) == 3 else ref.shape[1] // D
            for k in range(min(blocks, tiles - tile)):
                left = ref[k] if len(ref.shape) == 3 else ref[:, k * D : (k + 1) * D]
                right = ws[n][k] if len(ws) > 1 else ws[0][quarters_ref[tile]]
                part = dot_rt(left, right)
                total = part if total is None else total + part
                tile += 1
        finish(span, scal_ref, pl.program_id(0), total, late_refs, out_refs)

    def part_spec(part):
        offset = 0 if part.shape[-2] == count else first
        if part.ndim == 2:
            return pl.BlockSpec((GRID, part.shape[1]), lambda s, *_: (s + offset, 0))
        return pl.BlockSpec((part.shape[0], GRID, D), lambda s, *_: (0, s + offset, 0))

    def weight_spec(weight):
        blocks = min(weight.shape[0], tiles)
        return pl.BlockSpec((blocks, D, D), lambda s, *_: (0, 0, 0), pipeline_mode=pl.Buffered(1))

    return pl.pallas_call(
        body,
        grid_spec=pltpu.PrefetchScalarGridSpec(
            num_scalar_prefetch=2,
            grid=(samples,),
            in_specs=[part_spec(part) for part in parts]
            + [weight_spec(weight) for weight in weights]
            + [spec(first) for spec in late_specs]
            + [anywhere(first)] * len(kept),
            out_specs=[spec(first) for _, _, spec in outs],
        ),
        out_shape=[jax.ShapeDtypeStruct(shape, kind) for shape, kind, _ in outs],
        input_output_aliases={2 + used + len(late) + n: i for n, (i, _) in enumerate(kept)},
        compiler_params=params(),
        cost_estimate=cost(2 * count * D * D * tiles, 2 * D * tiles * (count + D) + 10 * count * D),
        name=name,
    )(scal, quarters, *parts, *weights, *late, *[v for _, v in kept])


def mid_back_finish(span, scal, sample, grad, late, outs):
    middle, branch, cg, mods = late
    gmid, gbr, gbr_sum, grads = outs
    unit, inverse = normal(middle[...])
    whole = cg[...].astype(F32) + norm_back(unit, inverse, grad * (1.0 + mods[0, 4:5]))
    gmid[...] = whole
    low = (mods[0, 2:3] * whole).astype(BF)
    gbr[...] = low
    accumulate(gbr_sum, column_sum(low), sample)
    grads[0, 0:1] = column_sum(whole * branch[...].astype(F32))
    grads[0, 1:2] = column_sum(grad)
    grads[0, 2:3] = column_sum(grad * unit)


def front_back_finish(span, scal, sample, grad, late, outs):
    xg, gmid, mods, column = late
    tgrad, grads = outs
    unit, inverse = normal(xg[...].astype(F32))
    grads[0, 0:1] = column_sum(grad)
    grads[0, 1:2] = column_sum(grad * unit)
    whole = gmid[...] + norm_back(unit, inverse, grad * (1.0 + mods[0, 1:2]))
    pick = (lax.broadcasted_iota(jnp.int32, (GRID, GRID), 1) == column[...]).astype(F32).astype(BF)
    high = whole.astype(BF)
    rest = (whole - high.astype(F32)).astype(BF)
    tgrad[...] = dot(pick, high) + dot(pick, rest)


def down_finish(span, scal, sample, product, late, outs):
    middle, cg, mods, bias, column = late
    out, grads = outs
    mlp = product + bias[...]
    grads[0] = column_sum(cg[...].astype(F32) * mlp)
    final = (middle[...] + mods[0, 5:6] * mlp).astype(BF)
    length = scal[2 + span[0] + sample]
    spots = lax.broadcasted_iota(jnp.int32, (GRID, GRID), 1)
    slots = lax.broadcasted_iota(jnp.int32, (GRID, GRID), 0)
    pick = jnp.logical_and(spots == column[...], slots < length).astype(F32).astype(BF)
    out[...] = dot(pick, final).astype(BF)


def attend_back_kernel(span, scal, gbr, packed, lse, mask, table, weight, joined, joined_sum, placed, gatt, gq, gk, gv):
    gatt[...] = dot_rt(gbr[...], weight[0]).astype(BF)
    for ref in (gq, gk, gv):
        ref[...] = jnp.zeros_like(ref)

    @pl.when(pl.program_id(0) == 0)
    def _():
        placed[...] = jnp.zeros_like(placed)
        joined_sum[...] = jnp.zeros_like(joined_sum)

    lane = lax.broadcasted_iota(jnp.int32, (GRID, 128), 1)

    def head(h, _):
        start, inside = window(h)
        cols = pl.ds(start, 256)
        query = packed[:, cols] * inside
        key = packed[:, pl.ds(pl.multiple_of(D + start, 128), 256)] * inside
        value = packed[:, pl.ds(pl.multiple_of(2 * D + start, 128), 256)]
        grad = gatt[:, cols] * inside
        scores = dot_rt(query, key) * (SCALE * LIFT) + table[h] + mask[0]
        own = jnp.sum(jnp.where(lane == h, lse[...], 0.0), axis=1, keepdims=True)
        probs = jnp.exp2(scores - own)
        gprobs = dot_rt(grad, value)
        weighted = probs * gprobs
        inner = jnp.sum(weighted, axis=1, keepdims=True)
        gscores = (weighted - probs * inner).astype(BF)
        placed[h] = placed[h] + gscores.astype(F32)
        gq[:, cols] = gq[:, cols] + dot(gscores, key)
        gk[:, cols] = gk[:, cols] + dot_lt(gscores, query)
        gv[:, cols] = gv[:, cols] + dot_lt(probs.astype(BF), grad)
        return 0

    lax.fori_loop(0, HEADS, head, 0, unroll=HEADS)
    for j, (ref, factor) in enumerate(((gq, SCALE), (gk, SCALE), (gv, 1.0))):
        cols = slice(j * D, (j + 1) * D)
        low = (ref[...] * factor).astype(BF)
        joined[:, cols] = low
        joined_sum[:, cols] = joined_sum[:, cols] + column_sum(low)
    joined[:, 3 * D :] = gbr[...]


def column_block(array, rows, width, at, row=0):
    if array.ndim == 2:
        return pl.BlockSpec((rows, width), lambda *a: (row, at(*a)))
    return pl.BlockSpec((None, rows, width), lambda *a: (at(*a), row, 0))


def plain_outer_kernel(kinds, scal, *refs):
    lefts, (right, out) = refs[:kinds], refs[kinds:]
    for kind, left in enumerate(lefts):
        def product():
            out[0] = dot_lt(left[...], right[...]).astype(BF)

        if kinds == 1:
            product()
        else:
            pl.when((pl.program_id(0) == QUARTERS - 1) == (kind == 1))(product)


def plain_outer(lefts, right, scal, name):
    count = right.shape[-2]
    return pl.pallas_call(
        functools.partial(plain_outer_kernel, len(lefts)),
        grid_spec=pltpu.PrefetchScalarGridSpec(
            num_scalar_prefetch=1,
            grid=(QUARTERS,),
            in_specs=[pl.BlockSpec((count, D), lambda q, *_: (0, 0))] * len(lefts)
            + [column_block(right, count, D, lambda q, *_: q)],
            out_specs=pl.BlockSpec((1, D, D), lambda q, *_: (q, 0, 0)),
        ),
        out_shape=jax.ShapeDtypeStruct((QUARTERS, D, D), BF),
        compiler_params=params(),
        cost_estimate=cost(2 * count * D * WIDE, 2 * count * (D + WIDE) + 2 * D * WIDE),
        name=name,
    )(scal, *lefts, right)


def outer_kernel(kinds, sources, tile_width, roles, parts, order, scal, blocks, *refs):
    lefts, rights = refs[: sources * kinds], refs[sources * kinds : sources * (kinds + 1)]
    outs, tile = refs[sources * (kinds + 1) : -1], refs[-1]
    step = pl.program_id(0)

    def product(kind, cols):
        total = dot_lt(lefts[sources * kind][...], rights[0][:, cols])
        for n in range(1, sources):
            total = total + dot_lt(lefts[sources * kind + n][...], rights[n][:, cols])
        tile[:, cols] = total.astype(BF)

    if kinds == 1:
        product(0, slice(0, tile_width))
    else:
        half = tile_width // 2
        for part in range(2):
            from_first = blocks[step] * 2 + part < 3 * D // half
            cols = slice(part * half, (part + 1) * half)
            pl.when(from_first)(functools.partial(product, 0, cols))
            pl.when(jnp.logical_not(from_first))(functools.partial(product, 1, cols))
    for r in range(roles):
        @pl.when(step == r)
        def _():
            for i in range(8):
                start = i * ROWS8 if order is None else pl.multiple_of((scal[0] ^ order[i]) * ROWS8, ROWS8)
                rows = pl.ds(start, ROWS8)
                outs[parts * r + i * parts // 8][i % (8 // parts)] = tile[rows, :]


def outer_tiles(lefts, rights, scal, blocks, width, parts, order, name):
    count, kinds, roles, sources = rights[0].shape[-2], len(lefts), blocks.shape[0], len(rights)
    some = pl.BlockSpec((8 // parts, ROWS8, width), lambda r, *_: (0, 0, 0))
    each = sources // len(lefts[0])
    left_specs = [pl.BlockSpec((count, D), lambda r, *_, n=n: (n, 0)) for n in range(each)] * (len(lefts[0]) * kinds)
    return pl.pallas_call(
        functools.partial(outer_kernel, kinds, sources, width, roles, parts, order),
        grid_spec=pltpu.PrefetchScalarGridSpec(
            num_scalar_prefetch=2,
            grid=(roles,),
            in_specs=left_specs + [column_block(rights[0], count, width, lambda r, scal, blocks: blocks[r])] * sources,
            out_specs=[some] * (parts * roles),
            scratch_shapes=[pltpu.VMEM((D, width), BF)],
        ),
        out_shape=[jax.ShapeDtypeStruct((8 // parts, ROWS8, width), BF)] * (parts * roles),
        compiler_params=params(),
        cost_estimate=cost(
            2 * sources * count * D * width * roles, 2 * sources * count * (D * kinds + width * roles)
        ),
        name=name,
    )(scal, blocks, *[v for left in lefts for v in left for _ in range(each)], *rights)


ON_THE_WAY = []


def flip(value, axis, size, bit):
    ON_THE_WAY.append(lax.ppermute(value, axis, [(i, i ^ bit) for i in range(size)]))
    return ON_THE_WAY[-1]


def bits_of(size):
    return [1 << k for k in range(size.bit_length() - 1)]


def gather_steps(value, axes):
    for axis, size in axes:
        own = lax.axis_index(axis)
        for bit in bits_of(size):
            (value,) = yield [value]
            other = flip(value, axis, size, bit)
            low = (own & bit) == 0
            value = jnp.concatenate([jnp.where(low, value, other), jnp.where(low, other, value)], axis=0)
    return value


def scatter_steps(value, axis, size):
    own = lax.axis_index(axis)
    for bit in bits_of(size):
        value = value.reshape((value.shape[0] // 2, 2) + value.shape[1:])
        low = (own & bit) == 0
        keep = jnp.where(low, value[:, 0], value[:, 1])
        send = jnp.where(low, value[:, 1], value[:, 0]).astype(BF)
        (send,) = yield [send]
        value = keep + flip(send, axis, size, bit).astype(F32)
    return value


class Chain:
    def __init__(self, steps):
        self.steps, self.result = steps, None
        self.ready = next(steps)

    def advance(self, operands):
        if self.result is None:
            try:
                self.ready = self.steps.send(operands)
            except StopIteration as end:
                self.ready, self.result = [], end.value

    def finish(self):
        while self.result is None:
            self.advance(self.ready)
        return self.result


def slot(inputs, chains=(), after=(), slow=()):
    chains, slow = list(chains), list(slow)
    inputs, operands, _ = lax.optimization_barrier(
        (tuple(inputs), [c.ready for c in chains + slow], (*after, *ON_THE_WAY))
    )
    ON_THE_WAY.clear()
    for chain, ready in zip(slow, operands[len(chains) :]):
        chain.advance(ready)
    ON_THE_WAY.clear()
    for chain, ready in zip(chains, operands):
        chain.advance(ready)
    return inputs


class Wires:
    def __init__(self, mesh):
        self.dp, self.seq = mesh.shape["dp"], mesh.shape["seq"]
        self.cube = self.dp == 4 and self.seq == 8
        self.place, self.me = lax.axis_index("dp"), lax.axis_index("seq")

    def far(self, value, bit):
        return flip(value, "seq", self.seq, bit)

    def across(self, value):
        return flip(value, "dp", self.dp, 2)

    def sibling(self, value):
        return flip(value, "dp", self.dp, 1)

    def quarter(self, shards):
        if len(shards) == 1:
            return lax.dynamic_slice_in_dim(shards[0], self.place * D, D, 1)[None]
        heads = lax.dynamic_slice_in_dim(shards[0], jnp.minimum(self.place, 2) * D, D, 1)
        return jnp.where(self.place == 3, shards[1], heads)[None]

    def gather(self, quarter):
        return lax.all_gather(quarter, ("dp", "seq"), axis=0, tiled=True).reshape(QUARTERS, D, D)

    def gather_steps(self, quarter):
        (one,) = yield [quarter]
        two = jnp.concatenate([one, self.far(one, 4)], axis=0)
        (two,) = yield [two]
        four = jnp.concatenate([two, self.far(two, 2)], axis=0)
        (four,) = yield [four]
        rest, cross = self.far(four, 1), self.across(four)
        rest, cross, four = yield [rest, cross, four]
        cross_rest, near = self.across(rest), [self.sibling(four), self.sibling(rest), self.sibling(cross)]
        cross_rest, *near = yield [cross_rest, *near]
        return [four, rest, cross, cross_rest], [*near, self.sibling(cross_rest)]

    def scatter(self, whole):
        rows = D // self.seq
        parts = whole.reshape(QUARTERS * self.seq, rows, D)
        return lax.psum_scatter(parts, ("dp", "seq"), scatter_dimension=0, tiled=True)

    def spread(self, part):
        parts = yield from gather_steps(part, (("dp", self.dp),))
        return jnp.concatenate([parts[q] for q in range(QUARTERS)], axis=1)

    def reduce_quarter(self, cross, quarter, groups):
        got = {}
        for group in groups:
            sent = yield [cross[part] for part in group]
            for part, value in zip(group, sent):
                got[part] = self.across(value)
        upper = [(quarter[part].astype(F32) + got[part].astype(F32)).astype(BF) for part in (2, 3)]
        left = [part for part in (0, 1) if part not in got]
        send, *sent = yield [jnp.concatenate(upper, axis=0)] + [cross[part] for part in left]
        near = self.far(send, 1)
        for part, value in zip(left, sent):
            got[part] = self.across(value)
        (send,) = yield [(total_of([quarter[1], got[1]], 0, 2) + near[2:4].astype(F32)).astype(BF)]
        parts = [quarter[0], got[0], near, self.far(send, 2)]
        (send,) = yield [total_of(parts, 1, 2).astype(BF)]
        parts.append(self.far(send, 4))
        return (yield from self.spread(total_of(parts, 0, 1).astype(BF)))

    def reduce(self, give):
        core, x = self.place % 2, self.place // 2
        give = yield [give[1], give[0], give[2]]
        got = [self.sibling(value) for value in give]
        keep = yield []
        cross, quarter, common = [keep[1], got[0]], [keep[0], got[1]], [keep[2], got[2]]
        (high,) = yield [total_of(cross, 4, 8).astype(BF)]
        high = self.across(high)
        low, send = yield [total_of(cross, 0, 4).astype(BF), total_of(common, 4, 8).astype(BF)]
        low = self.across(low)
        common.append(self.far(send, 1))
        send, other = yield [
            (total_of(quarter, 4, 8) + high.astype(F32)).astype(BF), total_of(common, 2, 4).astype(BF)
        ]
        quarter += [low, self.far(send, 1)]
        common.append(self.far(other, 2))
        send, other = yield [total_of(quarter, 2, 4).astype(BF), total_of(common, 1, 2).astype(BF)]
        quarter.append(self.far(send, 2))
        common.append(self.far(other, 4))
        send, end = yield [total_of(quarter, 1, 2).astype(BF), total_of(common, 0, 1).astype(BF)]
        quarter.append(self.far(send, 4))
        (ends,) = yield [jnp.concatenate([total_of(quarter, 0, 1).astype(BF), end], axis=0)]
        other = self.across(ends)
        shared = (ends[1].astype(F32) + other[1].astype(F32)).astype(BF)
        (mine,) = yield [jnp.stack([ends[0], other[0], shared])]
        theirs = self.sibling(mine)
        columns = []
        first, left = core == 0, x == 0
        for quarter_index in range(4):
            of_core, of_x = divmod(quarter_index, 2)
            near, far = (mine, theirs) if of_core == 0 else (theirs, mine)
            same = jnp.where(first, near[:2], far[:2])
            columns.append(jnp.where(left == (of_x == 0), same[0], same[1]))
        columns.append(jnp.where(first, mine[2], theirs[2]))
        columns.append(jnp.where(first, theirs[2], mine[2]))
        return jnp.concatenate(columns, axis=1)

    def roles(self):
        core, x = self.place % 2, self.place // 2
        return jnp.stack([2 * core + x, 2 * core + 1 - x, 4 + core]).astype(jnp.int32)


def total_of(parts, start, stop):
    summed = 0.0
    for part in parts:
        summed = summed + part[start:stop].astype(F32)
    return summed


def unit_gaps():
    spots = np.arange(SIDE)
    reach = np.arange(SPAN)
    return (spots[None, :, None] - spots[None, None, :] + (SIDE - 1) == reach[:, None, None]).astype(np.float32)


def local(
    mesh,
    tokens,
    condition,
    lengths,
    kept_index,
    heads_weight,
    heads_bias,
    merge_weight,
    merge_bias,
    up_weight,
    up_bias,
    down_weight,
    down_bias,
    modulate_weight,
    modulate_bias,
    relative_table,
    cotangent,
):
    ON_THE_WAY.clear()
    wires = Wires(mesh)
    dp, seq = wires.dp, wires.seq
    samples, count = kept_index.shape[0], tokens.shape[0]
    shard_rows = heads_weight.shape[0]
    everything, half_a, half_b = (0, samples), (0, samples // 2), (samples // 2, samples - samples // 2)
    everyone = (("seq", seq), ("dp", dp))
    line = lambda v: v.astype(F32).reshape(1, -1)
    scal = jnp.concatenate([jnp.stack([wires.me, wires.place]).astype(jnp.int32), lengths])
    in_order = jnp.arange(QUARTERS, dtype=jnp.int32)

    own_cols = lax.dynamic_slice_in_dim(condition, wires.me * shard_rows, shard_rows, 1)
    own_silu = jax.nn.silu(own_cols.astype(F32)).astype(BF)
    partial = dot(own_silu, modulate_weight).reshape(seq, samples, 6 * D)
    mod_chain = Chain(scatter_steps(partial, "seq", seq))
    cond_chain = Chain(gather_steps(own_cols, (("dp", dp),)))
    joint = wires.gather(wires.quarter([heads_weight, merge_weight]))
    up_chain = [Chain(wires.gather_steps(wires.quarter([up_weight])))] if wires.cube else []
    upw = None if wires.cube else wires.gather(wires.quarter([up_weight]))

    index_row = kept_index.reshape(samples, 1, GRID)
    index_col = kept_index.reshape(count, 1)
    inputs = slot((tokens, cotangent, index_row), [cond_chain], slow=up_chain)
    xg, cg, mask = call(
        place_kernel, scal, inputs, [rows_spec(D), rows_spec(D), per_sample(1, GRID)],
        [((count, D), BF, rows_spec(D)), ((count, D), BF, rows_spec(D)), ((samples, 1, GRID), F32, per_sample(1, GRID))],
        [], everything, "place", cost(4 * count * GRID * D, 8 * count * D),
    )
    (later, _) = lax.optimization_barrier((down_weight, mask))
    downw = wires.gather(wires.quarter([later]))

    gaps = unit_gaps()
    turned = relative_table.reshape(HEADS, SPAN, SPAN)[:, ::-1]
    strips = jnp.einsum("hkj,jpq->hpkq", turned, jnp.asarray(gaps, BF), preferred_element_type=F32)
    strips = jnp.pad(strips.reshape(HEADS, SIDE, SPAN * SIDE), ((0, 0), (0, 0), (0, SIDE)))
    inputs = slot((strips,), up_chain + [mod_chain, cond_chain], (mask,))
    (table,) = call(
        bias_kernel, scal, inputs, [per_sample(SIDE, 2 * GRID)], [((HEADS, GRID, GRID), F32, per_sample(GRID, GRID))],
        [], (0, HEADS), "bias", cost(0, 5 << 20),
    )
    (table,) = slot((table,), [mod_chain], slow=up_chain)
    (table,) = slot((table,), [mod_chain])
    modulation = mod_chain.finish().reshape(samples, 6 * D) + modulate_bias.astype(F32)
    mods = modulation.reshape(samples, 6, D)

    full_bias = jnp.concatenate([heads_bias[:D], jnp.zeros((D,), BF), heads_bias[D:]])
    inputs = slot((xg, mods, line(full_bias), joint), slow=up_chain, after=(table,))
    h1, packed = call(
        qkv_kernel, scal, inputs,
        [rows_spec(D), per_sample(6, D), fixed(1, 3 * D), fixed(3, D, D)],
        [((count, D), BF, rows_spec(D)), ((count, 3 * D), BF, rows_spec(3 * D))],
        [], everything, "qkv", cost(2 * count * D * 3 * D, 22 << 20),
    )
    inputs = slot((packed, mask, table))
    attended, lse = call(
        attend_kernel, scal, inputs, [rows_spec(3 * D), per_sample(1, GRID), fixed(HEADS, GRID, GRID)],
        [((count, D), BF, rows_spec(D)), ((count, 128), F32, rows_spec(128))],
        [pltpu.VMEM((GRID, D), F32)], everything, "attend", cost(4 * count * GRID * 256 * HEADS, 15 << 20, count * GRID * HEADS),
    )
    inputs = slot((attended, xg, cg, mods, line(merge_bias), joint), slow=up_chain)
    branch, middle, h2, gm, gm_sum = call(
        merge_kernel, scal, inputs,
        [rows_spec(D), rows_spec(D), rows_spec(D), per_sample(6, D), fixed(1, D), fixed(1, D, D, at=(3, 0, 0))],
        [((count, D), BF, rows_spec(D)), ((count, D), F32, rows_spec(D)), ((count, D), BF, rows_spec(D)),
         ((count, D), BF, rows_spec(D)), ((1, D), F32, fixed(1, D))],
        [], everything, "merge", cost(2 * count * D * D, 20 << 20),
    )

    def pair(values):
        return [[v, wires.sibling(v)] for v in values]

    up_line, sums = line(up_bias), []
    if wires.cube:
        place = wires.place.astype(jnp.int32)
        own_quarters, their_quarters = jnp.stack([place, place ^ 2]), jnp.stack([place ^ 1, place ^ 3])
        order, cross_first = jnp.concatenate([own_quarters, their_quarters]), jnp.array([1, 0], jnp.int32)
        own_pieces, their_pieces = up_chain[0].finish()
        h2, *their_pieces = slot((h2, *their_pieces))
        act_theirs, slope_theirs, up_theirs = up_quarters(h2, up_line, their_pieces, scal, their_quarters, (1, 3))
        h2, *own_pieces = slot((h2, *own_pieces), after=(act_theirs,))
        arrived = wires.sibling(act_theirs)
        gm_pair, h2_pair = pair([gm, h2])
        act_own, slope_own, up_own = up_quarters(h2, up_line, own_pieces, scal, own_quarters, (0, 2))
        acts, upws = [act_own, act_theirs], [up_own, up_theirs]
        act_own, arrived = slot((act_own, arrived))
        tiles = outer_tiles([gm_pair], [act_own, arrived], scal, cross_first, D, 4, ORDER, "down_outer")
        down_sum = Chain(wires.reduce_quarter(tiles[:4], tiles[4:], ((2,), (3,))))
        gm, slope_theirs, downw = slot((gm, slope_theirs, downw), after=(tiles[0],))
        gu_theirs, gu_sum = act_back(gm, slope_theirs, downw, scal, their_quarters, None)
        gm, slope_own, downw, gu_sum = slot((gm, slope_own, downw, gu_sum), [down_sum], (gu_theirs,))
        arrived = wires.sibling(gu_theirs)
        gu_own, gu_sum = act_back(gm, slope_own, downw, scal, own_quarters, gu_sum)
        gu_parts = [gu_own, gu_theirs]
        gu_own, arrived = slot((gu_own, arrived), [down_sum])
        tiles = outer_tiles([h2_pair], [gu_own, arrived], scal, cross_first, D, 4, ORDER, "up_outer")
        up_sum = Chain(wires.reduce_quarter(tiles[:4], tiles[4:], ((2, 3),)))
        sums = [down_sum, up_sum]
        gu_parts = slot(gu_parts, [down_sum], (tiles[0],))
    else:
        order, upws = in_order, [upw]
        act, slope = up_quarters(h2, up_line, upw, scal, in_order, None)
        down_part = wires.scatter(plain_outer([gm], act, scal, "down_outer"))
        gu, gu_sum = act_back(gm, slope, downw, scal, in_order, None)
        up_part = wires.scatter(plain_outer([h2], gu, scal, "up_outer"))
        acts, gu_parts = [act], [gu]

    gmid, gbr, gbr_sum, mid_grads = turned_product(
        gu_parts, scal, order, upws, (middle, branch, cg, mods), [rows_spec(D), rows_spec(D), rows_spec(D), per_sample(6, D)],
        [((count, D), F32, rows_spec(D)), ((count, D), BF, rows_spec(D)), ((1, D), F32, fixed(1, D)), ((samples, 3, D), F32, per_sample(3, D))],
        mid_back_finish, everything, "mid_back",
    )
    mid_rows = jnp.pad(mid_grads.astype(BF), ((0, 0), (0, 1), (0, 0))).reshape(1, samples * 4, D)
    mid_all = lax.all_gather(mid_rows, ("dp", "seq"), axis=0, tiled=True)

    def attend_part(chains, after, span):
        inputs = slot((gbr, packed, lse, mask, table, joint), chains, after)
        return call(
            attend_back_kernel, scal, inputs,
            [rows_spec(D), rows_spec(3 * D), rows_spec(128), per_sample(1, GRID), fixed(HEADS, GRID, GRID), fixed(1, D, D, at=(3, 0, 0))],
            [((span[1] * GRID, WIDE), BF, own_rows(WIDE)),
             ((1, 3 * D), F32, fixed(1, 3 * D)), ((HEADS, GRID, GRID), F32, fixed(HEADS, GRID, GRID))],
            [pltpu.VMEM((GRID, D), BF)] + [pltpu.VMEM((GRID, D), F32)] * 3,
            span, "attend_back", cost(count * D * D + 5 * count * GRID * 256 * HEADS, 20 << 20),
        )

    joined_a, joined_sum_a, placed_a = attend_part(sums, (), half_a)
    joined_b, joined_sum_b, placed_b = attend_part(sums, (joined_a,), half_b)
    joined_sum = joined_sum_a + joined_sum_b

    done = joined_b
    if wires.cube:
        lefts, roles = [[h1], [attended]], wires.roles()
        theirs = jnp.stack([roles[0] ^ 2, roles[1] ^ 2, roles[2] ^ 1])
        rights = slot((joined_a, joined_b), after=(mid_all,), slow=sums)
        give = outer_tiles(lefts, rights, scal, theirs, TILE, 1, ORDER, "joint_give")
        joint_sum = Chain(wires.reduce(give))
        rights = slot(rights, [joint_sum], (give[0],), slow=sums[:1])
        keep = outer_tiles(lefts, rights, scal, roles, TILE, 1, ORDER, "joint_keep")
        joint_sum.ready = tuple(keep)
        joint_sum.advance(joint_sum.ready)
        done = keep[0]

    joints = [joint_sum] if wires.cube else []
    placed_a, placed_b = slot((placed_a, placed_b), (), (done,), slow=joints + sums[1:])
    (strip_grad,) = call(
        strips_kernel, scal, (placed_a, placed_b), [four_heads(GRID)] * 2,
        [((HEADS, SIDE, 2 * GRID), F32, four_heads(SIDE, 2 * GRID))], [], (0, HEADS // 4), "strips", cost(0, 9 << 20),
    )
    strip_grad = strip_grad[:, :, : SPAN * SIDE].reshape(HEADS, SIDE, SPAN, SIDE)
    table_grad = jnp.einsum(
        "hpkq,jpq->hkj", strip_grad, jnp.asarray(gaps), precision=lax.Precision.HIGHEST
    )[:, ::-1].reshape(-1)
    sizes = [2 * D, D, FF, D, HEADS * SPAN * SPAN]
    loose = jnp.concatenate(
        [joined_sum[0, :D], joined_sum[0, 2 * D :], gbr_sum[0], gu_sum[0], gm_sum[0], table_grad]
    )
    loose = jnp.pad(loose, (0, -loose.shape[0] % 1024)).reshape(-1, 128)
    loose = jnp.sum(lax.all_gather(loose, ("dp", "seq")), axis=0)
    done = strip_grad
    def front_part(own, chains, after, span, prior):
        (own,) = slot((own,), chains, after)
        return turned_product(
            [own], scal, in_order[:3], [joint], (xg, gmid, mods, index_col),
            [rows_spec(D), rows_spec(D), per_sample(6, D), rows_spec(1)],
            [((count, D), F32, rows_spec(D)), ((samples, 2, D), F32, per_sample(2, D))],
            front_back_finish, span, "front_back", prior,
        )

    def down_part_of(chains, after, span, prior, slow=()):
        own = slot(acts, chains, after, slow)
        return turned_product(
            own, scal, order, [downw], (middle, cg, mods, line(down_bias), index_col),
            [rows_spec(D), rows_spec(D), per_sample(6, D), fixed(1, D), rows_spec(1)],
            [((count, D), BF, rows_spec(D)), ((samples, 1, D), F32, per_sample(1, D))],
            down_finish, span, "down", prior,
        )

    output, down_grads = down_part_of([], (done,), half_a, None, joints)
    output, down_grads = down_part_of(joints, (down_grads,), half_b, [output, down_grads])
    tgrad, front_grads = front_part(joined_a, joints + sums, (output,), half_a, None)
    tgrad, front_grads = front_part(joined_b, joints + sums, (front_grads,), half_b, [tgrad, front_grads])

    end_grads = jnp.concatenate([front_grads, down_grads], axis=1).astype(BF).reshape(samples, 3 * D)
    end_chain = Chain(gather_steps(end_grads, everyone))
    if wires.cube:
        (mid_all,) = slot((mid_all,), [joint_sum, end_chain])
        end_chain.advance(end_chain.ready)
        (mid_all,) = slot((mid_all,), [joint_sum, end_chain], (loose,))
        up_grad, down_grad, joint_grad = up_sum.finish(), down_sum.finish(), joint_sum.finish()
    else:
        up_grad = Chain(wires.spread(up_part)).finish()
        down_grad = Chain(wires.spread(down_part)).finish()
        joint_grad = wires.scatter(plain_outer([h1, attended], jnp.concatenate([joined_a, joined_b]), scal, "joint_outer"))
        joint_grad = Chain(wires.spread(joint_grad)).finish()
    loose = loose.reshape(-1)
    end_all = end_chain.finish()
    mid_all = mid_all.reshape(-1, 4, D)[:, :3].reshape(-1, 3 * D)
    mod_all = jnp.concatenate([end_all[:, : 2 * D], mid_all, end_all[:, 2 * D :]], axis=1)
    silu_all = jax.nn.silu(cond_chain.finish().astype(F32)).astype(BF)
    modulate_grad = dot_lt(silu_all, mod_all)
    modulate_total = jnp.sum(mod_all.astype(F32), axis=0)

    edges = np.cumsum([0] + sizes)
    heads_total, merge_total, up_total, down_total, table_total = [
        loose[a:b] for a, b in zip(edges[:-1], edges[1:])
    ]
    return (
        output,
        tgrad,
        joint_grad[:, : 3 * D].astype(F32),
        joint_grad[:, 3 * D :].astype(F32),
        up_grad.astype(F32),
        down_grad.astype(F32),
        modulate_grad,
        heads_total,
        merge_total,
        up_total,
        down_total,
        modulate_total,
        table_total.reshape(HEADS, SPAN * SPAN),
    )


def solution(mesh):
    in_specs = (
        P(("dp", "seq"), None),
        P("dp", None),
        P(("dp", "seq")),
        P(("dp", "seq"), None),
        P("seq", None),
        P(),
        P("seq", None),
        P(),
        P("seq", None),
        P(),
        P("seq", None),
        P(),
        P("seq", None),
        P(),
        P(),
        P(("dp", "seq"), None),
    )
    out_specs = (
        P(("dp", "seq"), None),
        P(("dp", "seq"), None),
        P("seq", None),
        P("seq", None),
        P("seq", None),
        P("seq", None),
        P("seq", None),
        P(),
        P(),
        P(),
        P(),
        P(),
        P(),
    )
    return jax.shard_map(
        functools.partial(local, mesh), mesh=mesh, in_specs=in_specs, out_specs=out_specs, check_vma=False
    )
```

```python
import functools
import math

import jax
import jax.numpy as jnp
import numpy as np
from jax import lax
from jax.experimental import pallas as pl
from jax.experimental.pallas import tpu as pltpu
from jax.sharding import PartitionSpec as P

D = 1152
HEADS = 16
HEAD = 72
FF = 4608
SIDE = 16
GRID = 256
SPAN = 2 * SIDE - 1
WIDE = 4608
TILE = 768
ROWS8 = 144
QUARTERS = 4
LIFT = math.log2(math.e)
SCALE = 1.0 / math.sqrt(HEAD)
EPS = 1e-06
ORDER = (0, 4, 2, 6, 1, 5, 3, 7)
BF = jnp.bfloat16
F32 = jnp.float32
VMEM_LIMIT = 60 * 1024 * 1024


def dot(a, b):
    return jnp.dot(a, b, preferred_element_type=F32)


def dot_rt(a, b):
    return lax.dot_general(a, b, (((1,), (1,)), ((), ())), preferred_element_type=F32)


def dot_lt(a, b):
    return lax.dot_general(a, b, (((0,), (0,)), ((), ())), preferred_element_type=F32)


def params():
    return pltpu.CompilerParams(
        vmem_limit_bytes=VMEM_LIMIT, dimension_semantics=("arbitrary",)
    )


def cost(flops, bytes_accessed, transcendentals=0):
    return pl.CostEstimate(
        flops=int(flops), bytes_accessed=int(bytes_accessed), transcendentals=int(transcendentals)
    )


def rows_spec(width):
    return lambda first: pl.BlockSpec((GRID, width), lambda s, *_: (s + first, 0))


def own_rows(width):
    return lambda first: pl.BlockSpec((GRID, width), lambda s, *_: (s, 0))


def per_sample(*tail):
    return lambda first: pl.BlockSpec((1,) + tail, lambda s, *_: (s + first,) + (0,) * len(tail))


def four_heads(rows, columns=GRID):
    return lambda first: pl.BlockSpec((4, rows, columns), lambda s, *_: (s, 0, 0))


def fixed(*shape, at=None):
    where = (0,) * len(shape) if at is None else at
    return lambda first: pl.BlockSpec(shape, lambda s, *_: where)


def anywhere(first):
    return pl.BlockSpec(memory_space=pl.ANY)


def call(kernel, scal, inputs, in_specs, outs, scratch, span, name, price, prior=None, steps=None):
    first, samples = span
    kept = [] if prior is None else [(i, v) for i, v in enumerate(prior) if v is not None]
    count = len(inputs)

    def body(scal_ref, *refs):
        kernel(span, scal_ref, *refs[:count], *refs[count + len(kept) :])

    return pl.pallas_call(
        body,
        grid_spec=pltpu.PrefetchScalarGridSpec(
            num_scalar_prefetch=1,
            grid=(samples if steps is None else steps,),
            in_specs=[spec(first) for spec in in_specs] + [anywhere(first)] * len(kept),
            out_specs=[spec(first) for _, _, spec in outs],
            scratch_shapes=scratch,
        ),
        out_shape=[jax.ShapeDtypeStruct(shape, kind) for shape, kind, _ in outs],
        input_output_aliases={1 + count + n: i for n, (i, _) in enumerate(kept)},
        compiler_params=params(),
        cost_estimate=price,
        name=name,
    )(scal, *inputs, *[v for _, v in kept])


def normal(values):
    center = values - jnp.mean(values, axis=-1, keepdims=True)
    inverse = lax.rsqrt(jnp.mean(center * center, axis=-1, keepdims=True) + EPS)
    return center * inverse, inverse


def norm_back(unit, inverse, grad):
    return (
        grad
        - jnp.mean(grad, axis=-1, keepdims=True)
        - unit * jnp.mean(grad * unit, axis=-1, keepdims=True)
    ) * inverse


def accumulate(ref, value, step):
    @pl.when(step == 0)
    def _():
        ref[...] = value

    @pl.when(step > 0)
    def _():
        ref[...] = ref[...] + value


def column_sum(values):
    return jnp.sum(values.astype(F32), axis=0, keepdims=True)


def place_kernel(span, scal, tokens, cotangent, index, xg, cg, mask):
    length = scal[2 + span[0] + pl.program_id(0)]
    spots = lax.broadcasted_iota(jnp.int32, (GRID, GRID), 0)
    slots = lax.broadcasted_iota(jnp.int32, (GRID, GRID), 1)
    hit = spots == index[0]
    xg[...] = dot(hit.astype(F32).astype(BF), tokens[...]).astype(BF)
    alive = jnp.logical_and(hit, slots < length).astype(F32).astype(BF)
    cg[...] = dot(alive, cotangent[...]).astype(BF)
    row = dot_rt(jnp.ones((8, GRID), BF), alive)[0:1]
    mask[0] = jnp.where(row > 0.5, 0.0, -1e30)


def bias_kernel(span, scal, strips, out):
    strip = strips[0]
    for row in range(SIDE):
        start = (SIDE - 1 - row) * SIDE
        out[0, row * SIDE : (row + 1) * SIDE, :] = strip[:, start : start + GRID] * LIFT


def strips_kernel(span, scal, first, second, out):
    for head in range(4):
        total = jnp.zeros((SIDE, 2 * GRID), F32)
        for row in range(SIDE):
            rows = slice(row * SIDE, (row + 1) * SIDE)
            pair = first[head, rows, :] + second[head, rows, :]
            wide = jnp.concatenate([pair, jnp.zeros((SIDE, GRID), F32)], axis=1)
            total = total + pltpu.roll(wide, (SIDE - 1 - row) * SIDE, axis=1)
        out[head] = total


def window(h):
    start = jnp.minimum((h * HEAD) // 128 * 128, D - 256)
    lanes = lax.broadcasted_iota(jnp.int32, (1, 256), 1) + start
    inside = jnp.logical_and(lanes >= h * HEAD, lanes < (h + 1) * HEAD)
    return pl.multiple_of(start, 128), inside.astype(F32).astype(BF)


def piece_copies(pieces, gap_dp, scal, target, sems):
    copies = []
    for i, gap in enumerate(ORDER):
        rows = pl.ds(pl.multiple_of((scal[0] ^ gap) * ROWS8, ROWS8), ROWS8)
        source = pieces[2 * (gap_dp // 2) + i // 4].at[i % 4]
        copies.append(pltpu.make_async_copy(source, target.at[rows, :], sems.at[i]))
    return copies


def qkv_kernel(span, scal, xg, mods, full_bias, weight, h1, packed):
    unit, _ = normal(xg[...].astype(F32))
    hidden = (unit * (1.0 + mods[0, 1:2]) + mods[0, 0:1]).astype(BF)
    h1[...] = hidden
    for j in range(3):
        cols = slice(j * D, (j + 1) * D)
        packed[:, cols] = (dot(hidden, weight[j]) + full_bias[:, cols]).astype(BF)


def attend_kernel(span, scal, packed, mask, table, attended, lse, mixed):
    mixed[...] = jnp.zeros_like(mixed)
    lse[...] = jnp.zeros_like(lse)
    lane = lax.broadcasted_iota(jnp.int32, (GRID, 128), 1)

    def head(h, _):
        start, inside = window(h)
        query = packed[:, pl.ds(start, 256)] * inside
        key = packed[:, pl.ds(pl.multiple_of(D + start, 128), 256)]
        value = packed[:, pl.ds(pl.multiple_of(2 * D + start, 128), 256)] * inside
        scores = dot_rt(query, key) * (SCALE * LIFT) + table[h] + mask[0]
        peak = jnp.max(scores, axis=1, keepdims=True)
        expo = jnp.exp2(scores - peak)
        mass = jnp.sum(expo, axis=1, keepdims=True)
        probs = (expo * (1.0 / mass)).astype(BF)
        cols = pl.ds(start, 256)
        mixed[:, cols] = mixed[:, cols] + dot(probs, value)
        lse[...] = jnp.where(lane == h, peak + jnp.log2(mass), lse[...])
        return 0

    lax.fori_loop(0, HEADS, head, 0, unroll=HEADS)
    attended[...] = mixed[...].astype(BF)


def merge_kernel(span, scal, attended, xg, cg, mods, merge_bias, weight, branch, middle, h2, gm, gm_sum):
    low = (mods[0, 5:6] * cg[...].astype(F32)).astype(BF)
    gm[...] = low
    accumulate(gm_sum, column_sum(low), pl.program_id(0))
    merged = dot(attended[...], weight[0]) + merge_bias[...]
    branch[...] = merged.astype(BF)
    mid = xg[...].astype(F32) + mods[0, 2:3] * merged
    middle[...] = mid
    unit, _ = normal(mid)
    h2[...] = (unit * (1.0 + mods[0, 4:5]) + mods[0, 3:4]).astype(BF)


def up_kernel(samples, gaps, scal, quarters, h2, bias, *refs):
    step = pl.program_id(0)
    if gaps is None:
        weight, act, slope = refs
        matrix = lambda: weight[0]
    else:
        pieces = refs[:4]
        act, slope, spread, target, sems, out_sems = refs[4:]
        steps = len(gaps)
        matrix = lambda: target[step]
        fetch = [piece_copies(pieces, gap, scal, target.at[n], sems.at[n]) for n, gap in enumerate(gaps)]
        store = [pltpu.make_async_copy(target.at[n], spread.at[n], out_sems.at[n]) for n in range(steps)]
        for n in range(steps):
            @pl.when(step == 0)
            def _():
                for copy in fetch[n]:
                    copy.start()
        for n in range(steps):
            @pl.when(step == n)
            def _():
                for copy in fetch[n]:
                    copy.wait()
                store[n].start()

    root = math.sqrt(2.0 / math.pi)
    for s in range(samples):
        rows = slice(s * GRID, (s + 1) * GRID)
        u = dot(h2[rows, :], matrix()) + bias[...]
        square = u * u
        t = jnp.tanh(u * ((root * 0.044715) * square + root))
        half = 0.5 * t + 0.5
        act[rows, :] = (u * half).astype(BF)
        bell = half * (1.0 - half)
        slope[rows, :] = (half + bell * (u * ((6 * root * 0.044715) * square + 2 * root))).astype(BF)
    if gaps is not None:
        for n in range(steps):
            @pl.when(step == steps - 1)
            def _():
                store[n].wait()


def up_quarters(h2, bias, weight, scal, quarters, gaps):
    count, steps = h2.shape[0], quarters.shape[0]
    column = pl.BlockSpec((None, count, D), lambda k, *_: (k, 0, 0))
    out = [jax.ShapeDtypeStruct((steps, count, D), BF)] * 2
    if gaps is None:
        weight = [weight]
        weight_specs, out_specs, scratch = [pl.BlockSpec((1, D, D), lambda k, scal, q: (q[k], 0, 0))], [column] * 2, []
    else:
        weight_specs, out_specs = [anywhere(0)] * 4, [column] * 2 + [anywhere(0)]
        out = out + [jax.ShapeDtypeStruct((steps, D, D), BF)]
        scratch = [pltpu.VMEM((steps, D, D), BF), pltpu.SemaphoreType.DMA((steps, 8)), pltpu.SemaphoreType.DMA((steps,))]
    return pl.pallas_call(
        functools.partial(up_kernel, count // GRID, gaps),
        grid_spec=pltpu.PrefetchScalarGridSpec(
            num_scalar_prefetch=2,
            grid=(steps,),
            in_specs=[pl.BlockSpec((count, D), lambda k, *_: (0, 0)), pl.BlockSpec((1, D), lambda k, scal, q: (0, q[k]))]
            + weight_specs,
            out_specs=out_specs,
            scratch_shapes=scratch,
        ),
        out_shape=out,
        compiler_params=params(),
        cost_estimate=cost(2 * count * D * D * steps, 2 * D * steps * (3 * count + 2 * D), count * D * steps),
        name="up",
    )(scal, quarters, h2, bias, *weight)


def act_back_kernel(samples, scal, quarters, gm, slope, weight, *refs):
    gu, gu_sum = refs[-2:]
    total = jnp.zeros((1, D), F32)
    for s in range(samples):
        rows = slice(s * GRID, (s + 1) * GRID)
        low = (dot(gm[rows, :], weight[0]) * slope[rows, :].astype(F32)).astype(BF)
        gu[0, rows, :] = low
        total = total + column_sum(low)
    gu_sum[...] = total


def act_back(gm, slope, weight, scal, quarters, prior):
    count, steps = gm.shape[0], quarters.shape[0]
    whole = pl.BlockSpec((count, D), lambda k, *_: (0, 0))
    return pl.pallas_call(
        functools.partial(act_back_kernel, count // GRID),
        grid_spec=pltpu.PrefetchScalarGridSpec(
            num_scalar_prefetch=2,
            grid=(steps,),
            in_specs=[
                whole,
                pl.BlockSpec((None, count, D), lambda k, *_: (k, 0, 0)),
                pl.BlockSpec((1, D, D), lambda k, scal, q: (q[k], 0, 0)),
            ]
            + [anywhere(0)] * (prior is not None),
            out_specs=[
                pl.BlockSpec((1, count, D), lambda k, *_: (k, 0, 0)),
                pl.BlockSpec((1, D), lambda k, scal, q: (0, q[k])),
            ],
        ),
        out_shape=[jax.ShapeDtypeStruct((steps, count, D), BF), jax.ShapeDtypeStruct((1, FF), F32)],
        input_output_aliases={} if prior is None else {5: 1},
        compiler_params=params(),
        cost_estimate=cost(2 * count * D * D * steps, 2 * D * steps * (2 * count + D)),
        name="act_back",
    )(scal, quarters, gm, slope, weight, *([] if prior is None else [prior]))


def turned_product(parts, scal, quarters, weights, late, late_specs, outs, finish, span, name, prior=None):
    first, samples = span
    count, tiles = samples * GRID, quarters.shape[0]
    kept = [] if prior is None else [(i, v) for i, v in enumerate(prior) if v is not None]
    used = len(parts) + len(weights)

    def body(scal_ref, quarters_ref, *refs):
        ins, ws = refs[: len(parts)], refs[len(parts) : used]
        late_refs = refs[used : used + len(late)]
        out_refs = refs[used + len(late) + len(kept) :]
        total, tile = None, 0
        for n, ref in enumerate(ins):
            blocks = ref.shape[0] if len(ref.shape) == 3 else ref.shape[1] // D
            for k in range(min(blocks, tiles - tile)):
                left = ref[k] if len(ref.shape) == 3 else ref[:, k * D : (k + 1) * D]
                right = ws[n][k] if len(ws) > 1 else ws[0][quarters_ref[tile]]
                part = dot_rt(left, right)
                total = part if total is None else total + part
                tile += 1
        finish(span, scal_ref, pl.program_id(0), total, late_refs, out_refs)

    def part_spec(part):
        offset = 0 if part.shape[-2] == count else first
        if part.ndim == 2:
            return pl.BlockSpec((GRID, part.shape[1]), lambda s, *_: (s + offset, 0))
        return pl.BlockSpec((part.shape[0], GRID, D), lambda s, *_: (0, s + offset, 0))

    def weight_spec(weight):
        blocks = min(weight.shape[0], tiles)
        return pl.BlockSpec((blocks, D, D), lambda s, *_: (0, 0, 0), pipeline_mode=pl.Buffered(1))

    return pl.pallas_call(
        body,
        grid_spec=pltpu.PrefetchScalarGridSpec(
            num_scalar_prefetch=2,
            grid=(samples,),
            in_specs=[part_spec(part) for part in parts]
            + [weight_spec(weight) for weight in weights]
            + [spec(first) for spec in late_specs]
            + [anywhere(first)] * len(kept),
            out_specs=[spec(first) for _, _, spec in outs],
        ),
        out_shape=[jax.ShapeDtypeStruct(shape, kind) for shape, kind, _ in outs],
        input_output_aliases={2 + used + len(late) + n: i for n, (i, _) in enumerate(kept)},
        compiler_params=params(),
        cost_estimate=cost(2 * count * D * D * tiles, 2 * D * tiles * (count + D) + 10 * count * D),
        name=name,
    )(scal, quarters, *parts, *weights, *late, *[v for _, v in kept])


def mid_back_finish(span, scal, sample, grad, late, outs):
    middle, branch, cg, mods = late
    gmid, gbr, gbr_sum, grads = outs
    unit, inverse = normal(middle[...])
    whole = cg[...].astype(F32) + norm_back(unit, inverse, grad * (1.0 + mods[0, 4:5]))
    gmid[...] = whole
    low = (mods[0, 2:3] * whole).astype(BF)
    gbr[...] = low
    accumulate(gbr_sum, column_sum(low), sample)
    grads[0, 0:1] = column_sum(whole * branch[...].astype(F32))
    grads[0, 1:2] = column_sum(grad)
    grads[0, 2:3] = column_sum(grad * unit)


def front_back_finish(span, scal, sample, grad, late, outs):
    xg, gmid, mods, column = late
    tgrad, grads = outs
    unit, inverse = normal(xg[...].astype(F32))
    grads[0, 0:1] = column_sum(grad)
    grads[0, 1:2] = column_sum(grad * unit)
    whole = gmid[...] + norm_back(unit, inverse, grad * (1.0 + mods[0, 1:2]))
    pick = (lax.broadcasted_iota(jnp.int32, (GRID, GRID), 1) == column[...]).astype(F32).astype(BF)
    high = whole.astype(BF)
    rest = (whole - high.astype(F32)).astype(BF)
    tgrad[...] = dot(pick, high) + dot(pick, rest)


def down_finish(span, scal, sample, product, late, outs):
    middle, cg, mods, bias, column = late
    out, grads = outs
    mlp = product + bias[...]
    grads[0] = column_sum(cg[...].astype(F32) * mlp)
    final = (middle[...] + mods[0, 5:6] * mlp).astype(BF)
    length = scal[2 + span[0] + sample]
    spots = lax.broadcasted_iota(jnp.int32, (GRID, GRID), 1)
    slots = lax.broadcasted_iota(jnp.int32, (GRID, GRID), 0)
    pick = jnp.logical_and(spots == column[...], slots < length).astype(F32).astype(BF)
    out[...] = dot(pick, final).astype(BF)


def attend_back_kernel(span, scal, gbr, packed, lse, mask, table, weight, joined, joined_sum, placed, gatt, gq, gk, gv):
    gatt[...] = dot_rt(gbr[...], weight[0]).astype(BF)
    for ref in (gq, gk, gv):
        ref[...] = jnp.zeros_like(ref)

    @pl.when(pl.program_id(0) == 0)
    def _():
        placed[...] = jnp.zeros_like(placed)
        joined_sum[...] = jnp.zeros_like(joined_sum)

    lane = lax.broadcasted_iota(jnp.int32, (GRID, 128), 1)

    def head(h, _):
        start, inside = window(h)
        cols = pl.ds(start, 256)
        query = packed[:, cols] * inside
        key = packed[:, pl.ds(pl.multiple_of(D + start, 128), 256)] * inside
        value = packed[:, pl.ds(pl.multiple_of(2 * D + start, 128), 256)]
        grad = gatt[:, cols] * inside
        scores = dot_rt(query, key) * (SCALE * LIFT) + table[h] + mask[0]
        own = jnp.sum(jnp.where(lane == h, lse[...], 0.0), axis=1, keepdims=True)
        probs = jnp.exp2(scores - own)
        gprobs = dot_rt(grad, value)
        weighted = probs * gprobs
        inner = jnp.sum(weighted, axis=1, keepdims=True)
        gscores = (weighted - probs * inner).astype(BF)
        placed[h] = placed[h] + gscores.astype(F32)
        gq[:, cols] = gq[:, cols] + dot(gscores, key)
        gk[:, cols] = gk[:, cols] + dot_lt(gscores, query)
        gv[:, cols] = gv[:, cols] + dot_lt(probs.astype(BF), grad)
        return 0

    lax.fori_loop(0, HEADS, head, 0, unroll=HEADS)
    for j, (ref, factor) in enumerate(((gq, SCALE), (gk, SCALE), (gv, 1.0))):
        cols = slice(j * D, (j + 1) * D)
        low = (ref[...] * factor).astype(BF)
        joined[:, cols] = low
        joined_sum[:, cols] = joined_sum[:, cols] + column_sum(low)
    joined[:, 3 * D :] = gbr[...]


def column_block(array, rows, width, at, row=0):
    if array.ndim == 2:
        return pl.BlockSpec((rows, width), lambda *a: (row, at(*a)))
    return pl.BlockSpec((None, rows, width), lambda *a: (at(*a), row, 0))


def plain_outer_kernel(kinds, scal, *refs):
    lefts, (right, out) = refs[:kinds], refs[kinds:]
    for kind, left in enumerate(lefts):
        def product():
            out[0] = dot_lt(left[...], right[...]).astype(BF)

        if kinds == 1:
            product()
        else:
            pl.when((pl.program_id(0) == QUARTERS - 1) == (kind == 1))(product)


def plain_outer(lefts, right, scal, name):
    count = right.shape[-2]
    return pl.pallas_call(
        functools.partial(plain_outer_kernel, len(lefts)),
        grid_spec=pltpu.PrefetchScalarGridSpec(
            num_scalar_prefetch=1,
            grid=(QUARTERS,),
            in_specs=[pl.BlockSpec((count, D), lambda q, *_: (0, 0))] * len(lefts)
            + [column_block(right, count, D, lambda q, *_: q)],
            out_specs=pl.BlockSpec((1, D, D), lambda q, *_: (q, 0, 0)),
        ),
        out_shape=jax.ShapeDtypeStruct((QUARTERS, D, D), BF),
        compiler_params=params(),
        cost_estimate=cost(2 * count * D * WIDE, 2 * count * (D + WIDE) + 2 * D * WIDE),
        name=name,
    )(scal, *lefts, right)


def outer_kernel(kinds, sources, tile_width, roles, parts, order, scal, blocks, *refs):
    lefts, rights = refs[: sources * kinds], refs[sources * kinds : sources * (kinds + 1)]
    outs, tile = refs[sources * (kinds + 1) : -1], refs[-1]
    step = pl.program_id(0)

    def product(kind, cols):
        total = dot_lt(lefts[sources * kind][...], rights[0][:, cols])
        for n in range(1, sources):
            total = total + dot_lt(lefts[sources * kind + n][...], rights[n][:, cols])
        tile[:, cols] = total.astype(BF)

    if kinds == 1:
        product(0, slice(0, tile_width))
    else:
        half = tile_width // 2
        for part in range(2):
            from_first = blocks[step] * 2 + part < 3 * D // half
            cols = slice(part * half, (part + 1) * half)
            pl.when(from_first)(functools.partial(product, 0, cols))
            pl.when(jnp.logical_not(from_first))(functools.partial(product, 1, cols))
    for r in range(roles):
        @pl.when(step == r)
        def _():
            for i in range(8):
                start = i * ROWS8 if order is None else pl.multiple_of((scal[0] ^ order[i]) * ROWS8, ROWS8)
                rows = pl.ds(start, ROWS8)
                outs[parts * r + i * parts // 8][i % (8 // parts)] = tile[rows, :]


def outer_tiles(lefts, rights, scal, blocks, width, parts, order, name):
    count, kinds, roles, sources = rights[0].shape[-2], len(lefts), blocks.shape[0], len(rights)
    some = pl.BlockSpec((8 // parts, ROWS8, width), lambda r, *_: (0, 0, 0))
    each = sources // len(lefts[0])
    left_specs = [pl.BlockSpec((count, D), lambda r, *_, n=n: (n, 0)) for n in range(each)] * (len(lefts[0]) * kinds)
    return pl.pallas_call(
        functools.partial(outer_kernel, kinds, sources, width, roles, parts, order),
        grid_spec=pltpu.PrefetchScalarGridSpec(
            num_scalar_prefetch=2,
            grid=(roles,),
            in_specs=left_specs + [column_block(rights[0], count, width, lambda r, scal, blocks: blocks[r])] * sources,
            out_specs=[some] * (parts * roles),
            scratch_shapes=[pltpu.VMEM((D, width), BF)],
        ),
        out_shape=[jax.ShapeDtypeStruct((8 // parts, ROWS8, width), BF)] * (parts * roles),
        compiler_params=params(),
        cost_estimate=cost(
            2 * sources * count * D * width * roles, 2 * sources * count * (D * kinds + width * roles)
        ),
        name=name,
    )(scal, blocks, *[v for left in lefts for v in left for _ in range(each)], *rights)


ON_THE_WAY = []


def flip(value, axis, size, bit):
    ON_THE_WAY.append(lax.ppermute(value, axis, [(i, i ^ bit) for i in range(size)]))
    return ON_THE_WAY[-1]


def bits_of(size):
    return [1 << k for k in range(size.bit_length() - 1)]


def gather_steps(value, axes):
    for axis, size in axes:
        own = lax.axis_index(axis)
        for bit in bits_of(size):
            (value,) = yield [value]
            other = flip(value, axis, size, bit)
            low = (own & bit) == 0
            value = jnp.concatenate([jnp.where(low, value, other), jnp.where(low, other, value)], axis=0)
    return value


def scatter_steps(value, axis, size):
    own = lax.axis_index(axis)
    for bit in bits_of(size):
        value = value.reshape((value.shape[0] // 2, 2) + value.shape[1:])
        low = (own & bit) == 0
        keep = jnp.where(low, value[:, 0], value[:, 1])
        send = jnp.where(low, value[:, 1], value[:, 0]).astype(BF)
        (send,) = yield [send]
        value = keep + flip(send, axis, size, bit).astype(F32)
    return value


class Chain:
    def __init__(self, steps):
        self.steps, self.result = steps, None
        self.ready = next(steps)

    def advance(self, operands):
        if self.result is None:
            try:
                self.ready = self.steps.send(operands)
            except StopIteration as end:
                self.ready, self.result = [], end.value

    def finish(self):
        while self.result is None:
            self.advance(self.ready)
        return self.result


def slot(inputs, chains=(), after=(), slow=()):
    chains, slow = list(chains), list(slow)
    inputs, operands, _ = lax.optimization_barrier(
        (tuple(inputs), [c.ready for c in chains + slow], (*after, *ON_THE_WAY))
    )
    ON_THE_WAY.clear()
    for chain, ready in zip(slow, operands[len(chains) :]):
        chain.advance(ready)
    ON_THE_WAY.clear()
    for chain, ready in zip(chains, operands):
        chain.advance(ready)
    return inputs


class Wires:
    def __init__(self, mesh):
        self.dp, self.seq = mesh.shape["dp"], mesh.shape["seq"]
        self.cube = self.dp == 4 and self.seq == 8
        self.place, self.me = lax.axis_index("dp"), lax.axis_index("seq")

    def far(self, value, bit):
        return flip(value, "seq", self.seq, bit)

    def across(self, value):
        return flip(value, "dp", self.dp, 2)

    def sibling(self, value):
        return flip(value, "dp", self.dp, 1)

    def quarter(self, shards):
        if len(shards) == 1:
            return lax.dynamic_slice_in_dim(shards[0], self.place * D, D, 1)[None]
        heads = lax.dynamic_slice_in_dim(shards[0], jnp.minimum(self.place, 2) * D, D, 1)
        return jnp.where(self.place == 3, shards[1], heads)[None]

    def gather(self, quarter):
        return lax.all_gather(quarter, ("dp", "seq"), axis=0, tiled=True).reshape(QUARTERS, D, D)

    def gather_steps(self, quarter):
        (one,) = yield [quarter]
        two = jnp.concatenate([one, self.far(one, 4)], axis=0)
        (two,) = yield [two]
        four = jnp.concatenate([two, self.far(two, 2)], axis=0)
        (four,) = yield [four]
        rest, cross = self.far(four, 1), self.across(four)
        rest, cross, four = yield [rest, cross, four]
        cross_rest, near = self.across(rest), [self.sibling(four), self.sibling(rest), self.sibling(cross)]
        cross_rest, *near = yield [cross_rest, *near]
        return [four, rest, cross, cross_rest], [*near, self.sibling(cross_rest)]

    def scatter(self, whole):
        rows = D // self.seq
        parts = whole.reshape(QUARTERS * self.seq, rows, D)
        return lax.psum_scatter(parts, ("dp", "seq"), scatter_dimension=0, tiled=True)

    def spread(self, part):
        return (yield from gather_steps(part, (("dp", self.dp),)))

    def reduce_quarter(self, cross, quarter, groups):
        got = {}
        for group in groups:
            sent = yield [cross[part] for part in group]
            for part, value in zip(group, sent):
                got[part] = self.across(value)
        upper = [(quarter[part].astype(F32) + got[part].astype(F32)).astype(BF) for part in (2, 3)]
        left = [part for part in (0, 1) if part not in got]
        send, *sent = yield [jnp.concatenate(upper, axis=0)] + [cross[part] for part in left]
        near = self.far(send, 1)
        for part, value in zip(left, sent):
            got[part] = self.across(value)
        (send,) = yield [(total_of([quarter[1], got[1]], 0, 2) + near[2:4].astype(F32)).astype(BF)]
        parts = [quarter[0], got[0], near, self.far(send, 2)]
        (send,) = yield [total_of(parts, 1, 2).astype(BF)]
        parts.append(self.far(send, 4))
        return (yield from self.spread(total_of(parts, 0, 1).astype(BF)))

    def reduce(self, give):
        core, x = self.place % 2, self.place // 2
        give = yield [give[1], give[0], give[2]]
        got = [self.sibling(value) for value in give]
        keep = yield []
        cross, quarter, common = [keep[1], got[0]], [keep[0], got[1]], [keep[2], got[2]]
        (high,) = yield [total_of(cross, 4, 8).astype(BF)]
        high = self.across(high)
        low, send = yield [total_of(cross, 0, 4).astype(BF), total_of(common, 4, 8).astype(BF)]
        low = self.across(low)
        common.append(self.far(send, 1))
        send, other = yield [
            (total_of(quarter, 4, 8) + high.astype(F32)).astype(BF), total_of(common, 2, 4).astype(BF)
        ]
        quarter += [low, self.far(send, 1)]
        common.append(self.far(other, 2))
        send, other = yield [total_of(quarter, 2, 4).astype(BF), total_of(common, 1, 2).astype(BF)]
        quarter.append(self.far(send, 2))
        common.append(self.far(other, 4))
        send, end = yield [total_of(quarter, 1, 2).astype(BF), total_of(common, 0, 1).astype(BF)]
        quarter.append(self.far(send, 4))
        (ends,) = yield [jnp.concatenate([total_of(quarter, 0, 1).astype(BF), end], axis=0)]
        other = self.across(ends)
        shared = (ends[1].astype(F32) + other[1].astype(F32)).astype(BF)
        (mine,) = yield [jnp.stack([ends[0], other[0], shared])]
        theirs = self.sibling(mine)
        columns = []
        first, left = core == 0, x == 0
        for quarter_index in range(4):
            of_core, of_x = divmod(quarter_index, 2)
            near, far = (mine, theirs) if of_core == 0 else (theirs, mine)
            same = jnp.where(first, near[:2], far[:2])
            columns.append(jnp.where(left == (of_x == 0), same[0], same[1]))
        columns.append(jnp.where(first, mine[2], theirs[2]))
        columns.append(jnp.where(first, theirs[2], mine[2]))
        return jnp.concatenate(columns, axis=1)

    def roles(self):
        core, x = self.place % 2, self.place // 2
        return jnp.stack([2 * core + x, 2 * core + 1 - x, 4 + core]).astype(jnp.int32)


def side_by_side(parts):
    return jnp.concatenate([parts[q] for q in range(QUARTERS)], axis=1)


def total_of(parts, start, stop):
    summed = 0.0
    for part in parts:
        summed = summed + part[start:stop].astype(F32)
    return summed


def unit_gaps():
    spots = np.arange(SIDE)
    reach = np.arange(SPAN)
    return (spots[None, :, None] - spots[None, None, :] + (SIDE - 1) == reach[:, None, None]).astype(np.float32)


def local(
    mesh,
    tokens,
    condition,
    lengths,
    kept_index,
    heads_weight,
    heads_bias,
    merge_weight,
    merge_bias,
    up_weight,
    up_bias,
    down_weight,
    down_bias,
    modulate_weight,
    modulate_bias,
    relative_table,
    cotangent,
):
    ON_THE_WAY.clear()
    wires = Wires(mesh)
    dp, seq = wires.dp, wires.seq
    samples, count = kept_index.shape[0], tokens.shape[0]
    shard_rows = heads_weight.shape[0]
    everything, half_a, half_b = (0, samples), (0, samples // 2), (samples // 2, samples - samples // 2)
    everyone = (("seq", seq), ("dp", dp))
    line = lambda v: v.astype(F32).reshape(1, -1)
    scal = jnp.concatenate([jnp.stack([wires.me, wires.place]).astype(jnp.int32), lengths])
    in_order = jnp.arange(QUARTERS, dtype=jnp.int32)

    own_cols = lax.dynamic_slice_in_dim(condition, wires.me * shard_rows, shard_rows, 1)
    own_silu = jax.nn.silu(own_cols.astype(F32)).astype(BF)
    partial = dot(own_silu, modulate_weight).reshape(seq, samples, 6 * D)
    mod_chain = Chain(scatter_steps(partial, "seq", seq))
    cond_chain = Chain(gather_steps(own_cols, (("dp", dp),)))
    joint = wires.gather(wires.quarter([heads_weight, merge_weight]))
    up_chain = [Chain(wires.gather_steps(wires.quarter([up_weight])))] if wires.cube else []
    upw = None if wires.cube else wires.gather(wires.quarter([up_weight]))

    index_row = kept_index.reshape(samples, 1, GRID)
    index_col = kept_index.reshape(count, 1)
    inputs = slot((tokens, cotangent, index_row), [cond_chain], slow=up_chain)
    xg, cg, mask = call(
        place_kernel, scal, inputs, [rows_spec(D), rows_spec(D), per_sample(1, GRID)],
        [((count, D), BF, rows_spec(D)), ((count, D), BF, rows_spec(D)), ((samples, 1, GRID), F32, per_sample(1, GRID))],
        [], everything, "place", cost(4 * count * GRID * D, 8 * count * D),
    )
    (later, _) = lax.optimization_barrier((down_weight, mask))
    downw = wires.gather(wires.quarter([later]))

    gaps = unit_gaps()
    turned = relative_table.reshape(HEADS, SPAN, SPAN)[:, ::-1]
    strips = jnp.einsum("hkj,jpq->hpkq", turned, jnp.asarray(gaps, BF), preferred_element_type=F32)
    strips = jnp.pad(strips.reshape(HEADS, SIDE, SPAN * SIDE), ((0, 0), (0, 0), (0, SIDE)))
    inputs = slot((strips,), up_chain + [mod_chain, cond_chain], (mask,))
    (table,) = call(
        bias_kernel, scal, inputs, [per_sample(SIDE, 2 * GRID)], [((HEADS, GRID, GRID), F32, per_sample(GRID, GRID))],
        [], (0, HEADS), "bias", cost(0, 5 << 20),
    )
    (table,) = slot((table,), [mod_chain], slow=up_chain)
    (table,) = slot((table,), [mod_chain])
    modulation = mod_chain.finish().reshape(samples, 6 * D) + modulate_bias.astype(F32)
    mods = modulation.reshape(samples, 6, D)

    full_bias = jnp.concatenate([heads_bias[:D], jnp.zeros((D,), BF), heads_bias[D:]])
    inputs = slot((xg, mods, line(full_bias), joint), slow=up_chain, after=(table,))
    h1, packed = call(
        qkv_kernel, scal, inputs,
        [rows_spec(D), per_sample(6, D), fixed(1, 3 * D), fixed(3, D, D)],
        [((count, D), BF, rows_spec(D)), ((count, 3 * D), BF, rows_spec(3 * D))],
        [], everything, "qkv", cost(2 * count * D * 3 * D, 22 << 20),
    )
    inputs = slot((packed, mask, table))
    attended, lse = call(
        attend_kernel, scal, inputs, [rows_spec(3 * D), per_sample(1, GRID), fixed(HEADS, GRID, GRID)],
        [((count, D), BF, rows_spec(D)), ((count, 128), F32, rows_spec(128))],
        [pltpu.VMEM((GRID, D), F32)], everything, "attend", cost(4 * count * GRID * 256 * HEADS, 15 << 20, count * GRID * HEADS),
    )
    inputs = slot((attended, xg, cg, mods, line(merge_bias), joint), slow=up_chain)
    branch, middle, h2, gm, gm_sum = call(
        merge_kernel, scal, inputs,
        [rows_spec(D), rows_spec(D), rows_spec(D), per_sample(6, D), fixed(1, D), fixed(1, D, D, at=(3, 0, 0))],
        [((count, D), BF, rows_spec(D)), ((count, D), F32, rows_spec(D)), ((count, D), BF, rows_spec(D)),
         ((count, D), BF, rows_spec(D)), ((1, D), F32, fixed(1, D))],
        [], everything, "merge", cost(2 * count * D * D, 20 << 20),
    )

    def pair(values):
        return [[v, wires.sibling(v)] for v in values]

    up_line, sums = line(up_bias), []
    if wires.cube:
        place = wires.place.astype(jnp.int32)
        own_quarters, their_quarters = jnp.stack([place, place ^ 2]), jnp.stack([place ^ 1, place ^ 3])
        order, cross_first = jnp.concatenate([own_quarters, their_quarters]), jnp.array([1, 0], jnp.int32)
        own_pieces, their_pieces = up_chain[0].finish()
        h2, *their_pieces = slot((h2, *their_pieces))
        act_theirs, slope_theirs, up_theirs = up_quarters(h2, up_line, their_pieces, scal, their_quarters, (1, 3))
        h2, *own_pieces = slot((h2, *own_pieces), after=(act_theirs,))
        arrived = wires.sibling(act_theirs)
        gm_pair, h2_pair = pair([gm, h2])
        act_own, slope_own, up_own = up_quarters(h2, up_line, own_pieces, scal, own_quarters, (0, 2))
        acts, upws = [act_own, act_theirs], [up_own, up_theirs]
        act_own, arrived = slot((act_own, arrived))
        tiles = outer_tiles([gm_pair], [act_own, arrived], scal, cross_first, D, 4, ORDER, "down_outer")
        down_sum = Chain(wires.reduce_quarter(tiles[:4], tiles[4:], ((2,), (3,))))
        gm, slope_theirs, downw = slot((gm, slope_theirs, downw), after=(tiles[0],))
        gu_theirs, gu_sum = act_back(gm, slope_theirs, downw, scal, their_quarters, None)
        gm, slope_own, downw, gu_sum = slot((gm, slope_own, downw, gu_sum), [down_sum], (gu_theirs,))
        arrived = wires.sibling(gu_theirs)
        gu_own, gu_sum = act_back(gm, slope_own, downw, scal, own_quarters, gu_sum)
        gu_parts = [gu_own, gu_theirs]
        gu_own, arrived = slot((gu_own, arrived), [down_sum])
        tiles = outer_tiles([h2_pair], [gu_own, arrived], scal, cross_first, D, 4, ORDER, "up_outer")
        up_sum = Chain(wires.reduce_quarter(tiles[:4], tiles[4:], ((2, 3),)))
        sums = [down_sum, up_sum]
        gu_parts = slot(gu_parts, [down_sum], (tiles[0],))
    else:
        order, upws = in_order, [upw]
        act, slope = up_quarters(h2, up_line, upw, scal, in_order, None)
        down_part = wires.scatter(plain_outer([gm], act, scal, "down_outer"))
        gu, gu_sum = act_back(gm, slope, downw, scal, in_order, None)
        up_part = wires.scatter(plain_outer([h2], gu, scal, "up_outer"))
        acts, gu_parts = [act], [gu]

    gmid, gbr, gbr_sum, mid_grads = turned_product(
        gu_parts, scal, order, upws, (middle, branch, cg, mods), [rows_spec(D), rows_spec(D), rows_spec(D), per_sample(6, D)],
        [((count, D), F32, rows_spec(D)), ((count, D), BF, rows_spec(D)), ((1, D), F32, fixed(1, D)), ((samples, 3, D), F32, per_sample(3, D))],
        mid_back_finish, everything, "mid_back",
    )
    mid_rows = jnp.pad(mid_grads.astype(BF), ((0, 0), (0, 1), (0, 0))).reshape(1, samples * 4, D)
    mid_all = lax.all_gather(mid_rows, ("dp", "seq"), axis=0, tiled=True)

    def attend_part(chains, after, span):
        inputs = slot((gbr, packed, lse, mask, table, joint), chains, after)
        return call(
            attend_back_kernel, scal, inputs,
            [rows_spec(D), rows_spec(3 * D), rows_spec(128), per_sample(1, GRID), fixed(HEADS, GRID, GRID), fixed(1, D, D, at=(3, 0, 0))],
            [((span[1] * GRID, WIDE), BF, own_rows(WIDE)),
             ((1, 3 * D), F32, fixed(1, 3 * D)), ((HEADS, GRID, GRID), F32, fixed(HEADS, GRID, GRID))],
            [pltpu.VMEM((GRID, D), BF)] + [pltpu.VMEM((GRID, D), F32)] * 3,
            span, "attend_back", cost(count * D * D + 5 * count * GRID * 256 * HEADS, 20 << 20),
        )

    joined_a, joined_sum_a, placed_a = attend_part(sums, (), half_a)
    joined_b, joined_sum_b, placed_b = attend_part(sums, (joined_a,), half_b)
    joined_sum = joined_sum_a + joined_sum_b

    done = joined_b
    if wires.cube:
        lefts, roles = [[h1], [attended]], wires.roles()
        theirs = jnp.stack([roles[0] ^ 2, roles[1] ^ 2, roles[2] ^ 1])
        rights = slot((joined_a, joined_b), after=(mid_all,), slow=sums)
        give = outer_tiles(lefts, rights, scal, theirs, TILE, 1, ORDER, "joint_give")
        joint_sum = Chain(wires.reduce(give))
        rights = slot(rights, [joint_sum], (give[0],), slow=sums[:1])
        keep = outer_tiles(lefts, rights, scal, roles, TILE, 1, ORDER, "joint_keep")
        joint_sum.ready = tuple(keep)
        joint_sum.advance(joint_sum.ready)
        done = keep[0]

    joints = [joint_sum] if wires.cube else []
    placed_a, placed_b = slot((placed_a, placed_b), (), (done,), slow=joints + sums[1:])
    (strip_grad,) = call(
        strips_kernel, scal, (placed_a, placed_b), [four_heads(GRID)] * 2,
        [((HEADS, SIDE, 2 * GRID), F32, four_heads(SIDE, 2 * GRID))], [], (0, HEADS // 4), "strips", cost(0, 9 << 20),
    )
    strip_grad = strip_grad[:, :, : SPAN * SIDE].reshape(HEADS, SIDE, SPAN, SIDE)
    table_grad = jnp.einsum(
        "hpkq,jpq->hkj", strip_grad, jnp.asarray(gaps), precision=lax.Precision.HIGHEST
    )[:, ::-1].reshape(-1)
    sizes = [2 * D, D, FF, D, HEADS * SPAN * SPAN]
    loose = jnp.concatenate(
        [joined_sum[0, :D], joined_sum[0, 2 * D :], gbr_sum[0], gu_sum[0], gm_sum[0], table_grad]
    )
    loose = jnp.pad(loose, (0, -loose.shape[0] % 1024)).reshape(-1, 128)
    loose = jnp.sum(lax.all_gather(loose, ("dp", "seq")), axis=0)
    done = strip_grad
    def front_part(own, chains, after, span, prior):
        (own,) = slot((own,), chains, after)
        return turned_product(
            [own], scal, in_order[:3], [joint], (xg, gmid, mods, index_col),
            [rows_spec(D), rows_spec(D), per_sample(6, D), rows_spec(1)],
            [((count, D), F32, rows_spec(D)), ((samples, 2, D), F32, per_sample(2, D))],
            front_back_finish, span, "front_back", prior,
        )

    def down_part_of(chains, after, span, prior, slow=()):
        own = slot(acts, chains, after, slow)
        return turned_product(
            own, scal, order, [downw], (middle, cg, mods, line(down_bias), index_col),
            [rows_spec(D), rows_spec(D), per_sample(6, D), fixed(1, D), rows_spec(1)],
            [((count, D), BF, rows_spec(D)), ((samples, 1, D), F32, per_sample(1, D))],
            down_finish, span, "down", prior,
        )

    output, down_grads = down_part_of([], (done,), half_a, None, joints)
    output, down_grads = down_part_of(joints, (down_grads,), half_b, [output, down_grads])
    tgrad, front_grads = front_part(joined_a, joints + sums, (output,), half_a, None)
    tgrad, front_grads = front_part(joined_b, joints + sums, (front_grads,), half_b, [tgrad, front_grads])

    end_grads = jnp.concatenate([front_grads, down_grads], axis=1).astype(BF).reshape(samples, 3 * D)
    end_chain = Chain(gather_steps(end_grads, everyone))
    if wires.cube:
        (mid_all,) = slot((mid_all,), [joint_sum, end_chain])
        end_chain.advance(end_chain.ready)
        mid_all, down_grad = slot((mid_all, down_sum.finish()), [joint_sum, end_chain], (loose,))
        up_grad, joint_grad = up_sum.finish(), joint_sum.finish()
    else:
        up_grad = Chain(wires.spread(up_part)).finish()
        down_grad = Chain(wires.spread(down_part)).finish()
        joint_grad = wires.scatter(plain_outer([h1, attended], jnp.concatenate([joined_a, joined_b]), scal, "joint_outer"))
        joint_grad = side_by_side(Chain(wires.spread(joint_grad)).finish())
    loose = loose.reshape(-1)
    end_all = end_chain.finish()
    mid_all = mid_all.reshape(-1, 4, D)[:, :3].reshape(-1, 3 * D)
    mod_all = jnp.concatenate([end_all[:, : 2 * D], mid_all, end_all[:, 2 * D :]], axis=1)
    silu_all = jax.nn.silu(cond_chain.finish().astype(F32)).astype(BF)
    modulate_grad = dot_lt(silu_all, mod_all)
    modulate_total = jnp.sum(mod_all.astype(F32), axis=0)

    edges = np.cumsum([0] + sizes)
    heads_total, merge_total, up_total, down_total, table_total = [
        loose[a:b] for a, b in zip(edges[:-1], edges[1:])
    ]
    return (
        output,
        tgrad,
        joint_grad[:, : 3 * D].astype(F32),
        joint_grad[:, 3 * D :].astype(F32),
        side_by_side(up_grad).astype(F32),
        side_by_side(down_grad).astype(F32),
        modulate_grad,
        heads_total,
        merge_total,
        up_total,
        down_total,
        modulate_total,
        table_total.reshape(HEADS, SPAN * SPAN),
    )


def solution(mesh):
    in_specs = (
        P(("dp", "seq"), None),
        P("dp", None),
        P(("dp", "seq")),
        P(("dp", "seq"), None),
        P("seq", None),
        P(),
        P("seq", None),
        P(),
        P("seq", None),
        P(),
        P("seq", None),
        P(),
        P("seq", None),
        P(),
        P(),
        P(("dp", "seq"), None),
    )
    out_specs = (
        P(("dp", "seq"), None),
        P(("dp", "seq"), None),
        P("seq", None),
        P("seq", None),
        P("seq", None),
        P("seq", None),
        P("seq", None),
        P(),
        P(),
        P(),
        P(),
        P(),
        P(),
    )
    return jax.shard_map(
        functools.partial(local, mesh), mesh=mesh, in_specs=in_specs, out_specs=out_specs, check_vma=False
    )
```
